32 devices in a mesh: strip: 8 (over z, x), period: 4 (over y, core).
Axes of the slice: x: 2, y: 2, z: 4, core: 2. Of those that a mesh axis runs over, the one named last changes fastest.
Arguments:
- u_start: float32 [8, 16, 64, 128], P('strip', 'period'), may hold values from 0 to 0.02
- dual_prec: float32 [5, 8, 16, 64, 128], P(None, 'strip', 'period'), may hold values from 0 to 0.5
- dual_bound: float32 [8, 16, 64, 128], P('strip', 'period'), may hold values from 0 to 0.5
- dual_cap: float32 [16], P('period'), may hold values from 0 to 2
- capacity: float32 [16], P('period'), may hold values from 0.005 to 0.03
- block_value: float32 [8, 64, 128], P('strip'), may hold values from -6 to 6
- ton_class: int32 [8, 64, 128], P('strip'), may hold values from 0 to 7
- density: float32 [8], replicated, may hold values from 1 to 3
- slope_code: int32 [8, 128], P('strip'), may hold values from 0 to 15
- omega_start: float32 [1], replicated, may hold values from 0.5 to 2
Outputs:
- mined_share: float32 [8, 16, 64, 128], P('strip', 'period')
- arc_prices: float32 [5, 8, 16, 64, 128], P(None, 'strip', 'period')
- bound_prices: float32 [8, 16, 64, 128], P('strip', 'period')
- capacity_prices: float32 [16], P('period')
- primal_weight: float32 [1], replicated
The draws below stay inside these ranges and needn't reach their ends.
All inputs are finite; a program needn't handle non-finite values.
Results may differ from the reference program's by a relative error of at most 0.0001.
Values sent between devices are 32-bit elements; how exact they have to be, the bound alone decides.
A program may use at most 64 MiB of HBM per device.

```python
import math
import jax
import jax.numpy as jnp
from jax import lax

NY = 128
NZ = 64
NARCS = 5
NCLASS = 8
OUTER = 2
INNER = 3
NX = 8
NP = 16


def draw_ton_class(key, part):
    base_class = jax.random.randint(key, (NX, NZ, NY), 0, NCLASS // 2)
    rising = jnp.arange(NX) * (NCLASS // 2 + 1) // NX
    return (base_class + rising[:, None, None]).astype(jnp.int32)


def touch_ends(array, key, smallest, top_value):
    shape = array.shape
    spot = [jax.random.randint(jax.random.fold_in(key, axis), (), 0, shape[axis]) for axis in range(len(shape))]
    array = array.at[tuple(spot)].set(smallest)
    longest = shape.index(max(shape))
    spot[longest] = (spot[longest] + 1) % shape[longest]
    return array.at[tuple(spot)].set(top_value)


def block_scale(key, extent, shards, least, high):
    level = 1.0
    for dim, parts in shards:
        draws = jax.random.uniform(jax.random.fold_in(jax.random.fold_in(key, 6), dim), (parts,), jnp.float32, least / len(shards), high / len(shards))
        level = level * jnp.repeat(jnp.exp(draws), extent[dim] // parts).reshape((-1,) + (1,) * (len(extent) - 1 - dim))
    return level


def bell_draw(key, extent, scale, most, split=(), held_as=jnp.bfloat16):
    values = jax.random.normal(key, extent, jnp.float32) * scale
    if len(split) > 0:
        values = block_scale(key, extent, split, -0.22, 0.18) * values
    return jnp.clip(values, min=-most, max=most).astype(held_as)


def setup_inputs(seed: int = 0) -> dict:
    splits = jax.random.split(jax.random.key(seed), 11)
    return {
        "u_start": jnp.clip(0.02 * jax.random.uniform(splits[0], (NX, NP, NZ, NY), jnp.float32) ** block_scale(splits[0], (NX, NP, NZ, NY), ((0, 8), (1, 4)), -0.2, 0.2), 0.0, 0.02),
        "dual_prec": jnp.clip(0.5 * jax.random.uniform(splits[1], (NARCS, NX, NP, NZ, NY), jnp.float32) ** block_scale(splits[1], (NARCS, NX, NP, NZ, NY), ((1, 8), (2, 4)), -0.2, 0.2), 0.0, 0.5),
        "dual_bound": jnp.clip(0.5 * jax.random.uniform(splits[2], (NX, NP, NZ, NY), jnp.float32) ** block_scale(splits[2], (NX, NP, NZ, NY), ((0, 8), (1, 4)), -0.2, 0.2), 0.0, 0.5),
        "dual_cap": jnp.clip(2.0 * jax.random.uniform(splits[3], (NP,), jnp.float32) ** block_scale(splits[3], (NP,), ((0, 4),), -0.2, 0.2), 0.0, 2.0),
        "capacity": jnp.clip(0.005 + 0.024999999 * jax.random.uniform(splits[4], (NP,), jnp.float32) ** block_scale(splits[4], (NP,), ((0, 4),), -0.2, 0.2), 0.005, 0.03),
        "block_value": bell_draw(splits[5], (NX, NZ, NY), 1.0, 6.0, ((0, 8),), jnp.float32),
        "ton_class": draw_ton_class(jax.random.fold_in(splits[10], 71), 0),
        "density": jnp.clip(jnp.exp(jax.random.uniform(splits[7], (NCLASS,), jnp.float32, math.log(1.0), math.log(3.0))), 1.0, 3.0),
        "slope_code": touch_ends(jax.random.randint(splits[8], (NX, NY), 0, 16), jax.random.fold_in(splits[8], 1), 0, 15).astype(jnp.int32),
        "omega_start": jnp.clip(jnp.exp(jax.random.uniform(splits[9], (1,), jnp.float32, math.log(0.5), math.log(2.0))), 0.5, 2.0),
    }


ARC_OFFSETS = ((0, 0), (1, 0), (-1, 0), (0, 1), (0, -1))
RATE = math.log(1.1) / 12.0
EPS = 1e-06
SLOPE = 11.0

def arc_masks(code_rows, first_row, total_rows, depth_cells, across):
    row_ids = (first_row + jnp.arange(code_rows.shape[0]))[:, None, None]
    depth_ids = jnp.arange(depth_cells)[None, :, None]
    col_ids = jnp.arange(across)[None, None, :]
    pattern = code_rows[:, None, :]
    mask_list = []
    for arc_index, (step_x, step_y) in enumerate(ARC_OFFSETS):
        inside = (row_ids >= 0) & (row_ids < total_rows) & (row_ids + step_x >= 0) & (row_ids + step_x < total_rows)
        inside = inside & (col_ids + step_y >= 0) & (col_ids + step_y < across) & (depth_ids >= 1)
        if arc_index > 0:
            inside = inside & (pattern // 2 ** (arc_index - 1) % 2 == 1)
        mask_list.append(inside.astype(jnp.float32))
    return jnp.stack(mask_list)

def tonnage(ton_class, density):
    class_ids = jnp.arange(density.shape[0])
    class_table = (1.0 + class_ids.astype(jnp.float32)) * density
    onehot = (class_ids[:, None, None, None] == ton_class[None]).astype(jnp.float32)
    return jnp.einsum('k,kxzy->xzy', class_table, onehot, precision=lax.Precision.HIGHEST)

def upper_cell(values_in, step_y):
    depth_cells = values_in.shape[2]
    across = values_in.shape[3]
    padded = jnp.pad(values_in, ((0, 0), (0, 0), (1, 0), (1, 1)))
    return padded[:, :, 0:depth_cells, 1 + step_y:1 + step_y + across]

def lower_cell(values_in, step_y):
    depth_cells = values_in.shape[2]
    across = values_in.shape[3]
    padded = jnp.pad(values_in, ((0, 0), (0, 0), (0, 1), (1, 1)))
    return padded[:, :, 1:depth_cells + 1, 1 - step_y:1 - step_y + across]

def adjoint(arc_duals, from_left, from_right, bound_duals):
    result = lax.optimization_barrier(jnp.sum(arc_duals, axis=0)) + bound_duals
    for arc_index, (step_x, step_y) in enumerate(ARC_OFFSETS):
        source = arc_duals[arc_index]
        if step_x == 1:
            source = jnp.concatenate([from_left, source[:-1]], axis=0)
        elif step_x == -1:
            source = jnp.concatenate([source[1:], from_right], axis=0)
        result = result - lower_cell(source, step_y)
    return result

def reference(u_start, dual_prec, dual_bound, dual_cap, capacity, block_value, ton_class, density, slope_code, omega_start):
    arc_active = arc_masks(slope_code, 0, NX, NZ, NY)[:, :, None]
    tonnage_grid = tonnage(ton_class, density)
    tons_col = tonnage_grid[:, None]
    tons_all = jnp.sum(tonnage_grid)
    blocks_all = float(NX * NY * NZ)
    root_blocks = math.sqrt(blocks_all)
    period_ids = jnp.arange(NP).astype(jnp.float32)[None, :, None, None]
    profit = block_value[:, None] * jnp.exp(-RATE * period_ids)
    zero_rim = jnp.zeros((1, NP, NZ, NY), jnp.float32)
    primal = u_start
    arc_duals = dual_prec * arc_active
    bound_duals = dual_bound
    cap_duals = dual_cap
    weight = omega_start[0]
    for restart in range(OUTER):
        primal_first, duals_first, bound_first, cap_first = (primal, arc_duals, bound_duals, cap_duals)
        primal_sum = jnp.zeros_like(primal)
        duals_sum = jnp.zeros_like(arc_duals)
        bound_sum = jnp.zeros_like(bound_duals)
        cap_sum = jnp.zeros_like(cap_duals)
        for sweep_index in range(INNER):
            gradient_x = adjoint(arc_duals, zero_rim, zero_rim, bound_duals)
            gradient_u = jnp.flip(jnp.cumsum(jnp.flip(gradient_x, 1), axis=1), 1) + tons_col * cap_duals[None, :, None, None] / root_blocks
            step_primal = 1.0 / (weight * (SLOPE * (NP - period_ids) + tons_col / root_blocks))
            primal_new = jnp.maximum(primal - step_primal * (gradient_u - profit), 0.0)
            extrapolated = 2.0 * primal_new - primal
            cumulative = jnp.cumsum(extrapolated, axis=1)
            padded = jnp.pad(cumulative, ((1, 1), (0, 0), (0, 0), (0, 0)))
            step_prec = weight / (2.0 * (period_ids + 1.0))
            step_bound = weight / (period_ids + 1.0)
            new_list = []
            for arc_index, (step_x, step_y) in enumerate(ARC_OFFSETS):
                ahead_cells = upper_cell(padded[1 + step_x:1 + step_x + NX], step_y)
                new_list.append(jnp.maximum(arc_duals[arc_index] + step_prec * (cumulative - ahead_cells), 0.0) * arc_active[arc_index])
            duals_new = jnp.stack(new_list)
            bound_new = jnp.maximum(bound_duals + step_bound * (cumulative - 1.0), 0.0)
            row_total = jnp.einsum('xzy,xtzy->t', tonnage_grid, extrapolated, precision=lax.Precision.HIGHEST)
            cap_new = jnp.maximum(cap_duals + weight * (row_total - blocks_all * capacity) / tons_all, 0.0)
            primal_sum = primal_sum + primal_new
            duals_sum = duals_sum + duals_new
            bound_sum = bound_sum + bound_new
            cap_sum = cap_sum + cap_new
            primal, arc_duals, bound_duals, cap_duals = (primal_new, duals_new, bound_new, cap_new)
        primal = primal_sum / INNER
        arc_duals = duals_sum / INNER
        bound_duals = bound_sum / INNER
        cap_duals = cap_sum / INNER
        primal_move = jnp.sum((primal - primal_first) ** 2)
        dual_move = jnp.sum((arc_duals - duals_first) ** 2) + jnp.sum((bound_duals - bound_first) ** 2) + jnp.sum((cap_duals - cap_first) ** 2)
        weight = jnp.sqrt(weight * jnp.sqrt((dual_move + EPS) / (primal_move + EPS)))
    return (primal, arc_duals, bound_duals, cap_duals, jnp.reshape(weight, (1,)))
```

```python
import functools
import math

import jax
import jax.numpy as jnp
from jax import lax
from jax.experimental import pallas as pl
from jax.experimental.pallas import tpu as pltpu
from jax.sharding import PartitionSpec as P

OUTER = 2
INNER = 3
STEPS = OUTER * INNER
RATE = math.log(1.1) / 12.0
EPS = 1e-06
SLOPE = 11.0
MESH = pl.DeviceIdType.MESH
ROWS = 8
CHUNK = 8


def kernel(
    NS, NPD, T, Z, Y, R,
    u_ref, prec_ref, bound_ref, cap_ref, capacity_ref, bv_ref, tc_ref, dens_ref, slope_ref, om_ref,
    u_out, prec_out, bound_out, cap_out, w_out,
    uf, uc, us, bf, bc, bs, fa, ca, sa, act, ton, tb, tl, cb, ex0,
    xs, xr, es, er, as_, ar, rs, rb, ps, pb, slr,
    praw, ti, to_sum, loc, ini_s, ini_r, xs_s, xs_r, e_s, e_r, a_s, a_r, r_s, r_r, p_s, p_r,
):
    me = lax.axis_index("strip")
    pe = lax.axis_index("period")
    total_rows = NS
    total_periods = NPD * T
    blocks_all = float(total_rows * Z * Y)
    root_blocks = math.sqrt(blocks_all)
    sends = []

    loads = (
        pltpu.make_async_copy(prec_ref.at[:, 0], praw, loc.at[0]),
        pltpu.make_async_copy(bound_ref.at[0], bf, loc.at[1]),
        pltpu.make_async_copy(u_ref.at[0], uf, loc.at[2]),
    )
    for load in loads:
        load.start()
    barrier = pltpu.get_barrier_semaphore()
    for k in range(1, NS):
        pl.semaphore_signal(barrier, inc=1, device_id={"strip": lax.rem(me + k, NS)}, device_id_type=MESH)
    for k in range(1, NPD):
        pl.semaphore_signal(barrier, inc=1, device_id={"period": lax.rem(pe + k, NPD)}, device_id_type=MESH)

    has = (me < NS - 1, me > 0)
    gets = (me > 0, me < NS - 1)
    to = (me + 1, me - 1)

    def remote(src, dst, ss, rr, dev):
        return pltpu.make_async_remote_copy(
            src_ref=src, dst_ref=dst, send_sem=ss, recv_sem=rr, device_id=dev, device_id_type=MESH
        )

    def ini_copy(d, what):
        if what == 2:
            return remote(to_sum.at[d], ti.at[d], ini_s.at[d, 2], ini_r.at[d, 2], {"strip": to[d]})
        if what == 0:
            rest = pl.ds(1, T - 1)
            return remote(praw.at[1 + d, rest], fa.at[5 + d, rest], ini_s.at[d, 0], ini_r.at[d, 0], {"strip": to[d]})
        return remote(slope_ref, slr.at[d], ini_s.at[d, 1], ini_r.at[d, 1], {"strip": to[d]})

    def x_copy(d, part, s):
        lo, size = (1, T - 1) if part == 0 else (0, 1)
        return remote(
            xs.at[s, pl.ds(lo, size)], xr.at[d, s, pl.ds(lo, size)],
            xs_s.at[d, part, s], xs_r.at[d, part, s], {"strip": to[d]},
        )

    def e_copy(k, s):
        return remote(es.at[s], er.at[s, k - 1], e_s.at[s, k - 1], e_r.at[s, k - 1], {"period": pe + k})

    def a_copy(k, s):
        return remote(as_.at[s], ar.at[s, k - 1], a_s.at[s, k - 1], a_r.at[s, k - 1], {"period": pe - k})

    def r_copy(k, slot):
        return remote(
            rs.at[slot], rb.at[slot, me], r_s.at[slot, k - 1], r_r.at[slot, k - 1],
            {"strip": lax.rem(me + k, NS)},
        )

    def p_copy(k, slot):
        return remote(
            ps.at[slot], pb.at[slot, pe], p_s.at[slot, k - 1], p_r.at[slot, k - 1],
            {"period": lax.rem(pe + k, NPD)},
        )

    def start(cond, copy):
        def go():
            copy.start()
        if cond is None:
            go()
        else:
            pl.when(cond)(go)
        sends.append((cond, copy))

    def wait_recv(cond, copy):
        if cond is None:
            copy.wait_recv()
        else:
            pl.when(cond)(lambda: copy.wait_recv())

    def reduce_start(slot, value):
        rs[slot] = value
        rb[slot, me] = value
        for k in range(1, NS):
            start(None, r_copy(k, slot))

    def reduce_done(slot):
        for k in range(1, NS):
            wait_recv(None, r_copy(k, slot))
        total = rb[slot, 0]
        for k in range(1, NS):
            total = total + rb[slot, k]
        return total

    loads[0].wait()
    for d in range(2):
        total = praw[1 + d, 0]
        for t in range(1, T):
            total = total + praw[1 + d, t]
        to_sum[d] = total
    pl.semaphore_wait(barrier, NS + NPD - 2)
    for d in range(2):
        start(has[d], ini_copy(d, 1))
        start(has[d], ini_copy(d, 2))
    for d in range(2):
        start(has[d], ini_copy(d, 0))

    rows = lax.broadcasted_iota(jnp.int32, (R, Y), 0)
    lanes = lax.broadcasted_iota(jnp.int32, (R, Y), 1)

    def as_lanes(value):
        sums = jnp.sum(value, axis=1, keepdims=True)
        return jnp.sum(jnp.where(lanes == rows, sums, 0.0), axis=0, keepdims=True)

    def as_rows(line):
        return jnp.sum(jnp.where(lanes == rows, line, 0.0), axis=1, keepdims=True)

    def fold(v):
        return jnp.sum(v.reshape(Z // 8, 8, Y), axis=0)

    cls = tc_ref[0]
    tons = jnp.zeros((Z, Y), jnp.float32)
    for c in range(dens_ref.shape[0]):
        tons = jnp.where(cls == c, (1.0 + c) * dens_ref[c], tons)
    ton[...] = tons
    part = jnp.sum(tons, axis=0, keepdims=True)
    reduce_start(0, part)

    z_ids = lax.broadcasted_iota(jnp.int32, (Z, Y), 0)
    y_ids = lax.broadcasted_iota(jnp.int32, (Z, Y), 1)

    def mask_of(codes, k, inside):
        ok = z_ids >= 1
        if k > 0:
            ok = ok & (jnp.broadcast_to((codes >> (k - 1)) & 1, (Z, Y)) == 1)
        if k == 3:
            ok = ok & (y_ids < Y - 1)
        if k == 4:
            ok = ok & (y_ids >= 1)
        if inside is not None:
            ok = ok & (jnp.full((Z, Y), inside.astype(jnp.int32)) == 1)
        return ok.astype(jnp.float32)

    own = slope_ref[...]
    act[0] = mask_of(own, 0, None)
    act[1] = mask_of(own, 1, me < NS - 1)
    act[2] = mask_of(own, 2, me > 0)
    act[3] = mask_of(own, 3, None)
    act[4] = mask_of(own, 4, None)

    period = [(pe * T + t).astype(jnp.float32) for t in range(T)]
    pid = [jnp.full((1, Y), period[t]) for t in range(T)]
    disc = [jnp.exp(-RATE * pid[t]) for t in range(T)]
    tonr = ton[...] * (1.0 / root_blocks)
    for load in loads[1:]:
        load.wait()
    for t in range(T):
        tb[t] = 1.0 / (SLOPE * (total_periods - pid[t]) + tonr)
        for k in range(5):
            fa[k, t] = praw[k, t] * act[k]

    caps = jnp.zeros((R, Y), jnp.float32)
    climit = jnp.zeros((R, Y), jnp.float32)
    for t in range(T):
        caps = jnp.where(rows == t, cap_ref[t], caps)
        climit = jnp.where(rows == t, capacity_ref[t] * blocks_all, climit)
    w = jnp.full((1, Y), om_ref[0])

    for d in range(2):
        @pl.when(jnp.logical_not(gets[d]))
        def _():
            act[5 + d] = jnp.zeros((Z, Y), jnp.float32)
            ti[d] = jnp.zeros((Z, Y), jnp.float32)
            fa[5 + d] = jnp.zeros((T, Z, Y), jnp.float32)
            for s in range(STEPS):
                xr[d, s] = jnp.zeros((T, Z, Y), jnp.float32)

    def up_y(v):
        return pltpu.roll(v, 1, 1)

    def dn_y(v):
        return pltpu.roll(v, Y - 1, 1)

    def up_z(v):
        return pltpu.roll(v, 1, 0)

    def dn_z(v):
        return pltpu.roll(v, Z - 1, 0)

    def settle(first, cur, acc, at, j, new, old):
        if j == 0:
            cur[at] = new
            return new, None
        if j == 1:
            cur[at] = new
            acc[at] = old + new
            return new, None
        mean = (acc[at] + new) * (1.0 / INNER)
        diff = mean - first[at]
        first[at] = mean
        return mean, fold(diff * diff)

    def gradient_own(arcs, bounds):
        for t in range(T):
            p0, p3, p4 = arcs[0, t], arcs[3, t], arcs[4, t]
            back = p0 + (up_y(p3) + dn_y(p4))
            tl[t] = ((p0 + p3) + (p4 + bounds[t])) - dn_z(back)

    def gradient(s, arcs):
        tail = None
        for t in range(T - 1, -1, -1):
            g = (tl[t] + (arcs[1, t] + arcs[2, t])) - dn_z(arcs[5, t] + arcs[6, t])
            tail = g if tail is None else tail + g
            tl[t] = tail
        as_[s] = tail
        for k in range(1, NPD):
            start(pe >= k, a_copy(k, s))

    tail = None
    for t in range(T - 1, -1, -1):
        p = [fa[k, t] for k in range(5)]
        g = (((p[0] + p[1]) + (p[2] + p[3])) + p[4]) + bf[t]
        g = g - dn_z(p[0] + (up_y(p[3]) + dn_y(p[4])))
        tail = g if tail is None else tail + g
        tl[t] = tail
    for d in range(2):
        wait_recv(gets[d], ini_copy(d, 1))
        wait_recv(gets[d], ini_copy(d, 2))

        @pl.when(gets[d])
        def _():
            act[5 + d] = mask_of(slr[d], 1 + d, None)
    as_[0] = tl[0] - dn_z(ti[0] * act[5] + ti[1] * act[6])
    for k in range(1, NPD):
        start(pe >= k, a_copy(k, 0))
    for d in range(2):
        wait_recv(gets[d], ini_copy(d, 0))
        rest = ti[d]
        for t in range(1, T):
            plane = fa[5 + d, t]
            rest = rest - plane
            fa[5 + d, t] = plane * act[5 + d]
        fa[5 + d, 0] = rest * act[5 + d]
    tail = None
    for t in range(T - 1, -1, -1):
        back = fa[5, t] + fa[6, t]
        tail = back if tail is None else tail + back
        tl[t] = tl[t] - dn_z(tail)
    tons_all = jnp.sum(reduce_done(0), axis=1, keepdims=True)
    inv_tons = 1.0 / tons_all
    cap_first = cap_sum = None

    for s in range(STEPS):
        j = s % INNER
        u_src = uf if j == 0 else uc
        b_src = bf if j == 0 else bc
        p_src = fa if j == 0 else ca
        inv_w = 1.0 / w
        move_p = jnp.zeros((8, Y), jnp.float32)
        move_d = jnp.zeros((8, Y), jnp.float32)
        for k in range(1, NPD):
            @pl.when(pe + k < NPD)
            def _():
                a_copy(k, s).wait_recv()
                for t in range(T):
                    tl[t] = tl[t] + ar[s, k - 1]
        head = None
        row = jnp.zeros((R, Y), jnp.float32)
        for t in range(T):
            old = u_src[t]
            grad = tl[t] + (ton[...] * (1.0 / root_blocks)) * caps[t : t + 1, :]
            new = jnp.maximum(old - (tb[t] * inv_w) * (grad - bv_ref[0] * disc[t]), 0.0)
            ext = 2.0 * new - old
            _, moved = settle(uf, uc, us, t, j, new, old)
            if moved is not None:
                move_p = move_p + moved
            if t == 0:
                ex0[...] = ext
            else:
                xs[s, t] = ext
            head = ext if head is None else head + ext
            row = jnp.where(rows == t, jnp.sum(ton[...] * ext, axis=0, keepdims=True), row)
        es[s] = head
        for k in range(1, NPD):
            start(pe + k < NPD, e_copy(k, s))
        for d in range(2):
            start(has[d], x_copy(d, 0, s))
        for k in range(1, NPD):
            @pl.when(pe >= k)
            def _():
                e_copy(k, s).wait_recv()
                ex0[...] = ex0[...] + er[s, k - 1]
        xs[s, 0] = ex0[...]
        for d in range(2):
            start(has[d], x_copy(d, 1, s))
        reduce_start(1 + s, as_lanes(row))
        total = None
        for t in range(T):
            total = xs[s, t] if t == 0 else total + xs[s, t]
            cb[t] = total
        rate_b = [w / (pid[t] + 1.0) for t in range(T)]
        rate_p = [w / (2.0 * (pid[t] + 1.0)) for t in range(T)]

        def arc(k, t, diff, move):
            old = p_src[k, t]
            new = jnp.maximum(old + rate_p[t] * diff, 0.0) * act[k]
            _, moved = settle(fa, ca, sa, (k, t), j, new, old)
            if moved is not None and k < 5:
                move = move + moved
            return move

        for t in range(T):
            c = cb[t]
            old = b_src[t]
            new = jnp.maximum(old + rate_b[t] * (c - 1.0), 0.0)
            _, moved = settle(bf, bc, bs, t, j, new, old)
            if moved is not None:
                move_d = move_d + moved
            cz = up_z(c)
            move_d = arc(0, t, c - cz, move_d)
            move_d = arc(3, t, c - dn_y(cz), move_d)
            move_d = arc(4, t, c - up_y(cz), move_d)
        last = j == INNER - 1
        if s < STEPS - 1:
            gradient_own(fa if last else ca, bf if last else bc)
        for part in range(2):
            for d in range(2):
                wait_recv(gets[d], x_copy(d, part, s))
        total_m = total_p = None
        for t in range(T):
            total_m = xr[0, s, t] if t == 0 else total_m + xr[0, s, t]
            total_p = xr[1, s, t] if t == 0 else total_p + xr[1, s, t]
            c = cb[t]
            cz = up_z(c)
            move_d = arc(1, t, c - up_z(total_p), move_d)
            move_d = arc(2, t, c - up_z(total_m), move_d)
            if s < STEPS - 1:
                arc(5, t, total_m - cz, None)
                arc(6, t, total_p - cz, None)
        if s < STEPS - 1:
            gradient(s + 1, fa if last else ca)
        if last:
            cyc = s // INNER
            mp = jnp.sum(move_p, axis=0, keepdims=True)
            md = jnp.sum(move_d, axis=0, keepdims=True)
            reduce_start(1 + STEPS + cyc, as_lanes(jnp.where(rows == 0, mp, jnp.where(rows == 1, md, 0.0))))
        row_total = as_rows(reduce_done(1 + s))
        new_caps = jnp.maximum(caps + w * ((row_total - climit) * inv_tons), 0.0)
        new_caps = jnp.where(rows < T, new_caps, 0.0)
        if j == 0:
            cap_first = caps
            cap_sum = new_caps
        else:
            cap_sum = cap_sum + new_caps
        caps = new_caps
        if last:
            caps = cap_sum * (1.0 / INNER)
            cap_move = jnp.sum((caps - cap_first) ** 2, axis=0, keepdims=True)
            got = reduce_done(1 + STEPS + cyc)
            msg = got + jnp.where(lanes[0:1] == 1, cap_move, 0.0)
            ps[cyc] = msg
            pb[cyc, pe] = msg
            for k in range(1, NPD):
                start(None, p_copy(k, cyc))
            if s == STEPS - 1:
                for t in range(T):
                    u_out[0, t] = uf[t]
                    bound_out[0, t] = bf[t]
                    for k in range(5):
                        prec_out[k, 0, t] = fa[k, t]
                    cap_out[t] = caps[t, 0]
            for k in range(1, NPD):
                wait_recv(None, p_copy(k, cyc))
            tot = pb[cyc, 0]
            for k in range(1, NPD):
                tot = tot + pb[cyc, k]
            tot = as_rows(tot)
            moved = jnp.sqrt((tot[1:2, :] + EPS) / (tot[0:1, :] + EPS))
            w = jnp.sqrt(w * moved)
    w_out[0] = w[0, 0]
    for cond, copy in sends:
        if cond is None:
            copy.wait_send()
        else:
            pl.when(cond)(lambda copy=copy: copy.wait_send())


def pair_kernel(
    NS, NPD, T, Z, Y,
    u_ref, prec_ref, bound_ref, cap_ref, capacity_ref, bv_ref, tc_ref, dens_ref, slope_ref, om_ref,
    u_out, prec_out, bound_out, cap_out, w_out,
    praw, hh, pu, pb, pp, hpr, nraw, hnr, bvb, tcb, slr,
    fa, ca, sa, fn, cn, sn, fh, ch, sh, bf, bc, bs, uf, uc, us,
    act, nact, hact, ton, tb, pr, tl, tt, rp, rh,
    xs, xr, hs, ls, zh, zl, dh, dl, rs, rb,
    loc, ini_s, ini_r, sl_s, sl_r, sm_s, sm_r, re_s, re_r,
    x_s, x_r, z_s, z_r, d_s, d_r, r_s, r_r, o_s, o_r,
):
    me = lax.axis_index("strip")
    pe = lax.axis_index("period")
    pairs, NP, NQ = NS // 2, NPD * T, 2 * NPD
    NT = NP // ROWS
    ND = NS * NPD
    a, h = me // 2, lax.rem(me, 2)
    q = jnp.where(h == 0, pe, NQ - 1 - pe)
    blocks_all = float(NS * Z * Y)
    inv_root = 1.0 / math.sqrt(blocks_all)
    sends = []

    def rows_of(block):
        return pl.ds(pl.multiple_of(ROWS * block, ROWS), ROWS)

    def block_of(hh_, pp_):
        return jnp.where(hh_ == 0, pp_, NQ - 1 - pp_)

    def device_at(pair, block):
        first = block < NPD
        return {
            "strip": 2 * pair + jnp.where(first, 0, 1),
            "period": jnp.where(first, block, NQ - 1 - block),
        }

    def remote(src, dst, ss, rr, dev):
        return pltpu.make_async_remote_copy(
            src_ref=src, dst_ref=dst, send_sem=ss, recv_sem=rr, device_id=dev, device_id_type=MESH
        )

    def start(cond, copy):
        if cond is None:
            copy.start()
        else:
            pl.when(cond)(lambda: copy.start())
        sends.append((cond, copy))

    def wait_recv(cond, copy):
        if cond is None:
            copy.wait_recv()
        else:
            pl.when(cond)(lambda: copy.wait_recv())

    mine = pl.ds(pe * T, T)
    loads = (
        pltpu.make_async_copy(prec_ref.at[:, 0], praw, loc.at[0]),
        pltpu.make_async_copy(prec_ref.at[:, 0, :, rows_of(q)], pp.at[:, h, mine], loc.at[1]),
        pltpu.make_async_copy(bound_ref.at[0, :, rows_of(q)], pb.at[h, mine], loc.at[2]),
        pltpu.make_async_copy(u_ref.at[0, :, rows_of(q)], pu.at[h, mine], loc.at[3]),
        pltpu.make_async_copy(bv_ref.at[0, rows_of(q)], bvb.at[h], loc.at[4]),
        pltpu.make_async_copy(tc_ref.at[0, rows_of(q)], tcb.at[h], loc.at[5]),
    )
    for load in loads:
        load.start()
    barrier = pltpu.get_barrier_semaphore()
    others = [divmod(k, NPD) for k in range(1, ND)]

    def other(ks, kp):
        return {"strip": lax.rem(me + ks, NS), "period": lax.rem(pe + kp, NPD)}

    for ks, kp in others:
        pl.semaphore_signal(barrier, inc=1, device_id=other(ks, kp), device_id_type=MESH)

    mates = [divmod(k, NPD) for k in range(1, NQ)]

    def mate(i):
        kh, kp = mates[i]
        return lax.rem(h + kh, 2), lax.rem(pe + kp, NPD)

    def in_copy(i, what):
        th, tp = mate(i)
        rows = rows_of(block_of(th, tp))
        dev = {"strip": 2 * a + th, "period": tp}
        ss, rr = ini_s.at[i, what], ini_r.at[i, what]
        if what == 0:
            return remote(prec_ref.at[pl.ds(1, 2), 0, :, rows], pp.at[pl.ds(1, 2), h, mine], ss, rr, dev)
        if what == 1:
            return remote(hh.at[block_of(th, tp)], hpr.at[pe, h], ss, rr, dev)
        if what == 2:
            return remote(prec_ref.at[0, 0, :, rows], pp.at[0, h, mine], ss, rr, dev)
        if what == 3:
            return remote(prec_ref.at[pl.ds(3, 2), 0, :, rows], pp.at[pl.ds(3, 2), h, mine], ss, rr, dev)
        if what == 4:
            return remote(bound_ref.at[0, :, rows], pb.at[h, mine], ss, rr, dev)
        return remote(u_ref.at[0, :, rows], pu.at[h, mine], ss, rr, dev)

    def partner_copy(what):
        rows = rows_of(block_of(1 - h, pe))
        dev = {"strip": 2 * a + 1 - h, "period": pe}
        if what == 0:
            return remote(tc_ref.at[0, rows], tcb.at[h], sm_s.at[0], sm_r.at[0], dev)
        return remote(bv_ref.at[0, rows], bvb.at[h], sm_s.at[1], sm_r.at[1], dev)

    has = (a > 0, a < pairs - 1)

    def slope_copy(what):
        if what == 0:
            return remote(slope_ref, slr.at[1 + h], sl_s.at[0], sl_r.at[0], {"strip": 2 * a + 1 - h, "period": pe})
        away = jnp.where(h == 0, a - 1, a + 1)
        return remote(
            slope_ref, slr.at[3 * (1 - h)], sl_s.at[what], sl_r.at[2 - h],
            {"strip": 2 * away + what - 1, "period": pe},
        )

    def slope_wait(d):
        return remote(slope_ref, slr.at[3 * d], sl_s.at[1], sl_r.at[1 + d], {"strip": lax.rem(me + 1, NS), "period": pe})

    has_away = jnp.where(h == 0, a - 1, pairs - 2 - a) >= 0

    def relay_copy(d, what):
        dev = device_at(a - 1 if d == 0 else a + 1, q)
        k, hs_ = (2, 0) if d == 0 else (1, 1)
        ss, rr = re_s.at[d, what], re_r.at[d, what]
        if what == 0:
            return remote(pp.at[k, hs_], nraw.at[1 - d], ss, rr, dev)
        return remote(hpr.at[:, hs_, k], hnr.at[1 - d], ss, rr, dev)

    def reduce_copy(i, slot):
        return remote(rs.at[slot], rb.at[slot, me * NPD + pe], r_s.at[slot, i], r_r.at[slot, i], other(*others[i]))

    def reduce_start(slot, value):
        rs[slot] = value
        rb[slot, me * NPD + pe] = value
        for i in range(ND - 1):
            start(None, reduce_copy(i, slot))

    def reduce_done(slot):
        for i in range(ND - 1):
            wait_recv(None, reduce_copy(i, slot))
        parts = [rb[slot, i] for i in range(ND)]
        while len(parts) > 1:
            parts = [parts[i] + parts[i + 1] if i + 1 < len(parts) else parts[i] for i in range(0, len(parts), 2)]
        return parts[0]

    def x_copy(d, s):
        dev = device_at(a - 1 if d == 0 else a + 1, q)
        return remote(xs.at[s, d], xr.at[s, 1 - d], x_s.at[s, d], x_r.at[s, 1 - d], dev)

    def z_copy(d, s):
        if d == 0:
            return remote(ls.at[s], zl.at[s], z_s.at[s, 0], z_r.at[s, 0], device_at(a, q - 1))
        return remote(hs.at[s], zh.at[s], z_s.at[s, 1], z_r.at[s, 1], device_at(a, q + 1))

    def d_copy(d, e, s):
        dev = device_at(a - 1 if d == 0 else a + 1, q - 1 if e == 0 else q + 1)
        src, dst = (ls, dl) if e == 0 else (hs, dh)
        return remote(src.at[s, d], dst.at[s, 1 - d], d_s.at[s, d, e], d_r.at[s, 1 - d, e], dev)

    def out_copy(i, what):
        th, tp = mate(i)
        dev = {"strip": 2 * a + th, "period": tp}
        part = pl.ds(tp * T, T)
        ss, rr = o_s.at[i, what], o_r.at[i, what]
        rows = rows_of(q)
        if what == 5:
            return remote(uf.at[th, part], u_out.at[0, :, rows], ss, rr, dev)
        if what == 6:
            return remote(bf.at[th, part], bound_out.at[0, :, rows], ss, rr, dev)
        return remote(fa.at[what, th, part], prec_out.at[what, 0, :, rows], ss, rr, dev)

    up = (q > 0, q < NQ - 1)

    for d in range(2):
        @pl.when(jnp.logical_not(has[d]))
        def _():
            for s in range(STEPS):
                xr[s, d] = jnp.zeros((NP, ROWS, Y), jnp.float32)
            nraw[d] = jnp.zeros((NP, ROWS, Y), jnp.float32)
            hnr[d] = jnp.zeros((NPD, T, Y), jnp.float32)
            slr[3 * d] = jnp.zeros((1, Y), jnp.int32)
        for e in range(2):
            buf = (dh, dl)[e]

            @pl.when(jnp.logical_not(has[d] & up[e]))
            def _():
                for s in range(STEPS):
                    buf[s, d] = jnp.zeros((NT, ROWS, Y), jnp.float32)
    for e in range(2):
        buf = (zh, zl)[e]

        @pl.when(jnp.logical_not(up[e]))
        def _():
            for s in range(STEPS):
                buf[s] = jnp.zeros((2, NT, ROWS, Y), jnp.float32)

    lanes1 = lax.broadcasted_iota(jnp.int32, (1, Y), 1)
    rows = lax.broadcasted_iota(jnp.int32, (NP, Y), 0)
    lanes = lax.broadcasted_iota(jnp.int32, (NP, Y), 1)

    def tons_of(cls):
        tons = jnp.zeros(cls.shape, jnp.float32)
        for c in range(dens_ref.shape[0]):
            tons = jnp.where(cls == c, (1.0 + c) * dens_ref[c], tons)
        return tons

    def as_lanes(value):
        sums = jnp.sum(value, axis=1, keepdims=True)
        return jnp.sum(jnp.where(lanes == rows, sums, 0.0), axis=0, keepdims=True)

    def as_rows(line, at=0):
        return jnp.broadcast_to(jnp.sum(jnp.where(lanes == rows + at, line, 0.0), axis=1, keepdims=True), (NP, Y))

    slr[1 + h] = slope_ref[...]
    loads[0].wait()
    for b in range(NQ):
        if b + 1 < NQ:
            for k in range(5):
                for t in range(T):
                    hh[b, k, pl.ds(t, 1)] = praw[k, t, pl.ds(ROWS * (b + 1), 1)]
        else:
            hh[b] = jnp.zeros((5, T, Y), jnp.float32)
    hpr[pe, h] = hh[q]
    deep = Z // NPD
    strip_part = tons_of(tc_ref[0, pl.ds(pl.multiple_of(pe * deep, ROWS), deep)])
    strip_part = jnp.sum(jnp.sum(strip_part, axis=0, keepdims=True), axis=1, keepdims=True)
    line = jnp.where(lanes1 == 2 * NP, strip_part, 0.0)
    lead = jnp.where(me == 0, 1.0, 0.0)
    for t in range(T):
        line = jnp.where(lanes1 == pe * T + t, cap_ref[t] * lead, line)
        line = jnp.where(lanes1 == NP + pe * T + t, capacity_ref[t] * lead, line)

    pl.semaphore_wait(barrier, ND - 1)
    for i in range(NQ - 1):
        start(None, in_copy(i, 0))
    for i in range(NQ - 1):
        start(None, in_copy(i, 1))
    start(None, slope_copy(0))
    for what in (1, 2):
        start(has_away, slope_copy(what))
    start(None, partner_copy(0))
    start(None, partner_copy(1))
    reduce_start(0, line)
    for what in range(2, 6):
        for i in range(NQ - 1):
            start(None, in_copy(i, what))

    z_ids = lax.broadcasted_iota(jnp.int32, (ROWS, Y), 0)
    y_ids = lax.broadcasted_iota(jnp.int32, (ROWS, Y), 1)
    low = z_ids == ROWS - 1

    def mask_of(code, k, depth, inside):
        ok = (depth >= 1) & (depth < Z)
        if k > 0:
            ok = ok & (jnp.broadcast_to((code >> (k - 1)) & 1, (ROWS, Y)) == 1)
        if k == 3:
            ok = ok & (y_ids < Y - 1)
        if k == 4:
            ok = ok & (y_ids >= 1)
        if inside is not None:
            ok = ok & (jnp.full((ROWS, Y), inside.astype(jnp.int32)) == 1)
        return ok.astype(jnp.float32)

    wait_recv(None, slope_copy(0))
    here, below = z_ids + ROWS * q, jnp.full((ROWS, Y), ROWS * (q + 1))
    for hh_ in range(2):
        code = slr[1 + hh_]
        for k in range(5):
            inside = None
            if k == 1 and hh_ == 1:
                inside = has[1]
            if k == 2 and hh_ == 0:
                inside = has[0]
            act[k, hh_] = mask_of(code, k, here, inside)
            hact[k, hh_] = mask_of(code, k, below, inside)
    for d in range(2):
        wait_recv(has[d], slope_wait(d))
        nact[d] = mask_of(slr[3 * d], 1 + d, here + 1, has[d])

    wait_recv(None, partner_copy(0))
    wait_recv(None, partner_copy(1))
    loads[4].wait()
    loads[5].wait()
    for hh_ in range(2):
        tons = tons_of(tcb[hh_])
        ton[hh_] = tons
        for t in range(NP):
            tb[hh_, t] = 1.0 / (SLOPE * (NP - t) + tons * inv_root)
            pr[hh_, t] = bvb[hh_] * math.exp(-RATE * t)

    t_plane = lax.broadcasted_iota(jnp.int32, (NP, ROWS, Y), 0).astype(jnp.float32)
    t_rows = (
        lax.broadcasted_iota(jnp.int32, (NT, ROWS, Y), 0) * ROWS + lax.broadcasted_iota(jnp.int32, (NT, ROWS, Y), 1)
    ).astype(jnp.float32)

    w = jnp.full((1, Y), om_ref[0])

    def set_rates(w):
        rp[...] = w[None] / (2.0 * (t_plane + 1.0))
        rh[...] = w[None] / (2.0 * (t_rows + 1.0))

    set_rates(w)

    loads[1].wait()
    for i in range(NQ - 1):
        wait_recv(None, in_copy(i, 0))
    for d in range(2):
        start(has[d], relay_copy(d, 0))
    for i in range(NQ - 1):
        wait_recv(None, in_copy(i, 1))
    for d in range(2):
        start(has[d], relay_copy(d, 1))

    chunks = [(lo, min(CHUNK, NP - lo)) for lo in range(0, NP, CHUNK)]

    def roll(v, by, axis):
        return pltpu.roll(v, by % v.shape[axis], axis)

    def up_y(v):
        return roll(v, 1, v.ndim - 1)

    def dn_y(v):
        return roll(v, -1, v.ndim - 1)

    def lines(ref, lo, size, *at):
        picked = [ref[(*at, t // ROWS, pl.ds(t % ROWS, 1))] for t in range(lo, lo + size)]
        return jnp.stack([jnp.broadcast_to(p, (ROWS, Y)) for p in picked])

    def from_above(v, line):
        return jnp.where(lax.broadcasted_iota(jnp.int32, v.shape, 1) == 0, line, roll(v, 1, 1))

    def from_below(v, line):
        return jnp.where(lax.broadcasted_iota(jnp.int32, v.shape, 1) == ROWS - 1, line, roll(v, -1, 1))

    def mask_arcs(ks):
        for k in ks:
            for hh_ in range(2):
                fa[k, hh_] = pp[k, hh_] * act[k, hh_][None]

    mask_arcs((1, 2))
    for i in range(NQ - 1):
        wait_recv(None, in_copy(i, 2))
    mask_arcs((0,))
    for i in range(NQ - 1):
        wait_recv(None, in_copy(i, 3))
    mask_arcs((3, 4))
    for k in range(5):
        for hh_ in range(2):
            for p in range(NPD):
                for t in range(T):
                    at = p * T + t
                    fh[k, hh_, at // ROWS, pl.ds(at % ROWS, 1)] = hpr[p, hh_, k, pl.ds(t, 1)] * hact[k, hh_, 0:1]
    for d in range(2):
        wait_recv(has[d], relay_copy(1 - d, 0))
        wait_recv(has[d], relay_copy(1 - d, 1))
        for t in range(NP):
            edge = jnp.broadcast_to(hnr[d, t // T, pl.ds(t % T, 1)], (ROWS, Y))
            fn[d, t] = jnp.where(low, edge, roll(nraw[d, t], -1, 0)) * nact[d]
    loads[2].wait()
    for i in range(NQ - 1):
        wait_recv(None, in_copy(i, 4))

    def settle(first, cur, acc, at, j, new, old):
        if j == 0:
            cur[at] = new
            return None
        if j == 1:
            cur[at] = new
            acc[at] = old + new
            return None
        mean = (acc[at] + new) * (1.0 / INNER)
        diff = mean - first[at]
        first[at] = mean
        return jnp.sum(diff * diff, axis=0)

    def gradient(arcs, near, halo, bounds):
        for hh_ in range(2):
            k_in = 2 if hh_ == 0 else 1
            edge = (halo[0, hh_] + halo[k_in, 1 - hh_]) + (up_y(halo[3, hh_]) + dn_y(halo[4, hh_]))
            hs_tmp = edge
            tail = None
            for lo, size in reversed(chunks):
                at = pl.ds(lo, size)
                p0, p3, p4 = arcs[0, hh_, at], arcs[3, hh_, at], arcs[4, hh_, at]
                back = (p0 + arcs[k_in, 1 - hh_, at]) + (up_y(p3) + dn_y(p4))
                rows_below = jnp.stack([
                    jnp.broadcast_to(hs_tmp[t // ROWS, t % ROWS : t % ROWS + 1], (ROWS, Y)) for t in range(lo, lo + size)
                ])
                g = ((p0 + p3) + (p4 + bounds[hh_, at])) + (arcs[1, hh_, at] + arcs[2, hh_, at])
                g = g - (from_below(back, rows_below) + near[hh_, at])
                for t in range(lo + size - 1, lo - 1, -1):
                    tail = g[t - lo] if tail is None else tail + g[t - lo]
                    tl[hh_, t] = tail

    gradient(fa, fn, fh, pb)
    loads[3].wait()
    for i in range(NQ - 1):
        wait_recv(None, in_copy(i, 5))
    got = reduce_done(0)
    caps = as_rows(got)
    climit = as_rows(got, NP) * blocks_all
    inv_tons = 1.0 / jnp.sum(jnp.where(lanes1 == 2 * NP, got, 0.0), axis=1, keepdims=True)
    cap_first = cap_sum = None

    for s in range(STEPS):
        j = s % INNER
        last, final = j == INNER - 1, s == STEPS - 1
        u_src = (pu if s == 0 else uf) if j == 0 else uc
        b_src = (pb if s == 0 else bf) if j == 0 else bc
        p_src, n_src, h_src = (fa, fn, fh) if j == 0 else (ca, cn, ch)
        u_first, b_first = (pu, pb) if s < INNER else (uf, bf)
        inv_w = 1.0 / w
        move_p = jnp.zeros((ROWS, Y), jnp.float32)
        move_d = jnp.zeros((ROWS, Y), jnp.float32)
        if j == 0:
            for hh_ in range(2):
                for t in range(NP):
                    tau = tb[hh_, t] * inv_w
                    tt[hh_, t] = tau * (ton[hh_] * inv_root)
                    tl[hh_, t] = u_src[hh_, t] - tau * (tl[hh_, t] - pr[hh_, t])
        row = jnp.zeros((NP, Y), jnp.float32)
        heads = [None, None]
        for t in range(NP):
            mined = None
            for hh_ in range(2):
                old = u_src[hh_, t]
                new = jnp.maximum(tl[hh_, t] - tt[hh_, t] * caps[t : t + 1, :], 0.0)
                ext = 2.0 * new - old
                if j == 0:
                    uc[hh_, t] = new
                elif j == 1:
                    uc[hh_, t] = new
                    us[hh_, t] = old + new
                else:
                    mean = (us[hh_, t] + new) * (1.0 / INNER)
                    diff = mean - u_first[hh_, t]
                    uf[hh_, t] = mean
                    move_p = move_p + diff * diff
                heads[hh_] = ext if t == 0 else heads[hh_] + ext
                xs[s, hh_, t] = heads[hh_]
                hs[s, hh_, t // ROWS, pl.ds(t % ROWS, 1)] = heads[hh_][ROWS - 1 : ROWS]
                if not final:
                    ls[s, hh_, t // ROWS, pl.ds(t % ROWS, 1)] = heads[hh_][0:1]
                part = ton[hh_] * ext
                mined = part if mined is None else mined + part
            row = jnp.where(rows == t, jnp.sum(mined, axis=0, keepdims=True), row)
        reduce_start(1 + s, as_lanes(row))
        start(up[1], z_copy(1, s))
        for d in range(2):
            start(has[d], x_copy(d, s))
        for d in range(2):
            start(has[d] & up[1], d_copy(d, 1, s))
        if not final:
            start(up[0], z_copy(0, s))
            for d in range(2):
                start(has[d] & up[0], d_copy(d, 0, s))
        if final:
            for i in range(NQ - 1):
                start(None, out_copy(i, 5))

        def arc(k, hh_, at, diff, move):
            old = p_src[k, hh_, at]
            new = jnp.maximum(old + rp[at] * diff, 0.0) * act[k, hh_][None]
            moved = settle(fa, ca, sa, (k, hh_, at), j, new, old)
            return move if moved is None else move + moved

        for hh_ in range(2):
            for lo, size in chunks:
                at = pl.ds(lo, size)
                old = b_src[hh_, at]
                new = jnp.maximum(old + 2.0 * rp[at] * (xs[s, hh_, at] - 1.0), 0.0)
                if j == 0:
                    bc[hh_, at] = new
                elif j == 1:
                    bc[hh_, at] = new
                    bs[hh_, at] = old + new
                else:
                    mean = (bs[hh_, at] + new) * (1.0 / INNER)
                    diff = mean - b_first[hh_, at]
                    bf[hh_, at] = mean
                    move_d = move_d + jnp.sum(diff * diff, axis=0)
        if final:
            for i in range(NQ - 1):
                start(None, out_copy(i, 6))
        wait_recv(up[0], z_copy(1, s))
        for lo, size in chunks:
            at = pl.ds(lo, size)
            c = [xs[s, hh_, at] for hh_ in range(2)]
            cz = [from_above(c[hh_], lines(zh, lo, size, s, hh_)) for hh_ in range(2)]
            for hh_ in range(2):
                move_d = arc(0, hh_, at, c[hh_] - cz[hh_], move_d)
                move_d = arc(3, hh_, at, c[hh_] - dn_y(cz[hh_]), move_d)
                move_d = arc(4, hh_, at, c[hh_] - up_y(cz[hh_]), move_d)
            move_d = arc(1, 0, at, c[0] - cz[1], move_d)
            move_d = arc(2, 1, at, c[1] - cz[0], move_d)
        if final:
            for i in range(NQ - 1):
                start(None, out_copy(i, 0))
        for d in range(2):
            wait_recv(has[d], x_copy(1 - d, s))
            wait_recv(has[d] & up[0], d_copy(1 - d, 1, s))
        for lo, size in chunks:
            at = pl.ds(lo, size)
            for d in range(2):
                cz = from_above(xr[s, d, at], lines(dh, lo, size, s, d))
                move_d = arc(2 - d, d, at, xs[s, d, at] - cz, move_d)
        if last:
            cyc = s // INNER
            mp = jnp.sum(move_p, axis=0, keepdims=True)
            md = jnp.sum(move_d, axis=0, keepdims=True)
            reduce_start(1 + STEPS + cyc, as_lanes(jnp.where(rows == 0, mp, jnp.where(rows == 1, md, 0.0))))
        if final:
            for what in range(1, 5):
                for i in range(NQ - 1):
                    start(None, out_copy(i, what))
        else:
            wait_recv(up[1], z_copy(0, s))
            for d in range(2):
                wait_recv(has[d] & up[1], d_copy(1 - d, 0, s))
            for lo, size in chunks:
                at = pl.ds(lo, size)
                for d in range(2):
                    old = n_src[d, at]
                    diff = from_below(xr[s, d, at], lines(dl, lo, size, s, d)) - xs[s, d, at]
                    new = jnp.maximum(old + rp[at] * diff, 0.0) * nact[d][None]
                    settle(fn, cn, sn, (d, at), j, new, old)
            for hh_ in range(2):
                c, cz = zl[s, hh_], hs[s, hh_]
                for k in (0, 3, 4, 1 + hh_):
                    ahead = (cz, hs[s, 1 - hh_], hs[s, 1 - hh_], dn_y(cz), up_y(cz))[k]
                    old = h_src[k, hh_]
                    new = jnp.maximum(old + rh[...] * (c - ahead), 0.0) * hact[k, hh_][None]
                    settle(fh, ch, sh, (k, hh_), j, new, old)
            if last:
                gradient(fa, fn, fh, bf)
            else:
                gradient(ca, cn, ch, bc)
                for hh_ in range(2):
                    for t in range(NP):
                        tau = tb[hh_, t] * inv_w
                        tl[hh_, t] = uc[hh_, t] - tau * (tl[hh_, t] - pr[hh_, t])
        row_total = as_rows(reduce_done(1 + s))
        new_caps = jnp.maximum(caps + w * ((row_total - climit) * inv_tons), 0.0)
        if j == 0:
            cap_first = caps
            cap_sum = new_caps
        else:
            cap_sum = cap_sum + new_caps
        caps = new_caps
        if last:
            caps = cap_sum * (1.0 / INNER)
            cap_move = jnp.sum((caps - cap_first) ** 2, axis=0, keepdims=True)
            if final:
                for t in range(T):
                    own = jnp.sum(jnp.where(rows == pe * T + t, caps, 0.0), axis=0, keepdims=True)
                    cap_out[t] = own[0, 0]
            tot = as_rows(reduce_done(1 + STEPS + cyc))
            moved = jnp.sqrt((tot[1:2, :] + cap_move + EPS) / (tot[0:1, :] + EPS))
            w = jnp.sqrt(w * moved)
            if not final:
                set_rates(w)
    w_out[0] = w[0, 0]
    u_out[0, :, rows_of(q)] = uf[h, mine]
    bound_out[0, :, rows_of(q)] = bf[h, mine]
    for k in range(5):
        prec_out[k, 0, :, rows_of(q)] = fa[k, h, mine]
    for what in range(7):
        for i in range(NQ - 1):
            wait_recv(None, out_copy(i, what))
    for cond, copy in sends:
        if cond is None:
            copy.wait_send()
        else:
            pl.when(cond)(lambda copy=copy: copy.wait_send())


def pair_call(NS, NPD, u, prec, bound, cap, capacity, bv, tc, dens, slope, om):
    _, T, Z, Y = u.shape
    f32 = jnp.float32
    NP, NQ, ND = NPD * T, 2 * NPD, NS * NPD
    NT = NP // ROWS
    vmem = pl.BlockSpec(memory_space=pltpu.VMEM)
    hbm = pl.BlockSpec(memory_space=pl.ANY)
    smem = pl.BlockSpec(memory_space=pltpu.SMEM)
    slots = 1 + STEPS + OUTER
    V = lambda *shape: pltpu.VMEM((*shape, Y), f32)
    whole = lambda *n: V(*n, NP, ROWS)
    edge = lambda *n: V(*n, NT, ROWS)
    dma = pltpu.SemaphoreType.DMA
    return pl.pallas_call(
        functools.partial(pair_kernel, NS, NPD, T, Z, Y),
        out_shape=(
            pltpu.VMEM(u.shape, f32),
            pltpu.VMEM(prec.shape, f32),
            pltpu.VMEM(bound.shape, f32),
            jax.ShapeDtypeStruct(cap.shape, f32),
            jax.ShapeDtypeStruct((1,), f32),
        ),
        in_specs=[hbm, hbm, hbm, smem, smem, vmem, vmem, smem, vmem, smem],
        out_specs=(vmem, vmem, vmem, smem, smem),
        scratch_shapes=[
            V(5, T, Z), V(NQ, 5, T), whole(2), whole(2), whole(5, 2), V(NPD, 2, 5, T), whole(2), V(2, NPD, T),
            V(2, ROWS), pltpu.VMEM((2, ROWS, Y), jnp.int32), pltpu.VMEM((4, 1, Y), jnp.int32),
            whole(5, 2), whole(5, 2), whole(5, 2), whole(2), whole(2), whole(2),
            edge(5, 2), edge(5, 2), edge(5, 2), whole(2), whole(2), whole(2), whole(2), whole(2), whole(2),
            V(5, 2, ROWS), V(2, ROWS), V(5, 2, ROWS), V(2, ROWS), whole(2), whole(2), whole(2), whole(2),
            whole(), edge(),
            whole(STEPS, 2), whole(STEPS, 2), edge(STEPS, 2), edge(STEPS, 2), edge(STEPS, 2), edge(STEPS, 2),
            edge(STEPS, 2), edge(STEPS, 2), V(slots, 1), V(slots, ND, 1),
            dma((6,)), dma((NQ - 1, 6)), dma((NQ - 1, 6)), dma((3,)), dma((3,)), dma((2,)), dma((2,)),
            dma((2, 2)), dma((2, 2)),
            dma((STEPS, 2)), dma((STEPS, 2)), dma((STEPS, 2)), dma((STEPS, 2)),
            dma((STEPS, 2, 2)), dma((STEPS, 2, 2)), dma((slots, ND - 1)), dma((slots, ND - 1)),
            dma((NQ - 1, 7)), dma((NQ - 1, 7)),
        ],
        compiler_params=pltpu.CompilerParams(collective_id=1, has_side_effects=True),
    )(u, prec, bound, cap, capacity, bv, tc, dens, slope, om)


def solution(mesh):
    NS, NPD = mesh.shape["strip"], mesh.shape["period"]

    def per_device(u, prec, bound, cap, capacity, bv, tc, dens, slope, om):
        rows_here, T, Z, Y = u.shape
        assert rows_here == 1
        NP = NPD * T
        if NS % 2 == 0 and Z == 2 * NPD * ROWS and NP % ROWS == 0 and 2 * NP < Y:
            return pair_call(NS, NPD, u, prec, bound, cap, capacity, bv, tc, dens, slope, om)
        R = -(-T // 8) * 8
        f32 = jnp.float32
        vmem = pl.BlockSpec(memory_space=pltpu.VMEM)
        hbm = pl.BlockSpec(memory_space=pl.ANY)
        smem = pl.BlockSpec(memory_space=pltpu.SMEM)
        plane = lambda *n: pltpu.VMEM((*n, Z, Y), f32)
        dma = pltpu.SemaphoreType.DMA
        slots = 1 + STEPS + OUTER
        far = max(NPD - 1, 1)
        return pl.pallas_call(
            functools.partial(kernel, NS, NPD, T, Z, Y, R),
            out_shape=(
                pltpu.VMEM(u.shape, f32),
                pltpu.VMEM(prec.shape, f32),
                pltpu.VMEM(bound.shape, f32),
                jax.ShapeDtypeStruct(cap.shape, f32),
                jax.ShapeDtypeStruct((1,), f32),
            ),
            in_specs=[hbm, hbm, hbm, smem, smem, vmem, vmem, smem, vmem, smem],
            out_specs=(vmem, vmem, vmem, smem, smem),
            scratch_shapes=[
                plane(T), plane(T), plane(T), plane(T), plane(T), plane(T),
                plane(7, T), plane(7, T), plane(7, T), plane(7), plane(), plane(T), plane(T), plane(T), plane(),
                plane(STEPS, T), plane(2, STEPS, T), plane(STEPS), plane(STEPS, far),
                plane(STEPS), plane(STEPS, far),
                pltpu.VMEM((slots, 1, Y), f32), pltpu.VMEM((slots, NS, 1, Y), f32),
                pltpu.VMEM((OUTER, 1, Y), f32), pltpu.VMEM((OUTER, NPD, 1, Y), f32),
                pltpu.VMEM((2, 1, Y), jnp.int32),
                plane(5, T), plane(2), plane(2), dma((3,)),
                dma((2, 3)), dma((2, 3)), dma((2, 2, STEPS)), dma((2, 2, STEPS)),
                dma((STEPS, far)), dma((STEPS, far)), dma((STEPS, far)), dma((STEPS, far)),
                dma((slots, NS - 1)), dma((slots, NS - 1)), dma((OUTER, far)), dma((OUTER, far)),
            ],
            compiler_params=pltpu.CompilerParams(collective_id=0, has_side_effects=True),
        )(u, prec, bound, cap, capacity, bv, tc, dens, slope, om)

    in_specs = (
        P("strip", "period", None, None),
        P(None, "strip", "period", None, None),
        P("strip", "period", None, None),
        P("period"),
        P("period"),
        P("strip", None, None),
        P("strip", None, None),
        P(),
        P("strip", None),
        P(),
    )
    out_specs = (
        P("strip", "period", None, None),
        P(None, "strip", "period", None, None),
        P("strip", "period", None, None),
        P("period"),
        P(),
    )
    return jax.shard_map(
        per_device, mesh=mesh, in_specs=in_specs, out_specs=out_specs, check_vma=False
    )
```

```python
import functools
import math

import jax
import jax.numpy as jnp
from jax import lax
from jax.experimental import pallas as pl
from jax.experimental.pallas import tpu as pltpu
from jax.sharding import PartitionSpec as P

OUTER = 2
INNER = 3
STEPS = OUTER * INNER
RATE = math.log(1.1) / 12.0
EPS = 1e-06
SLOPE = 11.0
MESH = pl.DeviceIdType.MESH
ROWS = 8
CHUNK = 8


def kernel(
    NS, NPD, T, Z, Y, R,
    u_ref, prec_ref, bound_ref, cap_ref, capacity_ref, bv_ref, tc_ref, dens_ref, slope_ref, om_ref,
    u_out, prec_out, bound_out, cap_out, w_out,
    uf, uc, us, bf, bc, bs, fa, ca, sa, act, ton, tb, tl, cb, ex0,
    xs, xr, es, er, as_, ar, rs, rb, ps, pb, slr,
    praw, ti, to_sum, loc, ini_s, ini_r, xs_s, xs_r, e_s, e_r, a_s, a_r, r_s, r_r, p_s, p_r,
):
    me = lax.axis_index("strip")
    pe = lax.axis_index("period")
    total_rows = NS
    total_periods = NPD * T
    blocks_all = float(total_rows * Z * Y)
    root_blocks = math.sqrt(blocks_all)
    sends = []

    loads = (
        pltpu.make_async_copy(prec_ref.at[:, 0], praw, loc.at[0]),
        pltpu.make_async_copy(bound_ref.at[0], bf, loc.at[1]),
        pltpu.make_async_copy(u_ref.at[0], uf, loc.at[2]),
    )
    for load in loads:
        load.start()
    barrier = pltpu.get_barrier_semaphore()
    for k in range(1, NS):
        pl.semaphore_signal(barrier, inc=1, device_id={"strip": lax.rem(me + k, NS)}, device_id_type=MESH)
    for k in range(1, NPD):
        pl.semaphore_signal(barrier, inc=1, device_id={"period": lax.rem(pe + k, NPD)}, device_id_type=MESH)

    has = (me < NS - 1, me > 0)
    gets = (me > 0, me < NS - 1)
    to = (me + 1, me - 1)

    def remote(src, dst, ss, rr, dev):
        return pltpu.make_async_remote_copy(
            src_ref=src, dst_ref=dst, send_sem=ss, recv_sem=rr, device_id=dev, device_id_type=MESH
        )

    def ini_copy(d, what):
        if what == 2:
            return remote(to_sum.at[d], ti.at[d], ini_s.at[d, 2], ini_r.at[d, 2], {"strip": to[d]})
        if what == 0:
            rest = pl.ds(1, T - 1)
            return remote(praw.at[1 + d, rest], fa.at[5 + d, rest], ini_s.at[d, 0], ini_r.at[d, 0], {"strip": to[d]})
        return remote(slope_ref, slr.at[d], ini_s.at[d, 1], ini_r.at[d, 1], {"strip": to[d]})

    def x_copy(d, part, s):
        lo, size = (1, T - 1) if part == 0 else (0, 1)
        return remote(
            xs.at[s, pl.ds(lo, size)], xr.at[d, s, pl.ds(lo, size)],
            xs_s.at[d, part, s], xs_r.at[d, part, s], {"strip": to[d]},
        )

    def e_copy(k, s):
        return remote(es.at[s], er.at[s, k - 1], e_s.at[s, k - 1], e_r.at[s, k - 1], {"period": pe + k})

    def a_copy(k, s):
        return remote(as_.at[s], ar.at[s, k - 1], a_s.at[s, k - 1], a_r.at[s, k - 1], {"period": pe - k})

    def r_copy(k, slot):
        return remote(
            rs.at[slot], rb.at[slot, me], r_s.at[slot, k - 1], r_r.at[slot, k - 1],
            {"strip": lax.rem(me + k, NS)},
        )

    def p_copy(k, slot):
        return remote(
            ps.at[slot], pb.at[slot, pe], p_s.at[slot, k - 1], p_r.at[slot, k - 1],
            {"period": lax.rem(pe + k, NPD)},
        )

    def start(cond, copy):
        def go():
            copy.start()
        if cond is None:
            go()
        else:
            pl.when(cond)(go)
        sends.append((cond, copy))

    def wait_recv(cond, copy):
        if cond is None:
            copy.wait_recv()
        else:
            pl.when(cond)(lambda: copy.wait_recv())

    def reduce_start(slot, value):
        rs[slot] = value
        rb[slot, me] = value
        for k in range(1, NS):
            start(None, r_copy(k, slot))

    def reduce_done(slot):
        for k in range(1, NS):
            wait_recv(None, r_copy(k, slot))
        total = rb[slot, 0]
        for k in range(1, NS):
            total = total + rb[slot, k]
        return total

    loads[0].wait()
    for d in range(2):
        total = praw[1 + d, 0]
        for t in range(1, T):
            total = total + praw[1 + d, t]
        to_sum[d] = total
    pl.semaphore_wait(barrier, NS + NPD - 2)
    for d in range(2):
        start(has[d], ini_copy(d, 1))
        start(has[d], ini_copy(d, 2))
    for d in range(2):
        start(has[d], ini_copy(d, 0))

    rows = lax.broadcasted_iota(jnp.int32, (R, Y), 0)
    lanes = lax.broadcasted_iota(jnp.int32, (R, Y), 1)

    def as_lanes(value):
        sums = jnp.sum(value, axis=1, keepdims=True)
        return jnp.sum(jnp.where(lanes == rows, sums, 0.0), axis=0, keepdims=True)

    def as_rows(line):
        return jnp.sum(jnp.where(lanes == rows, line, 0.0), axis=1, keepdims=True)

    def fold(v):
        return jnp.sum(v.reshape(Z // 8, 8, Y), axis=0)

    cls = tc_ref[0]
    tons = jnp.zeros((Z, Y), jnp.float32)
    for c in range(dens_ref.shape[0]):
        tons = jnp.where(cls == c, (1.0 + c) * dens_ref[c], tons)
    ton[...] = tons
    part = jnp.sum(tons, axis=0, keepdims=True)
    reduce_start(0, part)

    z_ids = lax.broadcasted_iota(jnp.int32, (Z, Y), 0)
    y_ids = lax.broadcasted_iota(jnp.int32, (Z, Y), 1)

    def mask_of(codes, k, inside):
        ok = z_ids >= 1
        if k > 0:
            ok = ok & (jnp.broadcast_to((codes >> (k - 1)) & 1, (Z, Y)) == 1)
        if k == 3:
            ok = ok & (y_ids < Y - 1)
        if k == 4:
            ok = ok & (y_ids >= 1)
        if inside is not None:
            ok = ok & (jnp.full((Z, Y), inside.astype(jnp.int32)) == 1)
        return ok.astype(jnp.float32)

    own = slope_ref[...]
    act[0] = mask_of(own, 0, None)
    act[1] = mask_of(own, 1, me < NS - 1)
    act[2] = mask_of(own, 2, me > 0)
    act[3] = mask_of(own, 3, None)
    act[4] = mask_of(own, 4, None)

    period = [(pe * T + t).astype(jnp.float32) for t in range(T)]
    pid = [jnp.full((1, Y), period[t]) for t in range(T)]
    disc = [jnp.exp(-RATE * pid[t]) for t in range(T)]
    tonr = ton[...] * (1.0 / root_blocks)
    for load in loads[1:]:
        load.wait()
    for t in range(T):
        tb[t] = 1.0 / (SLOPE * (total_periods - pid[t]) + tonr)
        for k in range(5):
            fa[k, t] = praw[k, t] * act[k]

    caps = jnp.zeros((R, Y), jnp.float32)
    climit = jnp.zeros((R, Y), jnp.float32)
    for t in range(T):
        caps = jnp.where(rows == t, cap_ref[t], caps)
        climit = jnp.where(rows == t, capacity_ref[t] * blocks_all, climit)
    w = jnp.full((1, Y), om_ref[0])

    for d in range(2):
        @pl.when(jnp.logical_not(gets[d]))
        def _():
            act[5 + d] = jnp.zeros((Z, Y), jnp.float32)
            ti[d] = jnp.zeros((Z, Y), jnp.float32)
            fa[5 + d] = jnp.zeros((T, Z, Y), jnp.float32)
            for s in range(STEPS):
                xr[d, s] = jnp.zeros((T, Z, Y), jnp.float32)

    def up_y(v):
        return pltpu.roll(v, 1, 1)

    def dn_y(v):
        return pltpu.roll(v, Y - 1, 1)

    def up_z(v):
        return pltpu.roll(v, 1, 0)

    def dn_z(v):
        return pltpu.roll(v, Z - 1, 0)

    def settle(first, cur, acc, at, j, new, old):
        if j == 0:
            cur[at] = new
            return new, None
        if j == 1:
            cur[at] = new
            acc[at] = old + new
            return new, None
        mean = (acc[at] + new) * (1.0 / INNER)
        diff = mean - first[at]
        first[at] = mean
        return mean, fold(diff * diff)

    def gradient_own(arcs, bounds):
        for t in range(T):
            p0, p3, p4 = arcs[0, t], arcs[3, t], arcs[4, t]
            back = p0 + (up_y(p3) + dn_y(p4))
            tl[t] = ((p0 + p3) + (p4 + bounds[t])) - dn_z(back)

    def gradient(s, arcs):
        tail = None
        for t in range(T - 1, -1, -1):
            g = (tl[t] + (arcs[1, t] + arcs[2, t])) - dn_z(arcs[5, t] + arcs[6, t])
            tail = g if tail is None else tail + g
            tl[t] = tail
        as_[s] = tail
        for k in range(1, NPD):
            start(pe >= k, a_copy(k, s))

    tail = None
    for t in range(T - 1, -1, -1):
        p = [fa[k, t] for k in range(5)]
        g = (((p[0] + p[1]) + (p[2] + p[3])) + p[4]) + bf[t]
        g = g - dn_z(p[0] + (up_y(p[3]) + dn_y(p[4])))
        tail = g if tail is None else tail + g
        tl[t] = tail
    for d in range(2):
        wait_recv(gets[d], ini_copy(d, 1))
        wait_recv(gets[d], ini_copy(d, 2))

        @pl.when(gets[d])
        def _():
            act[5 + d] = mask_of(slr[d], 1 + d, None)
    as_[0] = tl[0] - dn_z(ti[0] * act[5] + ti[1] * act[6])
    for k in range(1, NPD):
        start(pe >= k, a_copy(k, 0))
    for d in range(2):
        wait_recv(gets[d], ini_copy(d, 0))
        rest = ti[d]
        for t in range(1, T):
            plane = fa[5 + d, t]
            rest = rest - plane
            fa[5 + d, t] = plane * act[5 + d]
        fa[5 + d, 0] = rest * act[5 + d]
    tail = None
    for t in range(T - 1, -1, -1):
        back = fa[5, t] + fa[6, t]
        tail = back if tail is None else tail + back
        tl[t] = tl[t] - dn_z(tail)
    tons_all = jnp.sum(reduce_done(0), axis=1, keepdims=True)
    inv_tons = 1.0 / tons_all
    cap_first = cap_sum = None

    for s in range(STEPS):
        j = s % INNER
        u_src = uf if j == 0 else uc
        b_src = bf if j == 0 else bc
        p_src = fa if j == 0 else ca
        inv_w = 1.0 / w
        move_p = jnp.zeros((8, Y), jnp.float32)
        move_d = jnp.zeros((8, Y), jnp.float32)
        for k in range(1, NPD):
            @pl.when(pe + k < NPD)
            def _():
                a_copy(k, s).wait_recv()
                for t in range(T):
                    tl[t] = tl[t] + ar[s, k - 1]
        head = None
        row = jnp.zeros((R, Y), jnp.float32)
        for t in range(T):
            old = u_src[t]
            grad = tl[t] + (ton[...] * (1.0 / root_blocks)) * caps[t : t + 1, :]
            new = jnp.maximum(old - (tb[t] * inv_w) * (grad - bv_ref[0] * disc[t]), 0.0)
            ext = 2.0 * new - old
            _, moved = settle(uf, uc, us, t, j, new, old)
            if moved is not None:
                move_p = move_p + moved
            if t == 0:
                ex0[...] = ext
            else:
                xs[s, t] = ext
            head = ext if head is None else head + ext
            row = jnp.where(rows == t, jnp.sum(ton[...] * ext, axis=0, keepdims=True), row)
        es[s] = head
        for k in range(1, NPD):
            start(pe + k < NPD, e_copy(k, s))
        for d in range(2):
            start(has[d], x_copy(d, 0, s))
        for k in range(1, NPD):
            @pl.when(pe >= k)
            def _():
                e_copy(k, s).wait_recv()
                ex0[...] = ex0[...] + er[s, k - 1]
        xs[s, 0] = ex0[...]
        for d in range(2):
            start(has[d], x_copy(d, 1, s))
        reduce_start(1 + s, as_lanes(row))
        total = None
        for t in range(T):
            total = xs[s, t] if t == 0 else total + xs[s, t]
            cb[t] = total
        rate_b = [w / (pid[t] + 1.0) for t in range(T)]
        rate_p = [w / (2.0 * (pid[t] + 1.0)) for t in range(T)]

        def arc(k, t, diff, move):
            old = p_src[k, t]
            new = jnp.maximum(old + rate_p[t] * diff, 0.0) * act[k]
            _, moved = settle(fa, ca, sa, (k, t), j, new, old)
            if moved is not None and k < 5:
                move = move + moved
            return move

        for t in range(T):
            c = cb[t]
            old = b_src[t]
            new = jnp.maximum(old + rate_b[t] * (c - 1.0), 0.0)
            _, moved = settle(bf, bc, bs, t, j, new, old)
            if moved is not None:
                move_d = move_d + moved
            cz = up_z(c)
            move_d = arc(0, t, c - cz, move_d)
            move_d = arc(3, t, c - dn_y(cz), move_d)
            move_d = arc(4, t, c - up_y(cz), move_d)
        last = j == INNER - 1
        if s < STEPS - 1:
            gradient_own(fa if last else ca, bf if last else bc)
        for part in range(2):
            for d in range(2):
                wait_recv(gets[d], x_copy(d, part, s))
        total_m = total_p = None
        for t in range(T):
            total_m = xr[0, s, t] if t == 0 else total_m + xr[0, s, t]
            total_p = xr[1, s, t] if t == 0 else total_p + xr[1, s, t]
            c = cb[t]
            cz = up_z(c)
            move_d = arc(1, t, c - up_z(total_p), move_d)
            move_d = arc(2, t, c - up_z(total_m), move_d)
            if s < STEPS - 1:
                arc(5, t, total_m - cz, None)
                arc(6, t, total_p - cz, None)
        if s < STEPS - 1:
            gradient(s + 1, fa if last else ca)
        if last:
            cyc = s // INNER
            mp = jnp.sum(move_p, axis=0, keepdims=True)
            md = jnp.sum(move_d, axis=0, keepdims=True)
            reduce_start(1 + STEPS + cyc, as_lanes(jnp.where(rows == 0, mp, jnp.where(rows == 1, md, 0.0))))
        row_total = as_rows(reduce_done(1 + s))
        new_caps = jnp.maximum(caps + w * ((row_total - climit) * inv_tons), 0.0)
        new_caps = jnp.where(rows < T, new_caps, 0.0)
        if j == 0:
            cap_first = caps
            cap_sum = new_caps
        else:
            cap_sum = cap_sum + new_caps
        caps = new_caps
        if last:
            caps = cap_sum * (1.0 / INNER)
            cap_move = jnp.sum((caps - cap_first) ** 2, axis=0, keepdims=True)
            got = reduce_done(1 + STEPS + cyc)
            msg = got + jnp.where(lanes[0:1] == 1, cap_move, 0.0)
            ps[cyc] = msg
            pb[cyc, pe] = msg
            for k in range(1, NPD):
                start(None, p_copy(k, cyc))
            if s == STEPS - 1:
                for t in range(T):
                    u_out[0, t] = uf[t]
                    bound_out[0, t] = bf[t]
                    for k in range(5):
                        prec_out[k, 0, t] = fa[k, t]
                    cap_out[t] = caps[t, 0]
            for k in range(1, NPD):
                wait_recv(None, p_copy(k, cyc))
            tot = pb[cyc, 0]
            for k in range(1, NPD):
                tot = tot + pb[cyc, k]
            tot = as_rows(tot)
            moved = jnp.sqrt((tot[1:2, :] + EPS) / (tot[0:1, :] + EPS))
            w = jnp.sqrt(w * moved)
    w_out[0] = w[0, 0]
    for cond, copy in sends:
        if cond is None:
            copy.wait_send()
        else:
            pl.when(cond)(lambda copy=copy: copy.wait_send())


def pair_kernel(
    NS, NPD, T, Z, Y,
    u_ref, prec_ref, bound_ref, cap_ref, capacity_ref, bv_ref, tc_ref, dens_ref, slope_ref, om_ref,
    u_out, prec_out, bound_out, cap_out, w_out,
    praw, hh, pu, pb, pp, hpr, nraw, hnr, bvb, tcb, slr,
    fa, ca, sa, fn, cn, sn, fh, ch, sh, bf, bc, bs, uf, uc, us,
    act, nact, hact, ton, tb, pr, tl, tt, rp, rh,
    xs, xr, hs, ls, zh, zl, dh, dl, rs, rb,
    loc, ini_s, ini_r, sl_s, sl_r, sm_s, sm_r, re_s, re_r,
    x_s, x_r, z_s, z_r, d_s, d_r, r_s, r_r, o_s, o_r,
):
    me = lax.axis_index("strip")
    pe = lax.axis_index("period")
    pairs, NP, NQ = NS // 2, NPD * T, 2 * NPD
    NT = NP // ROWS
    ND = NS * NPD
    a, h = me // 2, lax.rem(me, 2)
    q = jnp.where(h == 0, pe, NQ - 1 - pe)
    blocks_all = float(NS * Z * Y)
    inv_root = 1.0 / math.sqrt(blocks_all)
    sends = []

    def rows_of(block):
        return pl.ds(pl.multiple_of(ROWS * block, ROWS), ROWS)

    def block_of(hh_, pp_):
        return jnp.where(hh_ == 0, pp_, NQ - 1 - pp_)

    def device_at(pair, block):
        first = block < NPD
        return {
            "strip": 2 * pair + jnp.where(first, 0, 1),
            "period": jnp.where(first, block, NQ - 1 - block),
        }

    def remote(src, dst, ss, rr, dev):
        return pltpu.make_async_remote_copy(
            src_ref=src, dst_ref=dst, send_sem=ss, recv_sem=rr, device_id=dev, device_id_type=MESH
        )

    def start(cond, copy):
        if cond is None:
            copy.start()
        else:
            pl.when(cond)(lambda: copy.start())
        sends.append((cond, copy))

    def wait_recv(cond, copy):
        if cond is None:
            copy.wait_recv()
        else:
            pl.when(cond)(lambda: copy.wait_recv())

    mine = pl.ds(pe * T, T)
    unit = h * NPD + pe
    peers = pl.ds(0, NQ - 1)
    loads = (
        pltpu.make_async_copy(prec_ref.at[:, 0], praw, loc.at[0]),
        pltpu.make_async_copy(prec_ref.at[:, 0, :, rows_of(q)], pp.at[:, unit], loc.at[1]),
        pltpu.make_async_copy(bound_ref.at[0, :, rows_of(q)], pb.at[unit], loc.at[2]),
        pltpu.make_async_copy(u_ref.at[0, :, rows_of(q)], pu.at[unit], loc.at[3]),
    )
    for load in loads:
        load.start()
    barrier = pltpu.get_barrier_semaphore()
    others = [divmod(k, NPD) for k in range(1, ND)]

    def other(ks, kp):
        return {"strip": lax.rem(me + ks, NS), "period": lax.rem(pe + kp, NPD)}

    for ks, kp in others:
        pl.semaphore_signal(barrier, inc=1, device_id=other(ks, kp), device_id_type=MESH)

    mates = [divmod(k, NPD) for k in range(1, NQ)]

    def mate(i):
        kh, kp = mates[i]
        return lax.rem(h + kh, 2), lax.rem(pe + kp, NPD)

    def in_ends(what, rows, block, at):
        if what == 1:
            return hh.at[block], hpr.at[at]
        if what == 4:
            return bound_ref.at[0, :, rows], pb.at[at]
        if what == 5:
            return u_ref.at[0, :, rows], pu.at[at]
        arcs = (pl.ds(1, 2), None, 0, pl.ds(3, 2))[what]
        return prec_ref.at[arcs, 0, :, rows], pp.at[arcs, at]

    def in_copy(i, what):
        th, tp = mate(i)
        block = block_of(th, tp)
        src, dst = in_ends(what, rows_of(block), block, unit)
        return remote(src, dst, ini_s.at[what], ini_r.at[what], {"strip": 2 * a + th, "period": tp})

    def in_all(what):
        dst = in_ends(what, rows_of(0), 0, peers)[1]
        return remote(dst, dst, ini_s.at[what], ini_r.at[what], other(0, 1))

    def partner_copy(what):
        rows = rows_of(block_of(1 - h, pe))
        dev = {"strip": 2 * a + 1 - h, "period": pe}
        if what == 0:
            return remote(tc_ref.at[0, rows], tcb.at[h], sm_s.at[0], sm_r.at[0], dev)
        return remote(bv_ref.at[0, rows], bvb.at[h], sm_s.at[1], sm_r.at[1], dev)

    has = (a > 0, a < pairs - 1)

    def slope_copy(what):
        if what == 0:
            return remote(slope_ref, slr.at[1 + h], sl_s.at[0], sl_r.at[0], {"strip": 2 * a + 1 - h, "period": pe})
        away = jnp.where(h == 0, a - 1, a + 1)
        return remote(
            slope_ref, slr.at[3 * (1 - h)], sl_s.at[what], sl_r.at[2 - h],
            {"strip": 2 * away + what - 1, "period": pe},
        )

    def slope_wait(d):
        return remote(slope_ref, slr.at[3 * d], sl_s.at[1], sl_r.at[1 + d], {"strip": lax.rem(me + 1, NS), "period": pe})

    has_away = jnp.where(h == 0, a - 1, pairs - 2 - a) >= 0

    def relay_copy(d, what):
        dev = device_at(a - 1 if d == 0 else a + 1, q)
        k, hs_ = (2, 0) if d == 0 else (1, 1)
        ss, rr = re_s.at[d, what], re_r.at[d, what]
        if what == 0:
            return remote(pp.at[k, pl.ds(hs_ * NPD, NPD)], nraw.at[1 - d], ss, rr, dev)
        return remote(hpr.at[pl.ds(hs_ * NPD, NPD), k], hnr.at[1 - d], ss, rr, dev)

    def reduce_sem(slot):
        return r_r.at[slot % 2 if slot <= STEPS else 2]

    def reduce_start(slot, value):
        rs[slot] = value
        rb[slot, me * NPD + pe] = value
        for ks, kp in others:
            remote(
                rs.at[slot], rb.at[slot, me * NPD + pe], r_s.at[0], reduce_sem(slot), other(ks, kp)
            ).start()

    def reduce_done(slot):
        rest = rb.at[slot, pl.ds(0, ND - 1)]
        remote(rest, rest, r_s.at[0], reduce_sem(slot), other(0, 1)).wait_recv()
        parts = [rb[slot, i] for i in range(ND)]
        while len(parts) > 1:
            parts = [parts[i] + parts[i + 1] if i + 1 < len(parts) else parts[i] for i in range(0, len(parts), 2)]
        return parts[0]

    def x_copy(d, s):
        dev = device_at(a - 1 if d == 0 else a + 1, q)
        return remote(xs.at[s, d], xr.at[s, 1 - d], x_s.at[d], x_r.at[s % 2, 1 - d], dev)

    def z_copy(d, s):
        if d == 0:
            return remote(ls.at[s], zl.at[s], z_s.at[0], z_r.at[s % 2, 0], device_at(a, q - 1))
        return remote(hs.at[s], zh.at[s], z_s.at[1], z_r.at[s % 2, 1], device_at(a, q + 1))

    def d_copy(d, e, s):
        dev = device_at(a - 1 if d == 0 else a + 1, q - 1 if e == 0 else q + 1)
        src, dst = (ls, dl) if e == 0 else (hs, dh)
        return remote(src.at[s, d], dst.at[s, 1 - d], d_s.at[d, e], d_r.at[s % 2, 1 - d, e], dev)

    def out_ends(what, th, part, rows):
        if what == 0:
            return uf.at[th, part], u_out.at[0, :, rows]
        if what == 1:
            return bf.at[th, part], bound_out.at[0, :, rows]
        arcs = (0, pl.ds(3, 2), pl.ds(1, 2))[what - 2]
        return fa.at[arcs, th, part], prec_out.at[arcs, 0, :, rows]

    def out_start(what):
        for i in range(NQ - 1):
            th, tp = mate(i)
            src, dst = out_ends(what, th, pl.ds(tp * T, T), rows_of(q))
            remote(src, dst, o_s.at[what], o_r.at[what], {"strip": 2 * a + th, "period": tp}).start()

    def out_all(what):
        dst = out_ends(what, 0, mine, pl.ds(0, ROWS * (NQ - 1)))[1]
        return remote(dst, dst, o_s.at[what], o_r.at[what], other(0, 1))

    up = (q > 0, q < NQ - 1)

    for d in range(2):
        @pl.when(jnp.logical_not(has[d]))
        def _():
            for s in range(STEPS):
                xr[s, d] = jnp.zeros((NP, ROWS, Y), jnp.float32)
            nraw[d] = jnp.zeros((NPD, T, ROWS, Y), jnp.float32)
            hnr[d] = jnp.zeros((NPD, T, Y), jnp.float32)
            slr[3 * d] = jnp.zeros((1, Y), jnp.int32)
        for e in range(2):
            buf = (dh, dl)[e]

            @pl.when(jnp.logical_not(has[d] & up[e]))
            def _():
                for s in range(STEPS):
                    buf[s, d] = jnp.zeros((NT, ROWS, Y), jnp.float32)
    for e in range(2):
        buf = (zh, zl)[e]

        @pl.when(jnp.logical_not(up[e]))
        def _():
            for s in range(STEPS):
                buf[s] = jnp.zeros((2, NT, ROWS, Y), jnp.float32)

    lanes1 = lax.broadcasted_iota(jnp.int32, (1, Y), 1)
    rows = lax.broadcasted_iota(jnp.int32, (NP, Y), 0)
    lanes = lax.broadcasted_iota(jnp.int32, (NP, Y), 1)

    def tons_of(cls):
        tons = jnp.zeros(cls.shape, jnp.float32)
        for c in range(dens_ref.shape[0]):
            tons = jnp.where(cls == c, (1.0 + c) * dens_ref[c], tons)
        return tons

    def as_lanes(value):
        sums = jnp.sum(value, axis=1, keepdims=True)
        return jnp.sum(jnp.where(lanes == rows, sums, 0.0), axis=0, keepdims=True)

    def as_rows(line, at=0):
        return jnp.broadcast_to(jnp.sum(jnp.where(lanes == rows + at, line, 0.0), axis=1, keepdims=True), (NP, Y))

    slr[1 + h] = slope_ref[...]
    loads[0].wait()
    for b in range(NQ):
        if b + 1 < NQ:
            for k in range(5):
                for t in range(T):
                    hh[b, k, pl.ds(t, 1)] = praw[k, t, pl.ds(ROWS * (b + 1), 1)]
        else:
            hh[b] = jnp.zeros((5, T, Y), jnp.float32)
    hpr[unit] = hh[q]
    bvb[h] = bv_ref[0, rows_of(q)]
    tcb[h] = tc_ref[0, rows_of(q)]
    deep = Z // NPD
    strip_part = tons_of(tc_ref[0, pl.ds(pl.multiple_of(pe * deep, ROWS), deep)])
    strip_part = jnp.sum(jnp.sum(strip_part, axis=0, keepdims=True), axis=1, keepdims=True)
    line = jnp.where(lanes1 == 2 * NP, strip_part, 0.0)
    lead = jnp.where(me == 0, 1.0, 0.0)
    for t in range(T):
        line = jnp.where(lanes1 == pe * T + t, cap_ref[t] * lead, line)
        line = jnp.where(lanes1 == NP + pe * T + t, capacity_ref[t] * lead, line)

    pl.semaphore_wait(barrier, ND - 1)
    for what in range(2):
        for i in range(NQ - 1):
            in_copy(i, what).start()
    start(None, slope_copy(0))
    for what in (1, 2):
        start(has_away, slope_copy(what))
    start(None, partner_copy(0))
    start(None, partner_copy(1))
    reduce_start(0, line)
    for what in range(2, 6):
        for i in range(NQ - 1):
            in_copy(i, what).start()

    z_ids = lax.broadcasted_iota(jnp.int32, (ROWS, Y), 0)
    y_ids = lax.broadcasted_iota(jnp.int32, (ROWS, Y), 1)
    low = z_ids == ROWS - 1

    def mask_of(code, k, depth, inside):
        ok = (depth >= 1) & (depth < Z)
        if k > 0:
            ok = ok & (jnp.broadcast_to((code >> (k - 1)) & 1, (ROWS, Y)) == 1)
        if k == 3:
            ok = ok & (y_ids < Y - 1)
        if k == 4:
            ok = ok & (y_ids >= 1)
        if inside is not None:
            ok = ok & (jnp.full((ROWS, Y), inside.astype(jnp.int32)) == 1)
        return ok.astype(jnp.float32)

    wait_recv(None, slope_copy(0))
    here, below = z_ids + ROWS * q, jnp.full((ROWS, Y), ROWS * (q + 1))
    for hh_ in range(2):
        code = slr[1 + hh_]
        for k in range(5):
            inside = None
            if k == 1 and hh_ == 1:
                inside = has[1]
            if k == 2 and hh_ == 0:
                inside = has[0]
            act[k, hh_] = mask_of(code, k, here, inside)
            hact[k, hh_] = mask_of(code, k, below, inside)
    for d in range(2):
        wait_recv(has[d], slope_wait(d))
        nact[d] = mask_of(slr[3 * d], 1 + d, here + 1, has[d])

    wait_recv(None, partner_copy(0))
    wait_recv(None, partner_copy(1))
    for hh_ in range(2):
        tons = tons_of(tcb[hh_])
        ton[hh_] = tons
        for t in range(NP):
            tb[hh_, t] = 1.0 / (SLOPE * (NP - t) + tons * inv_root)
            pr[hh_, t] = bvb[hh_] * math.exp(-RATE * t)

    t_plane = lax.broadcasted_iota(jnp.int32, (NP, ROWS, Y), 0).astype(jnp.float32)
    t_rows = (
        lax.broadcasted_iota(jnp.int32, (NT, ROWS, Y), 0) * ROWS + lax.broadcasted_iota(jnp.int32, (NT, ROWS, Y), 1)
    ).astype(jnp.float32)

    w = jnp.full((1, Y), om_ref[0])

    def set_rates(w):
        rp[...] = w[None] / (2.0 * (t_plane + 1.0))
        rh[...] = w[None] / (2.0 * (t_rows + 1.0))

    set_rates(w)

    loads[1].wait()
    in_all(0).wait_recv()
    for d in range(2):
        start(has[d], relay_copy(d, 0))
    in_all(1).wait_recv()
    for d in range(2):
        start(has[d], relay_copy(d, 1))

    chunks = [(lo, min(CHUNK, NP - lo)) for lo in range(0, NP, CHUNK)]

    def roll(v, by, axis):
        return pltpu.roll(v, by % v.shape[axis], axis)

    def up_y(v):
        return roll(v, 1, v.ndim - 1)

    def dn_y(v):
        return roll(v, -1, v.ndim - 1)

    def lines(ref, lo, size, *at):
        picked = [ref[(*at, t // ROWS, pl.ds(t % ROWS, 1))] for t in range(lo, lo + size)]
        return jnp.stack([jnp.broadcast_to(p, (ROWS, Y)) for p in picked])

    def from_above(v, line):
        return jnp.where(lax.broadcasted_iota(jnp.int32, v.shape, 1) == 0, line, roll(v, 1, 1))

    def from_below(v, line):
        return jnp.where(lax.broadcasted_iota(jnp.int32, v.shape, 1) == ROWS - 1, line, roll(v, -1, 1))

    def landed(ref, hh_, *at):
        return ref[(*at, pl.ds(hh_ * NPD, NPD))].reshape(NP, ROWS, Y)

    def mask_arcs(ks):
        for k in ks:
            for hh_ in range(2):
                fa[k, hh_] = landed(pp, hh_, k) * act[k, hh_][None]

    mask_arcs((1, 2))
    in_all(2).wait_recv()
    mask_arcs((0,))
    in_all(3).wait_recv()
    mask_arcs((3, 4))
    for k in range(5):
        for hh_ in range(2):
            for p in range(NPD):
                for t in range(T):
                    at = p * T + t
                    fh[k, hh_, at // ROWS, pl.ds(at % ROWS, 1)] = hpr[hh_ * NPD + p, k, pl.ds(t, 1)] * hact[k, hh_, 0:1]
    for d in range(2):
        wait_recv(has[d], relay_copy(1 - d, 0))
        wait_recv(has[d], relay_copy(1 - d, 1))
        for t in range(NP):
            edge = jnp.broadcast_to(hnr[d, t // T, pl.ds(t % T, 1)], (ROWS, Y))
            fn[d, t] = jnp.where(low, edge, roll(nraw[d, t // T, t % T], -1, 0)) * nact[d]
    loads[2].wait()
    in_all(4).wait_recv()

    def settle(first, cur, acc, at, j, new, old):
        if j == 0:
            cur[at] = new
            return None
        if j == 1:
            cur[at] = new
            acc[at] = old + new
            return None
        mean = (acc[at] + new) * (1.0 / INNER)
        diff = mean - first[at]
        first[at] = mean
        return jnp.sum(diff * diff, axis=0)

    def gradient(arcs, near, halo, bounds):
        for hh_ in range(2):
            k_in = 2 if hh_ == 0 else 1
            edge = (halo[0, hh_] + halo[k_in, 1 - hh_]) + (up_y(halo[3, hh_]) + dn_y(halo[4, hh_]))
            hs_tmp = edge
            tail = None
            for lo, size in reversed(chunks):
                at = pl.ds(lo, size)
                p0, p3, p4 = arcs[0, hh_, at], arcs[3, hh_, at], arcs[4, hh_, at]
                back = (p0 + arcs[k_in, 1 - hh_, at]) + (up_y(p3) + dn_y(p4))
                rows_below = jnp.stack([
                    jnp.broadcast_to(hs_tmp[t // ROWS, t % ROWS : t % ROWS + 1], (ROWS, Y)) for t in range(lo, lo + size)
                ])
                g = ((p0 + p3) + (p4 + bounds[hh_, at])) + (arcs[1, hh_, at] + arcs[2, hh_, at])
                g = g - (from_below(back, rows_below) + near[hh_, at])
                for t in range(lo + size - 1, lo - 1, -1):
                    tail = g[t - lo] if tail is None else tail + g[t - lo]
                    tl[hh_, t] = tail

    for hh_ in range(2):
        bf[hh_] = landed(pb, hh_)
    gradient(fa, fn, fh, bf)
    loads[3].wait()
    in_all(5).wait_recv()
    for hh_ in range(2):
        uf[hh_] = landed(pu, hh_)
    got = reduce_done(0)
    caps = as_rows(got)
    climit = as_rows(got, NP) * blocks_all
    inv_tons = 1.0 / jnp.sum(jnp.where(lanes1 == 2 * NP, got, 0.0), axis=1, keepdims=True)
    cap_first = cap_sum = None

    for s in range(STEPS):
        j = s % INNER
        last, final = j == INNER - 1, s == STEPS - 1
        u_src = uf if j == 0 else uc
        b_src = bf if j == 0 else bc
        p_src, n_src, h_src = (fa, fn, fh) if j == 0 else (ca, cn, ch)
        inv_w = 1.0 / w
        move_p = jnp.zeros((ROWS, Y), jnp.float32)
        move_d = jnp.zeros((ROWS, Y), jnp.float32)
        if j == 0:
            for hh_ in range(2):
                for t in range(NP):
                    tau = tb[hh_, t] * inv_w
                    tt[hh_, t] = tau * (ton[hh_] * inv_root)
                    tl[hh_, t] = u_src[hh_, t] - tau * (tl[hh_, t] - pr[hh_, t])
        row = jnp.zeros((NP, Y), jnp.float32)
        heads = [None, None]
        for t in range(NP):
            mined = None
            for hh_ in range(2):
                old = u_src[hh_, t]
                new = jnp.maximum(tl[hh_, t] - tt[hh_, t] * caps[t : t + 1, :], 0.0)
                ext = 2.0 * new - old
                if j == 0:
                    uc[hh_, t] = new
                elif j == 1:
                    uc[hh_, t] = new
                    us[hh_, t] = old + new
                else:
                    mean = (us[hh_, t] + new) * (1.0 / INNER)
                    diff = mean - uf[hh_, t]
                    uf[hh_, t] = mean
                    move_p = move_p + diff * diff
                heads[hh_] = ext if t == 0 else heads[hh_] + ext
                xs[s, hh_, t] = heads[hh_]
                hs[s, hh_, t // ROWS, pl.ds(t % ROWS, 1)] = heads[hh_][ROWS - 1 : ROWS]
                if not final:
                    ls[s, hh_, t // ROWS, pl.ds(t % ROWS, 1)] = heads[hh_][0:1]
                part = ton[hh_] * ext
                mined = part if mined is None else mined + part
            row = jnp.where(rows == t, jnp.sum(mined, axis=0, keepdims=True), row)
        reduce_start(1 + s, as_lanes(row))
        pl.when(up[1])(z_copy(1, s).start)
        for d in range(2):
            pl.when(has[d])(x_copy(d, s).start)
        for d in range(2):
            pl.when(has[d] & up[1])(d_copy(d, 1, s).start)
        if not final:
            pl.when(up[0])(z_copy(0, s).start)
            for d in range(2):
                pl.when(has[d] & up[0])(d_copy(d, 0, s).start)
        if final:
            out_start(0)

        def arc(k, hh_, at, diff, move):
            old = p_src[k, hh_, at]
            new = jnp.maximum(old + rp[at] * diff, 0.0) * act[k, hh_][None]
            moved = settle(fa, ca, sa, (k, hh_, at), j, new, old)
            return move if moved is None else move + moved

        for hh_ in range(2):
            for lo, size in chunks:
                at = pl.ds(lo, size)
                old = b_src[hh_, at]
                new = jnp.maximum(old + 2.0 * rp[at] * (xs[s, hh_, at] - 1.0), 0.0)
                if j == 0:
                    bc[hh_, at] = new
                elif j == 1:
                    bc[hh_, at] = new
                    bs[hh_, at] = old + new
                else:
                    mean = (bs[hh_, at] + new) * (1.0 / INNER)
                    diff = mean - bf[hh_, at]
                    bf[hh_, at] = mean
                    move_d = move_d + jnp.sum(diff * diff, axis=0)
        if final:
            out_start(1)
        wait_recv(up[0], z_copy(1, s))
        for lo, size in chunks:
            at = pl.ds(lo, size)
            c = [xs[s, hh_, at] for hh_ in range(2)]
            cz = [from_above(c[hh_], lines(zh, lo, size, s, hh_)) for hh_ in range(2)]
            for hh_ in range(2):
                move_d = arc(0, hh_, at, c[hh_] - cz[hh_], move_d)
                move_d = arc(3, hh_, at, c[hh_] - dn_y(cz[hh_]), move_d)
                move_d = arc(4, hh_, at, c[hh_] - up_y(cz[hh_]), move_d)
            move_d = arc(1, 0, at, c[0] - cz[1], move_d)
            move_d = arc(2, 1, at, c[1] - cz[0], move_d)
        if final:
            out_start(2)
            out_start(3)
        for d in range(2):
            wait_recv(has[d], x_copy(1 - d, s))
            wait_recv(has[d] & up[0], d_copy(1 - d, 1, s))
        for lo, size in chunks:
            at = pl.ds(lo, size)
            for d in range(2):
                cz = from_above(xr[s, d, at], lines(dh, lo, size, s, d))
                move_d = arc(2 - d, d, at, xs[s, d, at] - cz, move_d)
        if last:
            cyc = s // INNER
            mp = jnp.sum(move_p, axis=0, keepdims=True)
            md = jnp.sum(move_d, axis=0, keepdims=True)
            reduce_start(1 + STEPS + cyc, as_lanes(jnp.where(rows == 0, mp, jnp.where(rows == 1, md, 0.0))))
        if final:
            out_start(4)
        else:
            wait_recv(up[1], z_copy(0, s))
            for d in range(2):
                wait_recv(has[d] & up[1], d_copy(1 - d, 0, s))
            for lo, size in chunks:
                at = pl.ds(lo, size)
                for d in range(2):
                    old = n_src[d, at]
                    diff = from_below(xr[s, d, at], lines(dl, lo, size, s, d)) - xs[s, d, at]
                    new = jnp.maximum(old + rp[at] * diff, 0.0) * nact[d][None]
                    settle(fn, cn, sn, (d, at), j, new, old)
            for hh_ in range(2):
                c, cz = zl[s, hh_], hs[s, hh_]
                for k in (0, 3, 4, 1 + hh_):
                    ahead = (cz, hs[s, 1 - hh_], hs[s, 1 - hh_], dn_y(cz), up_y(cz))[k]
                    old = h_src[k, hh_]
                    new = jnp.maximum(old + rh[...] * (c - ahead), 0.0) * hact[k, hh_][None]
                    settle(fh, ch, sh, (k, hh_), j, new, old)
            if last:
                gradient(fa, fn, fh, bf)
            else:
                gradient(ca, cn, ch, bc)
                for hh_ in range(2):
                    for t in range(NP):
                        tau = tb[hh_, t] * inv_w
                        tl[hh_, t] = uc[hh_, t] - tau * (tl[hh_, t] - pr[hh_, t])
        row_total = as_rows(reduce_done(1 + s))
        new_caps = jnp.maximum(caps + w * ((row_total - climit) * inv_tons), 0.0)
        if j == 0:
            cap_first = caps
            cap_sum = new_caps
        else:
            cap_sum = cap_sum + new_caps
        caps = new_caps
        if last:
            caps = cap_sum * (1.0 / INNER)
            cap_move = jnp.sum((caps - cap_first) ** 2, axis=0, keepdims=True)
            if final:
                for t in range(T):
                    own = jnp.sum(jnp.where(rows == pe * T + t, caps, 0.0), axis=0, keepdims=True)
                    cap_out[t] = own[0, 0]
            tot = as_rows(reduce_done(1 + STEPS + cyc))
            moved = jnp.sqrt((tot[1:2, :] + cap_move + EPS) / (tot[0:1, :] + EPS))
            w = jnp.sqrt(w * moved)
            if not final:
                set_rates(w)
    w_out[0] = w[0, 0]
    u_out[0, :, rows_of(q)] = uf[h, mine]
    bound_out[0, :, rows_of(q)] = bf[h, mine]
    for k in range(5):
        prec_out[k, 0, :, rows_of(q)] = fa[k, h, mine]
    for what in range(5):
        out_all(what).wait_recv()
    for what in range(5):
        out_all(what).wait_send()
    for what in range(6):
        in_all(what).wait_send()
    rest = rb.at[:, pl.ds(0, ND - 1)]
    remote(rest, rest, r_s.at[0], r_r.at[0], other(0, 1)).wait_send()

    def wait_sent(cond, ref, sem):
        pl.when(cond)(lambda: remote(ref, ref, sem, sem, other(0, 1)).wait_send())

    rows_down, rows_up = ls.at[pl.ds(0, STEPS - 1)], hs
    wait_sent(up[0], rows_down, z_s.at[0])
    wait_sent(up[1], rows_up, z_s.at[1])
    for d in range(2):
        wait_sent(has[d], xs.at[:, d], x_s.at[d])
        wait_sent(has[d] & up[0], ls.at[pl.ds(0, STEPS - 1), d], d_s.at[d, 0])
        wait_sent(has[d] & up[1], hs.at[:, d], d_s.at[d, 1])
    for cond, copy in sends:
        if cond is None:
            copy.wait_send()
        else:
            pl.when(cond)(lambda copy=copy: copy.wait_send())


def pair_call(NS, NPD, u, prec, bound, cap, capacity, bv, tc, dens, slope, om):
    _, T, Z, Y = u.shape
    f32 = jnp.float32
    NP, NQ, ND = NPD * T, 2 * NPD, NS * NPD
    NT = NP // ROWS
    vmem = pl.BlockSpec(memory_space=pltpu.VMEM)
    hbm = pl.BlockSpec(memory_space=pl.ANY)
    smem = pl.BlockSpec(memory_space=pltpu.SMEM)
    slots = 1 + STEPS + OUTER
    V = lambda *shape: pltpu.VMEM((*shape, Y), f32)
    unit = lambda *n: V(*n, NQ, T, ROWS)
    whole = lambda *n: V(*n, NP, ROWS)
    edge = lambda *n: V(*n, NT, ROWS)
    dma = pltpu.SemaphoreType.DMA
    return pl.pallas_call(
        functools.partial(pair_kernel, NS, NPD, T, Z, Y),
        out_shape=(
            pltpu.VMEM(u.shape, f32),
            pltpu.VMEM(prec.shape, f32),
            pltpu.VMEM(bound.shape, f32),
            jax.ShapeDtypeStruct(cap.shape, f32),
            jax.ShapeDtypeStruct((1,), f32),
        ),
        in_specs=[hbm, hbm, hbm, smem, smem, vmem, vmem, smem, vmem, smem],
        out_specs=(vmem, vmem, vmem, smem, smem),
        scratch_shapes=[
            V(5, T, Z), V(NQ, 5, T), unit(), unit(), unit(5), V(NQ, 5, T), V(2, NPD, T, ROWS), V(2, NPD, T),
            V(2, ROWS), pltpu.VMEM((2, ROWS, Y), jnp.int32), pltpu.VMEM((4, 1, Y), jnp.int32),
            whole(5, 2), whole(5, 2), whole(5, 2), whole(2), whole(2), whole(2),
            edge(5, 2), edge(5, 2), edge(5, 2), whole(2), whole(2), whole(2), whole(2), whole(2), whole(2),
            V(5, 2, ROWS), V(2, ROWS), V(5, 2, ROWS), V(2, ROWS), whole(2), whole(2), whole(2), whole(2),
            whole(), edge(),
            whole(STEPS, 2), whole(STEPS, 2), edge(STEPS, 2), edge(STEPS, 2), edge(STEPS, 2), edge(STEPS, 2),
            edge(STEPS, 2), edge(STEPS, 2), V(slots, 1), V(slots, ND, 1),
            dma((4,)), dma((6,)), dma((6,)), dma((3,)), dma((3,)), dma((2,)), dma((2,)), dma((2, 2)), dma((2, 2)),
            dma((2,)), dma((2, 2)), dma((2,)), dma((2, 2)), dma((2, 2)), dma((2, 2, 2)), dma((1,)), dma((3,)),
            dma((5,)), dma((5,)),
        ],
        compiler_params=pltpu.CompilerParams(collective_id=1, has_side_effects=True),
    )(u, prec, bound, cap, capacity, bv, tc, dens, slope, om)


def solution(mesh):
    NS, NPD = mesh.shape["strip"], mesh.shape["period"]

    def per_device(u, prec, bound, cap, capacity, bv, tc, dens, slope, om):
        rows_here, T, Z, Y = u.shape
        assert rows_here == 1
        NP = NPD * T
        if NS % 2 == 0 and Z == 2 * NPD * ROWS and NP % ROWS == 0 and 2 * NP < Y:
            return pair_call(NS, NPD, u, prec, bound, cap, capacity, bv, tc, dens, slope, om)
        R = -(-T // 8) * 8
        f32 = jnp.float32
        vmem = pl.BlockSpec(memory_space=pltpu.VMEM)
        hbm = pl.BlockSpec(memory_space=pl.ANY)
        smem = pl.BlockSpec(memory_space=pltpu.SMEM)
        plane = lambda *n: pltpu.VMEM((*n, Z, Y), f32)
        dma = pltpu.SemaphoreType.DMA
        slots = 1 + STEPS + OUTER
        far = max(NPD - 1, 1)
        return pl.pallas_call(
            functools.partial(kernel, NS, NPD, T, Z, Y, R),
            out_shape=(
                pltpu.VMEM(u.shape, f32),
                pltpu.VMEM(prec.shape, f32),
                pltpu.VMEM(bound.shape, f32),
                jax.ShapeDtypeStruct(cap.shape, f32),
                jax.ShapeDtypeStruct((1,), f32),
            ),
            in_specs=[hbm, hbm, hbm, smem, smem, vmem, vmem, smem, vmem, smem],
            out_specs=(vmem, vmem, vmem, smem, smem),
            scratch_shapes=[
                plane(T), plane(T), plane(T), plane(T), plane(T), plane(T),
                plane(7, T), plane(7, T), plane(7, T), plane(7), plane(), plane(T), plane(T), plane(T), plane(),
                plane(STEPS, T), plane(2, STEPS, T), plane(STEPS), plane(STEPS, far),
                plane(STEPS), plane(STEPS, far),
                pltpu.VMEM((slots, 1, Y), f32), pltpu.VMEM((slots, NS, 1, Y), f32),
                pltpu.VMEM((OUTER, 1, Y), f32), pltpu.VMEM((OUTER, NPD, 1, Y), f32),
                pltpu.VMEM((2, 1, Y), jnp.int32),
                plane(5, T), plane(2), plane(2), dma((3,)),
                dma((2, 3)), dma((2, 3)), dma((2, 2, STEPS)), dma((2, 2, STEPS)),
                dma((STEPS, far)), dma((STEPS, far)), dma((STEPS, far)), dma((STEPS, far)),
                dma((slots, NS - 1)), dma((slots, NS - 1)), dma((OUTER, far)), dma((OUTER, far)),
            ],
            compiler_params=pltpu.CompilerParams(collective_id=0, has_side_effects=True),
        )(u, prec, bound, cap, capacity, bv, tc, dens, slope, om)

    in_specs = (
        P("strip", "period", None, None),
        P(None, "strip", "period", None, None),
        P("strip", "period", None, None),
        P("period"),
        P("period"),
        P("strip", None, None),
        P("strip", None, None),
        P(),
        P("strip", None),
        P(),
    )
    out_specs = (
        P("strip", "period", None, None),
        P(None, "strip", "period", None, None),
        P("strip", "period", None, None),
        P("period"),
        P(),
    )
    return jax.shard_map(
        per_device, mesh=mesh, in_specs=in_specs, out_specs=out_specs, check_vma=False
    )
```

```python
import functools
import math

import jax
import jax.numpy as jnp
from jax import lax
from jax.experimental import pallas as pl
from jax.experimental.pallas import tpu as pltpu
from jax.sharding import PartitionSpec as P

OUTER = 2
INNER = 3
STEPS = OUTER * INNER
RATE = math.log(1.1) / 12.0
EPS = 1e-06
SLOPE = 11.0
MESH = pl.DeviceIdType.MESH
ROWS = 8
CHUNK = 8


def kernel(
    NS, NPD, T, Z, Y, R,
    u_ref, prec_ref, bound_ref, cap_ref, capacity_ref, bv_ref, tc_ref, dens_ref, slope_ref, om_ref,
    u_out, prec_out, bound_out, cap_out, w_out,
    uf, uc, us, bf, bc, bs, fa, ca, sa, act, ton, tb, tl, cb, ex0,
    xs, xr, es, er, as_, ar, rs, rb, ps, pb, slr,
    praw, ti, to_sum, loc, ini_s, ini_r, xs_s, xs_r, e_s, e_r, a_s, a_r, r_s, r_r, p_s, p_r,
):
    me = lax.axis_index("strip")
    pe = lax.axis_index("period")
    total_rows = NS
    total_periods = NPD * T
    blocks_all = float(total_rows * Z * Y)
    root_blocks = math.sqrt(blocks_all)
    sends = []

    loads = (
        pltpu.make_async_copy(prec_ref.at[:, 0], praw, loc.at[0]),
        pltpu.make_async_copy(bound_ref.at[0], bf, loc.at[1]),
        pltpu.make_async_copy(u_ref.at[0], uf, loc.at[2]),
    )
    for load in loads:
        load.start()
    barrier = pltpu.get_barrier_semaphore()
    for k in range(1, NS):
        pl.semaphore_signal(barrier, inc=1, device_id={"strip": lax.rem(me + k, NS)}, device_id_type=MESH)
    for k in range(1, NPD):
        pl.semaphore_signal(barrier, inc=1, device_id={"period": lax.rem(pe + k, NPD)}, device_id_type=MESH)

    has = (me < NS - 1, me > 0)
    gets = (me > 0, me < NS - 1)
    to = (me + 1, me - 1)

    def remote(src, dst, ss, rr, dev):
        return pltpu.make_async_remote_copy(
            src_ref=src, dst_ref=dst, send_sem=ss, recv_sem=rr, device_id=dev, device_id_type=MESH
        )

    def ini_copy(d, what):
        if what == 2:
            return remote(to_sum.at[d], ti.at[d], ini_s.at[d, 2], ini_r.at[d, 2], {"strip": to[d]})
        if what == 0:
            rest = pl.ds(1, T - 1)
            return remote(praw.at[1 + d, rest], fa.at[5 + d, rest], ini_s.at[d, 0], ini_r.at[d, 0], {"strip": to[d]})
        return remote(slope_ref, slr.at[d], ini_s.at[d, 1], ini_r.at[d, 1], {"strip": to[d]})

    def x_copy(d, part, s):
        lo, size = (1, T - 1) if part == 0 else (0, 1)
        return remote(
            xs.at[s, pl.ds(lo, size)], xr.at[d, s, pl.ds(lo, size)],
            xs_s.at[d, part, s], xs_r.at[d, part, s], {"strip": to[d]},
        )

    def e_copy(k, s):
        return remote(es.at[s], er.at[s, k - 1], e_s.at[s, k - 1], e_r.at[s, k - 1], {"period": pe + k})

    def a_copy(k, s):
        return remote(as_.at[s], ar.at[s, k - 1], a_s.at[s, k - 1], a_r.at[s, k - 1], {"period": pe - k})

    def r_copy(k, slot):
        return remote(
            rs.at[slot], rb.at[slot, me], r_s.at[slot, k - 1], r_r.at[slot, k - 1],
            {"strip": lax.rem(me + k, NS)},
        )

    def p_copy(k, slot):
        return remote(
            ps.at[slot], pb.at[slot, pe], p_s.at[slot, k - 1], p_r.at[slot, k - 1],
            {"period": lax.rem(pe + k, NPD)},
        )

    def start(cond, copy):
        def go():
            copy.start()
        if cond is None:
            go()
        else:
            pl.when(cond)(go)
        sends.append((cond, copy))

    def wait_recv(cond, copy):
        if cond is None:
            copy.wait_recv()
        else:
            pl.when(cond)(lambda: copy.wait_recv())

    def reduce_start(slot, value):
        rs[slot] = value
        rb[slot, me] = value
        for k in range(1, NS):
            start(None, r_copy(k, slot))

    def reduce_done(slot):
        for k in range(1, NS):
            wait_recv(None, r_copy(k, slot))
        total = rb[slot, 0]
        for k in range(1, NS):
            total = total + rb[slot, k]
        return total

    loads[0].wait()
    for d in range(2):
        total = praw[1 + d, 0]
        for t in range(1, T):
            total = total + praw[1 + d, t]
        to_sum[d] = total
    pl.semaphore_wait(barrier, NS + NPD - 2)
    for d in range(2):
        start(has[d], ini_copy(d, 1))
        start(has[d], ini_copy(d, 2))
    for d in range(2):
        start(has[d], ini_copy(d, 0))

    rows = lax.broadcasted_iota(jnp.int32, (R, Y), 0)
    lanes = lax.broadcasted_iota(jnp.int32, (R, Y), 1)

    def as_lanes(value):
        sums = jnp.sum(value, axis=1, keepdims=True)
        return jnp.sum(jnp.where(lanes == rows, sums, 0.0), axis=0, keepdims=True)

    def as_rows(line):
        return jnp.sum(jnp.where(lanes == rows, line, 0.0), axis=1, keepdims=True)

    def fold(v):
        return jnp.sum(v.reshape(Z // 8, 8, Y), axis=0)

    cls = tc_ref[0]
    tons = jnp.zeros((Z, Y), jnp.float32)
    for c in range(dens_ref.shape[0]):
        tons = jnp.where(cls == c, (1.0 + c) * dens_ref[c], tons)
    ton[...] = tons
    part = jnp.sum(tons, axis=0, keepdims=True)
    reduce_start(0, part)

    z_ids = lax.broadcasted_iota(jnp.int32, (Z, Y), 0)
    y_ids = lax.broadcasted_iota(jnp.int32, (Z, Y), 1)

    def mask_of(codes, k, inside):
        ok = z_ids >= 1
        if k > 0:
            ok = ok & (jnp.broadcast_to((codes >> (k - 1)) & 1, (Z, Y)) == 1)
        if k == 3:
            ok = ok & (y_ids < Y - 1)
        if k == 4:
            ok = ok & (y_ids >= 1)
        if inside is not None:
            ok = ok & (jnp.full((Z, Y), inside.astype(jnp.int32)) == 1)
        return ok.astype(jnp.float32)

    own = slope_ref[...]
    act[0] = mask_of(own, 0, None)
    act[1] = mask_of(own, 1, me < NS - 1)
    act[2] = mask_of(own, 2, me > 0)
    act[3] = mask_of(own, 3, None)
    act[4] = mask_of(own, 4, None)

    period = [(pe * T + t).astype(jnp.float32) for t in range(T)]
    pid = [jnp.full((1, Y), period[t]) for t in range(T)]
    disc = [jnp.exp(-RATE * pid[t]) for t in range(T)]
    tonr = ton[...] * (1.0 / root_blocks)
    for load in loads[1:]:
        load.wait()
    for t in range(T):
        tb[t] = 1.0 / (SLOPE * (total_periods - pid[t]) + tonr)
        for k in range(5):
            fa[k, t] = praw[k, t] * act[k]

    caps = jnp.zeros((R, Y), jnp.float32)
    climit = jnp.zeros((R, Y), jnp.float32)
    for t in range(T):
        caps = jnp.where(rows == t, cap_ref[t], caps)
        climit = jnp.where(rows == t, capacity_ref[t] * blocks_all, climit)
    w = jnp.full((1, Y), om_ref[0])

    for d in range(2):
        @pl.when(jnp.logical_not(gets[d]))
        def _():
            act[5 + d] = jnp.zeros((Z, Y), jnp.float32)
            ti[d] = jnp.zeros((Z, Y), jnp.float32)
            fa[5 + d] = jnp.zeros((T, Z, Y), jnp.float32)
            for s in range(STEPS):
                xr[d, s] = jnp.zeros((T, Z, Y), jnp.float32)

    def up_y(v):
        return pltpu.roll(v, 1, 1)

    def dn_y(v):
        return pltpu.roll(v, Y - 1, 1)

    def up_z(v):
        return pltpu.roll(v, 1, 0)

    def dn_z(v):
        return pltpu.roll(v, Z - 1, 0)

    def settle(first, cur, acc, at, j, new, old):
        if j == 0:
            cur[at] = new
            return new, None
        if j == 1:
            cur[at] = new
            acc[at] = old + new
            return new, None
        mean = (acc[at] + new) * (1.0 / INNER)
        diff = mean - first[at]
        first[at] = mean
        return mean, fold(diff * diff)

    def gradient_own(arcs, bounds):
        for t in range(T):
            p0, p3, p4 = arcs[0, t], arcs[3, t], arcs[4, t]
            back = p0 + (up_y(p3) + dn_y(p4))
            tl[t] = ((p0 + p3) + (p4 + bounds[t])) - dn_z(back)

    def gradient(s, arcs):
        tail = None
        for t in range(T - 1, -1, -1):
            g = (tl[t] + (arcs[1, t] + arcs[2, t])) - dn_z(arcs[5, t] + arcs[6, t])
            tail = g if tail is None else tail + g
            tl[t] = tail
        as_[s] = tail
        for k in range(1, NPD):
            start(pe >= k, a_copy(k, s))

    tail = None
    for t in range(T - 1, -1, -1):
        p = [fa[k, t] for k in range(5)]
        g = (((p[0] + p[1]) + (p[2] + p[3])) + p[4]) + bf[t]
        g = g - dn_z(p[0] + (up_y(p[3]) + dn_y(p[4])))
        tail = g if tail is None else tail + g
        tl[t] = tail
    for d in range(2):
        wait_recv(gets[d], ini_copy(d, 1))
        wait_recv(gets[d], ini_copy(d, 2))

        @pl.when(gets[d])
        def _():
            act[5 + d] = mask_of(slr[d], 1 + d, None)
    as_[0] = tl[0] - dn_z(ti[0] * act[5] + ti[1] * act[6])
    for k in range(1, NPD):
        start(pe >= k, a_copy(k, 0))
    for d in range(2):
        wait_recv(gets[d], ini_copy(d, 0))
        rest = ti[d]
        for t in range(1, T):
            plane = fa[5 + d, t]
            rest = rest - plane
            fa[5 + d, t] = plane * act[5 + d]
        fa[5 + d, 0] = rest * act[5 + d]
    tail = None
    for t in range(T - 1, -1, -1):
        back = fa[5, t] + fa[6, t]
        tail = back if tail is None else tail + back
        tl[t] = tl[t] - dn_z(tail)
    tons_all = jnp.sum(reduce_done(0), axis=1, keepdims=True)
    inv_tons = 1.0 / tons_all
    cap_first = cap_sum = None

    for s in range(STEPS):
        j = s % INNER
        u_src = uf if j == 0 else uc
        b_src = bf if j == 0 else bc
        p_src = fa if j == 0 else ca
        inv_w = 1.0 / w
        move_p = jnp.zeros((8, Y), jnp.float32)
        move_d = jnp.zeros((8, Y), jnp.float32)
        for k in range(1, NPD):
            @pl.when(pe + k < NPD)
            def _():
                a_copy(k, s).wait_recv()
                for t in range(T):
                    tl[t] = tl[t] + ar[s, k - 1]
        head = None
        row = jnp.zeros((R, Y), jnp.float32)
        for t in range(T):
            old = u_src[t]
            grad = tl[t] + (ton[...] * (1.0 / root_blocks)) * caps[t : t + 1, :]
            new = jnp.maximum(old - (tb[t] * inv_w) * (grad - bv_ref[0] * disc[t]), 0.0)
            ext = 2.0 * new - old
            _, moved = settle(uf, uc, us, t, j, new, old)
            if moved is not None:
                move_p = move_p + moved
            if t == 0:
                ex0[...] = ext
            else:
                xs[s, t] = ext
            head = ext if head is None else head + ext
            row = jnp.where(rows == t, jnp.sum(ton[...] * ext, axis=0, keepdims=True), row)
        es[s] = head
        for k in range(1, NPD):
            start(pe + k < NPD, e_copy(k, s))
        for d in range(2):
            start(has[d], x_copy(d, 0, s))
        for k in range(1, NPD):
            @pl.when(pe >= k)
            def _():
                e_copy(k, s).wait_recv()
                ex0[...] = ex0[...] + er[s, k - 1]
        xs[s, 0] = ex0[...]
        for d in range(2):
            start(has[d], x_copy(d, 1, s))
        reduce_start(1 + s, as_lanes(row))
        total = None
        for t in range(T):
            total = xs[s, t] if t == 0 else total + xs[s, t]
            cb[t] = total
        rate_b = [w / (pid[t] + 1.0) for t in range(T)]
        rate_p = [w / (2.0 * (pid[t] + 1.0)) for t in range(T)]

        def arc(k, t, diff, move):
            old = p_src[k, t]
            new = jnp.maximum(old + rate_p[t] * diff, 0.0) * act[k]
            _, moved = settle(fa, ca, sa, (k, t), j, new, old)
            if moved is not None and k < 5:
                move = move + moved
            return move

        for t in range(T):
            c = cb[t]
            old = b_src[t]
            new = jnp.maximum(old + rate_b[t] * (c - 1.0), 0.0)
            _, moved = settle(bf, bc, bs, t, j, new, old)
            if moved is not None:
                move_d = move_d + moved
            cz = up_z(c)
            move_d = arc(0, t, c - cz, move_d)
            move_d = arc(3, t, c - dn_y(cz), move_d)
            move_d = arc(4, t, c - up_y(cz), move_d)
        last = j == INNER - 1
        if s < STEPS - 1:
            gradient_own(fa if last else ca, bf if last else bc)
        for part in range(2):
            for d in range(2):
                wait_recv(gets[d], x_copy(d, part, s))
        total_m = total_p = None
        for t in range(T):
            total_m = xr[0, s, t] if t == 0 else total_m + xr[0, s, t]
            total_p = xr[1, s, t] if t == 0 else total_p + xr[1, s, t]
            c = cb[t]
            cz = up_z(c)
            move_d = arc(1, t, c - up_z(total_p), move_d)
            move_d = arc(2, t, c - up_z(total_m), move_d)
            if s < STEPS - 1:
                arc(5, t, total_m - cz, None)
                arc(6, t, total_p - cz, None)
        if s < STEPS - 1:
            gradient(s + 1, fa if last else ca)
        if last:
            cyc = s // INNER
            mp = jnp.sum(move_p, axis=0, keepdims=True)
            md = jnp.sum(move_d, axis=0, keepdims=True)
            reduce_start(1 + STEPS + cyc, as_lanes(jnp.where(rows == 0, mp, jnp.where(rows == 1, md, 0.0))))
        row_total = as_rows(reduce_done(1 + s))
        new_caps = jnp.maximum(caps + w * ((row_total - climit) * inv_tons), 0.0)
        new_caps = jnp.where(rows < T, new_caps, 0.0)
        if j == 0:
            cap_first = caps
            cap_sum = new_caps
        else:
            cap_sum = cap_sum + new_caps
        caps = new_caps
        if last:
            caps = cap_sum * (1.0 / INNER)
            cap_move = jnp.sum((caps - cap_first) ** 2, axis=0, keepdims=True)
            got = reduce_done(1 + STEPS + cyc)
            msg = got + jnp.where(lanes[0:1] == 1, cap_move, 0.0)
            ps[cyc] = msg
            pb[cyc, pe] = msg
            for k in range(1, NPD):
                start(None, p_copy(k, cyc))
            if s == STEPS - 1:
                for t in range(T):
                    u_out[0, t] = uf[t]
                    bound_out[0, t] = bf[t]
                    for k in range(5):
                        prec_out[k, 0, t] = fa[k, t]
                    cap_out[t] = caps[t, 0]
            for k in range(1, NPD):
                wait_recv(None, p_copy(k, cyc))
            tot = pb[cyc, 0]
            for k in range(1, NPD):
                tot = tot + pb[cyc, k]
            tot = as_rows(tot)
            moved = jnp.sqrt((tot[1:2, :] + EPS) / (tot[0:1, :] + EPS))
            w = jnp.sqrt(w * moved)
    w_out[0] = w[0, 0]
    for cond, copy in sends:
        if cond is None:
            copy.wait_send()
        else:
            pl.when(cond)(lambda copy=copy: copy.wait_send())


def pair_kernel(
    NS, NPD, T, Z, Y,
    u_ref, prec_ref, bound_ref, cap_ref, capacity_ref, bv_ref, tc_ref, dens_ref, slope_ref, om_ref,
    u_out, prec_out, bound_out, few_out,
    praw, hh, pu, pb, pp, hpr, nraw, hnr, bvb, tcb, slr,
    fa, ca, sa, fn, cn, sn, fh, ch, sh, bf, bc, bs, uf, uc, us,
    act, nact, hact, ton, tb, pr, tl, tt, rp, rh,
    xs, xr, hs, ls, zh, zl, dh, dl, rs, rb,
    token, loc, ini_s, ini_r, sl_s, sl_r, sm_s, sm_r, re_s, re_r,
    x_s, x_r, z_s, z_r, d_s, d_r, r_s, r_r, o_s, o_r,
):
    me = lax.axis_index("strip")
    pe = lax.axis_index("period")
    pairs, NP, NQ = NS // 2, NPD * T, 2 * NPD
    NT = NP // ROWS
    ND = NS * NPD
    a, h = me // 2, lax.rem(me, 2)
    q = jnp.where(h == 0, pe, NQ - 1 - pe)
    blocks_all = float(NS * Z * Y)
    inv_root = 1.0 / math.sqrt(blocks_all)
    sends = []

    def rows_of(block):
        return pl.ds(pl.multiple_of(ROWS * block, ROWS), ROWS)

    def block_of(hh_, pp_):
        return jnp.where(hh_ == 0, pp_, NQ - 1 - pp_)

    def device_at(pair, block):
        first = block < NPD
        return {
            "strip": 2 * pair + jnp.where(first, 0, 1),
            "period": jnp.where(first, block, NQ - 1 - block),
        }

    def remote(src, dst, ss, rr, dev):
        return pltpu.make_async_remote_copy(
            src_ref=src, dst_ref=dst, send_sem=ss, recv_sem=rr, device_id=dev, device_id_type=MESH
        )

    def start(cond, copy):
        if cond is None:
            copy.start()
        else:
            pl.when(cond)(lambda: copy.start())
        sends.append((cond, copy))

    def wait_recv(cond, copy):
        if cond is None:
            copy.wait_recv()
        else:
            pl.when(cond)(lambda: copy.wait_recv())

    mine = pl.ds(pe * T, T)
    unit = h * NPD + pe
    peers = pl.ds(0, NQ - 1)
    loads = (
        pltpu.make_async_copy(prec_ref.at[:, 0], praw, loc.at[0]),
        pltpu.make_async_copy(prec_ref.at[:, 0, :, rows_of(q)], pp.at[:, unit], loc.at[1]),
        pltpu.make_async_copy(bound_ref.at[0, :, rows_of(q)], pb.at[unit], loc.at[2]),
        pltpu.make_async_copy(u_ref.at[0, :, rows_of(q)], pu.at[unit], loc.at[3]),
    )
    for load in loads:
        load.start()
    barrier = pltpu.get_barrier_semaphore()
    others = [divmod(k, NPD) for k in range(1, ND)]
    others.sort(key=lambda o: -abs(o[0] - NS // 2) if o[0] else NS)

    def other(ks, kp):
        return {"strip": lax.rem(me + ks, NS), "period": lax.rem(pe + kp, NPD)}

    mates = [divmod(k, NPD) for k in range(1, NQ)]

    def mate(i):
        kh, kp = mates[i]
        return lax.rem(h + kh, 2), lax.rem(pe + kp, NPD)

    has = (a > 0, a < pairs - 1)
    up = (q > 0, q < NQ - 1)
    beside = [device_at(a - 1, q), device_at(a + 1, q)]
    for i in range(NQ - 1):
        th, tp = mate(i)
        pl.semaphore_signal(barrier, inc=1, device_id={"strip": 2 * a + th, "period": tp}, device_id_type=MESH)
    for d in range(2):
        pl.when(has[d])(
            lambda d=d: pl.semaphore_signal(barrier, inc=1, device_id=beside[d], device_id_type=MESH)
        )

    def in_ends(what, rows, block, at):
        if what == 1:
            return hh.at[block], hpr.at[at]
        if what == 4:
            return bound_ref.at[0, :, rows], pb.at[at]
        if what == 5:
            return u_ref.at[0, :, rows], pu.at[at]
        arcs = (pl.ds(1, 2), None, 0, pl.ds(3, 2))[what]
        return prec_ref.at[arcs, 0, :, rows], pp.at[arcs, at]

    def in_copy(i, what):
        th, tp = mate(i)
        block = block_of(th, tp)
        src, dst = in_ends(what, rows_of(block), block, unit)
        return remote(src, dst, ini_s.at[what], ini_r.at[what], {"strip": 2 * a + th, "period": tp})

    def in_all(what):
        dst = in_ends(what, rows_of(0), 0, peers)[1]
        return remote(dst, dst, ini_s.at[what], ini_r.at[what], other(0, 1))

    def partner_copy(what):
        rows = rows_of(block_of(1 - h, pe))
        dev = {"strip": 2 * a + 1 - h, "period": pe}
        if what == 0:
            return remote(tc_ref.at[0, rows], tcb.at[h], sm_s.at[0], sm_r.at[0], dev)
        return remote(bv_ref.at[0, rows], bvb.at[h], sm_s.at[1], sm_r.at[1], dev)

    def slope_copy(what):
        if what == 2:
            return remote(slope_ref, slr.at[1 + h], sl_s.at[2], sl_r.at[2], {"strip": 2 * a + 1 - h, "period": pe})
        return remote(slr.at[1 + what], slr.at[3 - 3 * what], sl_s.at[what], sl_r.at[1 - what], beside[what])

    def relay_copy(d, what):
        dev = beside[d]
        k, hs_ = (2, 0) if d == 0 else (1, 1)
        ss, rr = re_s.at[d, what], re_r.at[d, what]
        if what == 0:
            return remote(pp.at[k, pl.ds(hs_ * NPD, NPD)], nraw.at[1 - d], ss, rr, dev)
        return remote(hpr.at[pl.ds(hs_ * NPD, NPD), k], hnr.at[1 - d], ss, rr, dev)

    def reduce_sem(slot):
        return r_r.at[slot % 2 if slot <= STEPS else 2]

    def reduce_start(slot, value):
        rs[slot] = value
        rb[slot, me * NPD + pe] = value
        for ks, kp in others:
            remote(
                rs.at[slot], rb.at[slot, me * NPD + pe], r_s.at[0], reduce_sem(slot), other(ks, kp)
            ).start()

    def reduce_done(slot):
        rest = rb.at[slot, pl.ds(0, ND - 1)]
        remote(rest, rest, r_s.at[0], reduce_sem(slot), other(0, 1)).wait_recv()
        parts = [rb[slot, i] for i in range(ND)]
        while len(parts) > 1:
            parts = [parts[i] + parts[i + 1] if i + 1 < len(parts) else parts[i] for i in range(0, len(parts), 2)]
        return parts[0]

    def x_copy(d, s):
        dev = beside[d]
        return remote(xs.at[s, d], xr.at[s, 1 - d], x_s.at[d], x_r.at[s % 2, 1 - d], dev)

    def z_copy(d, s):
        if d == 0:
            return remote(ls.at[s], zl.at[s], z_s.at[0], z_r.at[s % 2, 0], device_at(a, q - 1))
        return remote(hs.at[s], zh.at[s], z_s.at[1], z_r.at[s % 2, 1], device_at(a, q + 1))

    def d_copy(d, e, s):
        dev = device_at(a - 1 if d == 0 else a + 1, q - 1 if e == 0 else q + 1)
        src, dst = (ls, dl) if e == 0 else (hs, dh)
        return remote(src.at[s, d], dst.at[s, 1 - d], d_s.at[d, e], d_r.at[s % 2, 1 - d, e], dev)

    def out_ends(what, th, part, rows):
        if what == 0:
            return uf.at[th, part], u_out.at[0, :, rows]
        if what == 1:
            return bf.at[th, part], bound_out.at[0, :, rows]
        arcs = (0, pl.ds(3, 2), pl.ds(1, 2))[what - 2]
        return fa.at[arcs, th, part], prec_out.at[arcs, 0, :, rows]

    def out_start(what):
        for i in range(NQ - 1):
            th, tp = mate(i)
            src, dst = out_ends(what, th, pl.ds(tp * T, T), rows_of(q))
            remote(src, dst, o_s.at[what], o_r.at[what], {"strip": 2 * a + th, "period": tp}).start()

    def out_all(what):
        dst = out_ends(what, 0, mine, pl.ds(0, ROWS * (NQ - 1)))[1]
        return remote(dst, dst, o_s.at[what], o_r.at[what], other(0, 1))

    for d in range(2):
        @pl.when(jnp.logical_not(has[d]))
        def _():
            for s in range(STEPS):
                xr[s, d] = jnp.zeros((NP, ROWS, Y), jnp.float32)
            nraw[d] = jnp.zeros((NPD, T, ROWS, Y), jnp.float32)
            hnr[d] = jnp.zeros((NPD, T, Y), jnp.float32)
            slr[3 * d] = jnp.zeros((1, Y), jnp.int32)
        for e in range(2):
            buf = (dh, dl)[e]

            @pl.when(jnp.logical_not(has[d] & up[e]))
            def _():
                for s in range(STEPS):
                    buf[s, d] = jnp.zeros((NT, ROWS, Y), jnp.float32)
    for e in range(2):
        buf = (zh, zl)[e]

        @pl.when(jnp.logical_not(up[e]))
        def _():
            for s in range(STEPS):
                buf[s] = jnp.zeros((2, NT, ROWS, Y), jnp.float32)

    lanes1 = lax.broadcasted_iota(jnp.int32, (1, Y), 1)
    rows = lax.broadcasted_iota(jnp.int32, (NP, Y), 0)
    lanes = lax.broadcasted_iota(jnp.int32, (NP, Y), 1)

    def tons_of(cls):
        tons = jnp.zeros(cls.shape, jnp.float32)
        for c in range(dens_ref.shape[0]):
            tons = jnp.where(cls == c, (1.0 + c) * dens_ref[c], tons)
        return tons

    def as_lanes(value):
        sums = jnp.sum(value, axis=1, keepdims=True)
        return jnp.sum(jnp.where(lanes == rows, sums, 0.0), axis=0, keepdims=True)

    def as_rows(line, at=0):
        return jnp.broadcast_to(jnp.sum(jnp.where(lanes == rows + at, line, 0.0), axis=1, keepdims=True), (NP, Y))

    slr[1 + h] = slope_ref[...]
    loads[0].wait()
    for b in range(NQ):
        if b + 1 < NQ:
            for k in range(5):
                for t in range(T):
                    hh[b, k, pl.ds(t, 1)] = praw[k, t, pl.ds(ROWS * (b + 1), 1)]
        else:
            hh[b] = jnp.zeros((5, T, Y), jnp.float32)
    hpr[unit] = hh[q]
    bvb[h] = bv_ref[0, rows_of(q)]
    tcb[h] = tc_ref[0, rows_of(q)]
    deep = Z // NPD
    strip_part = tons_of(tc_ref[0, pl.ds(pl.multiple_of(pe * deep, ROWS), deep)])
    strip_part = jnp.sum(jnp.sum(strip_part, axis=0, keepdims=True), axis=1, keepdims=True)
    line = jnp.where(lanes1 == 2 * NP, strip_part, 0.0)
    lead = jnp.where(me == 0, 1.0, 0.0)
    for t in range(T):
        line = jnp.where(lanes1 == pe * T + t, cap_ref[t] * lead, line)
        line = jnp.where(lanes1 == NP + pe * T + t, capacity_ref[t] * lead, line)

    pl.semaphore_wait(barrier, NQ - 1 + has[0].astype(jnp.int32) + has[1].astype(jnp.int32))
    start(None, slope_copy(2))
    for what in range(3):
        for i in range(NQ - 1):
            in_copy(i, what).start()
    start(None, partner_copy(0))
    start(None, partner_copy(1))
    for d in range(2):
        pl.when(has[1 - d])(lambda d=d: pl.semaphore_wait(token.at[d], 1))
        pl.when(has[d])(
            lambda d=d: pl.semaphore_signal(token.at[d], inc=1, device_id=beside[d], device_id_type=MESH)
        )
    reduce_start(0, line)
    for what in range(3, 6):
        for i in range(NQ - 1):
            in_copy(i, what).start()

    z_ids = lax.broadcasted_iota(jnp.int32, (ROWS, Y), 0)
    y_ids = lax.broadcasted_iota(jnp.int32, (ROWS, Y), 1)
    low = z_ids == ROWS - 1

    def mask_of(code, k, depth, inside):
        ok = (depth >= 1) & (depth < Z)
        if k > 0:
            ok = ok & (jnp.broadcast_to((code >> (k - 1)) & 1, (ROWS, Y)) == 1)
        if k == 3:
            ok = ok & (y_ids < Y - 1)
        if k == 4:
            ok = ok & (y_ids >= 1)
        if inside is not None:
            ok = ok & (jnp.full((ROWS, Y), inside.astype(jnp.int32)) == 1)
        return ok.astype(jnp.float32)

    wait_recv(None, slope_copy(2))
    for d in range(2):
        start(has[d], slope_copy(d))
    here, below = z_ids + ROWS * q, jnp.full((ROWS, Y), ROWS * (q + 1))
    for hh_ in range(2):
        code = slr[1 + hh_]
        for k in range(5):
            inside = None
            if k == 1 and hh_ == 1:
                inside = has[1]
            if k == 2 and hh_ == 0:
                inside = has[0]
            act[k, hh_] = mask_of(code, k, here, inside)
            hact[k, hh_] = mask_of(code, k, below, inside)
    for d in range(2):
        wait_recv(has[d], slope_copy(1 - d))
        nact[d] = mask_of(slr[3 * d], 1 + d, here + 1, has[d])

    wait_recv(None, partner_copy(0))
    wait_recv(None, partner_copy(1))
    for hh_ in range(2):
        tons = tons_of(tcb[hh_])
        ton[hh_] = tons
        for t in range(NP):
            tb[hh_, t] = 1.0 / (SLOPE * (NP - t) + tons * inv_root)
            pr[hh_, t] = bvb[hh_] * math.exp(-RATE * t)

    t_plane = lax.broadcasted_iota(jnp.int32, (NP, ROWS, Y), 0).astype(jnp.float32)
    t_rows = (
        lax.broadcasted_iota(jnp.int32, (NT, ROWS, Y), 0) * ROWS + lax.broadcasted_iota(jnp.int32, (NT, ROWS, Y), 1)
    ).astype(jnp.float32)

    w = jnp.full((1, Y), om_ref[0])

    def set_rates(w):
        rp[...] = w[None] / (2.0 * (t_plane + 1.0))
        rh[...] = w[None] / (2.0 * (t_rows + 1.0))

    set_rates(w)

    loads[1].wait()
    in_all(0).wait_recv()
    for d in range(2):
        start(has[d], relay_copy(d, 0))
    in_all(1).wait_recv()
    for d in range(2):
        start(has[d], relay_copy(d, 1))

    chunks = [(lo, min(CHUNK, NP - lo)) for lo in range(0, NP, CHUNK)]

    def roll(v, by, axis):
        return pltpu.roll(v, by % v.shape[axis], axis)

    def up_y(v):
        return roll(v, 1, v.ndim - 1)

    def dn_y(v):
        return roll(v, -1, v.ndim - 1)

    def lines(ref, lo, size, *at):
        picked = [ref[(*at, t // ROWS, pl.ds(t % ROWS, 1))] for t in range(lo, lo + size)]
        return jnp.stack([jnp.broadcast_to(p, (ROWS, Y)) for p in picked])

    def from_above(v, line):
        return jnp.where(lax.broadcasted_iota(jnp.int32, v.shape, 1) == 0, line, roll(v, 1, 1))

    def from_below(v, line):
        return jnp.where(lax.broadcasted_iota(jnp.int32, v.shape, 1) == ROWS - 1, line, roll(v, -1, 1))

    def landed(ref, hh_, *at):
        return ref[(*at, pl.ds(hh_ * NPD, NPD))].reshape(NP, ROWS, Y)

    def mask_arcs(ks):
        for k in ks:
            for hh_ in range(2):
                fa[k, hh_] = landed(pp, hh_, k) * act[k, hh_][None]

    mask_arcs((1, 2))
    in_all(2).wait_recv()
    mask_arcs((0,))
    in_all(3).wait_recv()
    mask_arcs((3, 4))
    for k in range(5):
        for hh_ in range(2):
            for p in range(NPD):
                for t in range(T):
                    at = p * T + t
                    fh[k, hh_, at // ROWS, pl.ds(at % ROWS, 1)] = hpr[hh_ * NPD + p, k, pl.ds(t, 1)] * hact[k, hh_, 0:1]
    for d in range(2):
        wait_recv(has[d], relay_copy(1 - d, 0))
        wait_recv(has[d], relay_copy(1 - d, 1))
        for t in range(NP):
            edge = jnp.broadcast_to(hnr[d, t // T, pl.ds(t % T, 1)], (ROWS, Y))
            fn[d, t] = jnp.where(low, edge, roll(nraw[d, t // T, t % T], -1, 0)) * nact[d]
    loads[2].wait()
    in_all(4).wait_recv()

    def settle(first, cur, acc, at, j, new, old):
        if j == 0:
            cur[at] = new
            return None
        if j == 1:
            cur[at] = new
            acc[at] = old + new
            return None
        mean = (acc[at] + new) * (1.0 / INNER)
        diff = mean - first[at]
        first[at] = mean
        return jnp.sum(diff * diff, axis=0)

    def gradient(arcs, near, halo, bounds):
        for hh_ in range(2):
            k_in = 2 if hh_ == 0 else 1
            edge = (halo[0, hh_] + halo[k_in, 1 - hh_]) + (up_y(halo[3, hh_]) + dn_y(halo[4, hh_]))
            hs_tmp = edge
            tail = None
            for lo, size in reversed(chunks):
                at = pl.ds(lo, size)
                p0, p3, p4 = arcs[0, hh_, at], arcs[3, hh_, at], arcs[4, hh_, at]
                back = (p0 + arcs[k_in, 1 - hh_, at]) + (up_y(p3) + dn_y(p4))
                rows_below = jnp.stack([
                    jnp.broadcast_to(hs_tmp[t // ROWS, t % ROWS : t % ROWS + 1], (ROWS, Y)) for t in range(lo, lo + size)
                ])
                g = ((p0 + p3) + (p4 + bounds[hh_, at])) + (arcs[1, hh_, at] + arcs[2, hh_, at])
                g = g - (from_below(back, rows_below) + near[hh_, at])
                for t in range(lo + size - 1, lo - 1, -1):
                    tail = g[t - lo] if tail is None else tail + g[t - lo]
                    tl[hh_, t] = tail

    for hh_ in range(2):
        bf[hh_] = landed(pb, hh_)
    gradient(fa, fn, fh, bf)
    loads[3].wait()
    in_all(5).wait_recv()
    for hh_ in range(2):
        uf[hh_] = landed(pu, hh_)
    got = reduce_done(0)
    caps = as_rows(got)
    climit = as_rows(got, NP) * blocks_all
    inv_tons = 1.0 / jnp.sum(jnp.where(lanes1 == 2 * NP, got, 0.0), axis=1, keepdims=True)
    cap_first = cap_sum = None

    for s in range(STEPS):
        j = s % INNER
        last, final = j == INNER - 1, s == STEPS - 1
        u_src = uf if j == 0 else uc
        b_src = bf if j == 0 else bc
        p_src, n_src, h_src = (fa, fn, fh) if j == 0 else (ca, cn, ch)
        inv_w = 1.0 / w
        move_p = jnp.zeros((ROWS, Y), jnp.float32)
        move_d = jnp.zeros((ROWS, Y), jnp.float32)
        if j == 0:
            for hh_ in range(2):
                for t in range(NP):
                    tau = tb[hh_, t] * inv_w
                    tt[hh_, t] = tau * (ton[hh_] * inv_root)
                    tl[hh_, t] = u_src[hh_, t] - tau * (tl[hh_, t] - pr[hh_, t])
        row = jnp.zeros((NP, Y), jnp.float32)
        heads = [None, None]
        for t in range(NP):
            mined = None
            for hh_ in range(2):
                old = u_src[hh_, t]
                new = jnp.maximum(tl[hh_, t] - tt[hh_, t] * caps[t : t + 1, :], 0.0)
                ext = 2.0 * new - old
                if j == 0:
                    uc[hh_, t] = new
                elif j == 1:
                    uc[hh_, t] = new
                    us[hh_, t] = old + new
                else:
                    mean = (us[hh_, t] + new) * (1.0 / INNER)
                    diff = mean - uf[hh_, t]
                    uf[hh_, t] = mean
                    move_p = move_p + diff * diff
                heads[hh_] = ext if t == 0 else heads[hh_] + ext
                xs[s, hh_, t] = heads[hh_]
                hs[s, hh_, t // ROWS, pl.ds(t % ROWS, 1)] = heads[hh_][ROWS - 1 : ROWS]
                if not final:
                    ls[s, hh_, t // ROWS, pl.ds(t % ROWS, 1)] = heads[hh_][0:1]
                part = ton[hh_] * ext
                mined = part if mined is None else mined + part
            row = jnp.where(rows == t, jnp.sum(mined, axis=0, keepdims=True), row)
        if not last:
            reduce_start(1 + s, as_lanes(row))
        if final:
            out_start(0)
        pl.when(up[1])(z_copy(1, s).start)
        for d in range(2):
            pl.when(has[d])(x_copy(d, s).start)
        for d in range(2):
            pl.when(has[d] & up[1])(d_copy(d, 1, s).start)
        if not final:
            pl.when(up[0])(z_copy(0, s).start)
            for d in range(2):
                pl.when(has[d] & up[0])(d_copy(d, 0, s).start)
        if last:
            reduce_start(1 + s, as_lanes(row))

        def arc(k, hh_, at, diff, move):
            old = p_src[k, hh_, at]
            new = jnp.maximum(old + rp[at] * diff, 0.0) * act[k, hh_][None]
            moved = settle(fa, ca, sa, (k, hh_, at), j, new, old)
            return move if moved is None else move + moved

        for hh_ in range(2):
            for lo, size in chunks:
                at = pl.ds(lo, size)
                old = b_src[hh_, at]
                new = jnp.maximum(old + 2.0 * rp[at] * (xs[s, hh_, at] - 1.0), 0.0)
                if j == 0:
                    bc[hh_, at] = new
                elif j == 1:
                    bc[hh_, at] = new
                    bs[hh_, at] = old + new
                else:
                    mean = (bs[hh_, at] + new) * (1.0 / INNER)
                    diff = mean - bf[hh_, at]
                    bf[hh_, at] = mean
                    move_d = move_d + jnp.sum(diff * diff, axis=0)
        if final:
            out_start(1)
        wait_recv(up[0], z_copy(1, s))
        for lo, size in chunks:
            at = pl.ds(lo, size)
            c = [xs[s, hh_, at] for hh_ in range(2)]
            cz = [from_above(c[hh_], lines(zh, lo, size, s, hh_)) for hh_ in range(2)]
            for hh_ in range(2):
                move_d = arc(0, hh_, at, c[hh_] - cz[hh_], move_d)
                move_d = arc(3, hh_, at, c[hh_] - dn_y(cz[hh_]), move_d)
                move_d = arc(4, hh_, at, c[hh_] - up_y(cz[hh_]), move_d)
            move_d = arc(1, 0, at, c[0] - cz[1], move_d)
            move_d = arc(2, 1, at, c[1] - cz[0], move_d)
        if final:
            out_start(2)
        for d in range(2):
            wait_recv(has[d], x_copy(1 - d, s))
            wait_recv(has[d] & up[0], d_copy(1 - d, 1, s))
        for lo, size in chunks:
            at = pl.ds(lo, size)
            for d in range(2):
                cz = from_above(xr[s, d, at], lines(dh, lo, size, s, d))
                move_d = arc(2 - d, d, at, xs[s, d, at] - cz, move_d)
        if last:
            cyc = s // INNER
            mp = jnp.sum(move_p, axis=0, keepdims=True)
            md = jnp.sum(move_d, axis=0, keepdims=True)
            reduce_start(1 + STEPS + cyc, as_lanes(jnp.where(rows == 0, mp, jnp.where(rows == 1, md, 0.0))))
        if final:
            out_start(3)
            out_start(4)
        else:
            wait_recv(up[1], z_copy(0, s))
            for d in range(2):
                wait_recv(has[d] & up[1], d_copy(1 - d, 0, s))
            for lo, size in chunks:
                at = pl.ds(lo, size)
                for d in range(2):
                    old = n_src[d, at]
                    diff = from_below(xr[s, d, at], lines(dl, lo, size, s, d)) - xs[s, d, at]
                    new = jnp.maximum(old + rp[at] * diff, 0.0) * nact[d][None]
                    settle(fn, cn, sn, (d, at), j, new, old)
            for hh_ in range(2):
                c, cz = zl[s, hh_], hs[s, hh_]
                for k in (0, 3, 4, 1 + hh_):
                    ahead = (cz, hs[s, 1 - hh_], hs[s, 1 - hh_], dn_y(cz), up_y(cz))[k]
                    old = h_src[k, hh_]
                    new = jnp.maximum(old + rh[...] * (c - ahead), 0.0) * hact[k, hh_][None]
                    settle(fh, ch, sh, (k, hh_), j, new, old)
            if last:
                gradient(fa, fn, fh, bf)
            else:
                gradient(ca, cn, ch, bc)
                for hh_ in range(2):
                    for t in range(NP):
                        tau = tb[hh_, t] * inv_w
                        tl[hh_, t] = uc[hh_, t] - tau * (tl[hh_, t] - pr[hh_, t])
        row_total = as_rows(reduce_done(1 + s))
        new_caps = jnp.maximum(caps + w * ((row_total - climit) * inv_tons), 0.0)
        if j == 0:
            cap_first = caps
            cap_sum = new_caps
        else:
            cap_sum = cap_sum + new_caps
        caps = new_caps
        if last:
            caps = cap_sum * (1.0 / INNER)
            cap_move = jnp.sum((caps - cap_first) ** 2, axis=0, keepdims=True)
            if final:
                for t in range(T):
                    few_out[t] = jnp.sum(jnp.where(rows == pe * T + t, caps, 0.0), axis=0)
            tot = as_rows(reduce_done(1 + STEPS + cyc))
            moved = jnp.sqrt((tot[1:2, :] + cap_move + EPS) / (tot[0:1, :] + EPS))
            w = jnp.sqrt(w * moved)
            if not final:
                set_rates(w)
    few_out[T] = w[0]
    u_out[0, :, rows_of(q)] = uf[h, mine]
    bound_out[0, :, rows_of(q)] = bf[h, mine]
    for k in range(5):
        prec_out[k, 0, :, rows_of(q)] = fa[k, h, mine]
    for what in range(5):
        out_all(what).wait_recv()
    for what in range(5):
        out_all(what).wait_send()
    for what in range(6):
        in_all(what).wait_send()
    rest = rb.at[:, pl.ds(0, ND - 1)]
    remote(rest, rest, r_s.at[0], r_r.at[0], other(0, 1)).wait_send()

    def wait_sent(cond, ref, sem):
        pl.when(cond)(lambda: remote(ref, ref, sem, sem, other(0, 1)).wait_send())

    rows_down, rows_up = ls.at[pl.ds(0, STEPS - 1)], hs
    wait_sent(up[0], rows_down, z_s.at[0])
    wait_sent(up[1], rows_up, z_s.at[1])
    for d in range(2):
        wait_sent(has[d], xs.at[:, d], x_s.at[d])
        wait_sent(has[d] & up[0], ls.at[pl.ds(0, STEPS - 1), d], d_s.at[d, 0])
        wait_sent(has[d] & up[1], hs.at[:, d], d_s.at[d, 1])
    for cond, copy in sends:
        if cond is None:
            copy.wait_send()
        else:
            pl.when(cond)(lambda copy=copy: copy.wait_send())


def store_kernel(u_ref, prec_ref, bound_ref, few_ref, u_out, prec_out, bound_out, cap_out, w_out, sem):
    stores = (
        pltpu.make_async_copy(prec_ref, prec_out, sem.at[0]),
        pltpu.make_async_copy(u_ref, u_out, sem.at[1]),
        pltpu.make_async_copy(bound_ref, bound_out, sem.at[2]),
    )
    for store in stores:
        store.start()
    T = cap_out.shape[0]
    for t in range(T):
        cap_out[t] = few_ref[t, 0]
    w_out[0] = few_ref[T, 0]
    for store in stores:
        store.wait()


def pair_call(NS, NPD, u, prec, bound, cap, capacity, bv, tc, dens, slope, om):
    _, T, Z, Y = u.shape
    f32 = jnp.float32
    NP, NQ, ND = NPD * T, 2 * NPD, NS * NPD
    NT = NP // ROWS
    vmem = pl.BlockSpec(memory_space=pltpu.VMEM)
    hbm = pl.BlockSpec(memory_space=pl.ANY)
    smem = pl.BlockSpec(memory_space=pltpu.SMEM)
    slots = 1 + STEPS + OUTER
    V = lambda *shape: pltpu.VMEM((*shape, Y), f32)
    unit = lambda *n: V(*n, NQ, T, ROWS)
    whole = lambda *n: V(*n, NP, ROWS)
    edge = lambda *n: V(*n, NT, ROWS)
    dma = pltpu.SemaphoreType.DMA
    ours = pl.pallas_call(
        functools.partial(pair_kernel, NS, NPD, T, Z, Y),
        out_shape=(
            pltpu.VMEM(u.shape, f32),
            pltpu.VMEM(prec.shape, f32),
            pltpu.VMEM(bound.shape, f32),
            pltpu.VMEM((T + 1, Y), f32),
        ),
        in_specs=[hbm, hbm, hbm, smem, smem, vmem, vmem, smem, vmem, smem],
        out_specs=(vmem, vmem, vmem, vmem),
        scratch_shapes=[
            V(5, T, Z), V(NQ, 5, T), unit(), unit(), unit(5), V(NQ, 5, T), V(2, NPD, T, ROWS), V(2, NPD, T),
            V(2, ROWS), pltpu.VMEM((2, ROWS, Y), jnp.int32), pltpu.VMEM((4, 1, Y), jnp.int32),
            whole(5, 2), whole(5, 2), whole(5, 2), whole(2), whole(2), whole(2),
            edge(5, 2), edge(5, 2), edge(5, 2), whole(2), whole(2), whole(2), whole(2), whole(2), whole(2),
            V(5, 2, ROWS), V(2, ROWS), V(5, 2, ROWS), V(2, ROWS), whole(2), whole(2), whole(2), whole(2),
            whole(), edge(),
            whole(STEPS, 2), whole(STEPS, 2), edge(STEPS, 2), edge(STEPS, 2), edge(STEPS, 2), edge(STEPS, 2),
            edge(STEPS, 2), edge(STEPS, 2), V(slots, 1), V(slots, ND, 1),
            pltpu.SemaphoreType.REGULAR((2,)), dma((4,)), dma((6,)), dma((6,)), dma((3,)), dma((3,)), dma((2,)), dma((2,)), dma((2, 2)), dma((2, 2)),
            dma((2,)), dma((2, 2)), dma((2,)), dma((2, 2)), dma((2, 2)), dma((2, 2, 2)), dma((1,)), dma((3,)),
            dma((5,)), dma((5,)),
        ],
        compiler_params=pltpu.CompilerParams(collective_id=1, has_side_effects=True),
    )(u, prec, bound, cap, capacity, bv, tc, dens, slope, om)
    return pl.pallas_call(
        store_kernel,
        out_shape=(
            jax.ShapeDtypeStruct(u.shape, f32),
            jax.ShapeDtypeStruct(prec.shape, f32),
            jax.ShapeDtypeStruct(bound.shape, f32),
            jax.ShapeDtypeStruct(cap.shape, f32),
            jax.ShapeDtypeStruct((1,), f32),
        ),
        in_specs=[vmem] * 4,
        out_specs=(hbm, hbm, hbm, smem, smem),
        scratch_shapes=[dma((3,))],
    )(*[pltpu.with_memory_space_constraint(x, pltpu.VMEM) for x in ours])


def solution(mesh):
    NS, NPD = mesh.shape["strip"], mesh.shape["period"]

    def per_device(u, prec, bound, cap, capacity, bv, tc, dens, slope, om):
        rows_here, T, Z, Y = u.shape
        assert rows_here == 1
        NP = NPD * T
        if NS % 2 == 0 and Z == 2 * NPD * ROWS and NP % ROWS == 0 and 2 * NP < Y:
            return pair_call(NS, NPD, u, prec, bound, cap, capacity, bv, tc, dens, slope, om)
        R = -(-T // 8) * 8
        f32 = jnp.float32
        vmem = pl.BlockSpec(memory_space=pltpu.VMEM)
        hbm = pl.BlockSpec(memory_space=pl.ANY)
        smem = pl.BlockSpec(memory_space=pltpu.SMEM)
        plane = lambda *n: pltpu.VMEM((*n, Z, Y), f32)
        dma = pltpu.SemaphoreType.DMA
        slots = 1 + STEPS + OUTER
        far = max(NPD - 1, 1)
        return pl.pallas_call(
            functools.partial(kernel, NS, NPD, T, Z, Y, R),
            out_shape=(
                pltpu.VMEM(u.shape, f32),
                pltpu.VMEM(prec.shape, f32),
                pltpu.VMEM(bound.shape, f32),
                jax.ShapeDtypeStruct(cap.shape, f32),
                jax.ShapeDtypeStruct((1,), f32),
            ),
            in_specs=[hbm, hbm, hbm, smem, smem, vmem, vmem, smem, vmem, smem],
            out_specs=(vmem, vmem, vmem, smem, smem),
            scratch_shapes=[
                plane(T), plane(T), plane(T), plane(T), plane(T), plane(T),
                plane(7, T), plane(7, T), plane(7, T), plane(7), plane(), plane(T), plane(T), plane(T), plane(),
                plane(STEPS, T), plane(2, STEPS, T), plane(STEPS), plane(STEPS, far),
                plane(STEPS), plane(STEPS, far),
                pltpu.VMEM((slots, 1, Y), f32), pltpu.VMEM((slots, NS, 1, Y), f32),
                pltpu.VMEM((OUTER, 1, Y), f32), pltpu.VMEM((OUTER, NPD, 1, Y), f32),
                pltpu.VMEM((2, 1, Y), jnp.int32),
                plane(5, T), plane(2), plane(2), dma((3,)),
                dma((2, 3)), dma((2, 3)), dma((2, 2, STEPS)), dma((2, 2, STEPS)),
                dma((STEPS, far)), dma((STEPS, far)), dma((STEPS, far)), dma((STEPS, far)),
                dma((slots, NS - 1)), dma((slots, NS - 1)), dma((OUTER, far)), dma((OUTER, far)),
            ],
            compiler_params=pltpu.CompilerParams(collective_id=0, has_side_effects=True),
        )(u, prec, bound, cap, capacity, bv, tc, dens, slope, om)

    in_specs = (
        P("strip", "period", None, None),
        P(None, "strip", "period", None, None),
        P("strip", "period", None, None),
        P("period"),
        P("period"),
        P("strip", None, None),
        P("strip", None, None),
        P(),
        P("strip", None),
        P(),
    )
    out_specs = (
        P("strip", "period", None, None),
        P(None, "strip", "period", None, None),
        P("strip", "period", None, None),
        P("period"),
        P(),
    )
    return jax.shard_map(
        per_device, mesh=mesh, in_specs=in_specs, out_specs=out_specs, check_vma=False
    )
```

```python
import functools
import math

import jax
import jax.numpy as jnp
from jax import lax
from jax.experimental import pallas as pl
from jax.experimental.pallas import tpu as pltpu
from jax.sharding import PartitionSpec as P

OUTER = 2
INNER = 3
STEPS = OUTER * INNER
RATE = math.log(1.1) / 12.0
EPS = 1e-06
SLOPE = 11.0
MESH = pl.DeviceIdType.MESH
ROWS = 8
CHUNK = 8


def kernel(
    NS, NPD, T, Z, Y, R,
    u_ref, prec_ref, bound_ref, cap_ref, capacity_ref, bv_ref, tc_ref, dens_ref, slope_ref, om_ref,
    u_out, prec_out, bound_out, cap_out, w_out,
    uf, uc, us, bf, bc, bs, fa, ca, sa, act, ton, tb, tl, cb, ex0,
    xs, xr, es, er, as_, ar, rs, rb, ps, pb, slr,
    praw, ti, to_sum, loc, ini_s, ini_r, xs_s, xs_r, e_s, e_r, a_s, a_r, r_s, r_r, p_s, p_r,
):
    me = lax.axis_index("strip")
    pe = lax.axis_index("period")
    total_rows = NS
    total_periods = NPD * T
    blocks_all = float(total_rows * Z * Y)
    root_blocks = math.sqrt(blocks_all)
    sends = []

    loads = (
        pltpu.make_async_copy(prec_ref.at[:, 0], praw, loc.at[0]),
        pltpu.make_async_copy(bound_ref.at[0], bf, loc.at[1]),
        pltpu.make_async_copy(u_ref.at[0], uf, loc.at[2]),
    )
    for load in loads:
        load.start()
    barrier = pltpu.get_barrier_semaphore()
    for k in range(1, NS):
        pl.semaphore_signal(barrier, inc=1, device_id={"strip": lax.rem(me + k, NS)}, device_id_type=MESH)
    for k in range(1, NPD):
        pl.semaphore_signal(barrier, inc=1, device_id={"period": lax.rem(pe + k, NPD)}, device_id_type=MESH)

    has = (me < NS - 1, me > 0)
    gets = (me > 0, me < NS - 1)
    to = (me + 1, me - 1)

    def remote(src, dst, ss, rr, dev):
        return pltpu.make_async_remote_copy(
            src_ref=src, dst_ref=dst, send_sem=ss, recv_sem=rr, device_id=dev, device_id_type=MESH
        )

    def ini_copy(d, what):
        if what == 2:
            return remote(to_sum.at[d], ti.at[d], ini_s.at[d, 2], ini_r.at[d, 2], {"strip": to[d]})
        if what == 0:
            rest = pl.ds(1, T - 1)
            return remote(praw.at[1 + d, rest], fa.at[5 + d, rest], ini_s.at[d, 0], ini_r.at[d, 0], {"strip": to[d]})
        return remote(slope_ref, slr.at[d], ini_s.at[d, 1], ini_r.at[d, 1], {"strip": to[d]})

    def x_copy(d, part, s):
        lo, size = (1, T - 1) if part == 0 else (0, 1)
        return remote(
            xs.at[s, pl.ds(lo, size)], xr.at[d, s, pl.ds(lo, size)],
            xs_s.at[d, part, s], xs_r.at[d, part, s], {"strip": to[d]},
        )

    def e_copy(k, s):
        return remote(es.at[s], er.at[s, k - 1], e_s.at[s, k - 1], e_r.at[s, k - 1], {"period": pe + k})

    def a_copy(k, s):
        return remote(as_.at[s], ar.at[s, k - 1], a_s.at[s, k - 1], a_r.at[s, k - 1], {"period": pe - k})

    def r_copy(k, slot):
        return remote(
            rs.at[slot], rb.at[slot, me], r_s.at[slot, k - 1], r_r.at[slot, k - 1],
            {"strip": lax.rem(me + k, NS)},
        )

    def p_copy(k, slot):
        return remote(
            ps.at[slot], pb.at[slot, pe], p_s.at[slot, k - 1], p_r.at[slot, k - 1],
            {"period": lax.rem(pe + k, NPD)},
        )

    def start(cond, copy):
        def go():
            copy.start()
        if cond is None:
            go()
        else:
            pl.when(cond)(go)
        sends.append((cond, copy))

    def wait_recv(cond, copy):
        if cond is None:
            copy.wait_recv()
        else:
            pl.when(cond)(lambda: copy.wait_recv())

    def reduce_start(slot, value):
        rs[slot] = value
        rb[slot, me] = value
        for k in range(1, NS):
            start(None, r_copy(k, slot))

    def reduce_done(slot):
        for k in range(1, NS):
            wait_recv(None, r_copy(k, slot))
        total = rb[slot, 0]
        for k in range(1, NS):
            total = total + rb[slot, k]
        return total

    loads[0].wait()
    for d in range(2):
        total = praw[1 + d, 0]
        for t in range(1, T):
            total = total + praw[1 + d, t]
        to_sum[d] = total
    pl.semaphore_wait(barrier, NS + NPD - 2)
    for d in range(2):
        start(has[d], ini_copy(d, 1))
        start(has[d], ini_copy(d, 2))
    for d in range(2):
        start(has[d], ini_copy(d, 0))

    rows = lax.broadcasted_iota(jnp.int32, (R, Y), 0)
    lanes = lax.broadcasted_iota(jnp.int32, (R, Y), 1)

    def as_lanes(value):
        sums = jnp.sum(value, axis=1, keepdims=True)
        return jnp.sum(jnp.where(lanes == rows, sums, 0.0), axis=0, keepdims=True)

    def as_rows(line):
        return jnp.sum(jnp.where(lanes == rows, line, 0.0), axis=1, keepdims=True)

    def fold(v):
        return jnp.sum(v.reshape(Z // 8, 8, Y), axis=0)

    cls = tc_ref[0]
    tons = jnp.zeros((Z, Y), jnp.float32)
    for c in range(dens_ref.shape[0]):
        tons = jnp.where(cls == c, (1.0 + c) * dens_ref[c], tons)
    ton[...] = tons
    part = jnp.sum(tons, axis=0, keepdims=True)
    reduce_start(0, part)

    z_ids = lax.broadcasted_iota(jnp.int32, (Z, Y), 0)
    y_ids = lax.broadcasted_iota(jnp.int32, (Z, Y), 1)

    def mask_of(codes, k, inside):
        ok = z_ids >= 1
        if k > 0:
            ok = ok & (jnp.broadcast_to((codes >> (k - 1)) & 1, (Z, Y)) == 1)
        if k == 3:
            ok = ok & (y_ids < Y - 1)
        if k == 4:
            ok = ok & (y_ids >= 1)
        if inside is not None:
            ok = ok & (jnp.full((Z, Y), inside.astype(jnp.int32)) == 1)
        return ok.astype(jnp.float32)

    own = slope_ref[...]
    act[0] = mask_of(own, 0, None)
    act[1] = mask_of(own, 1, me < NS - 1)
    act[2] = mask_of(own, 2, me > 0)
    act[3] = mask_of(own, 3, None)
    act[4] = mask_of(own, 4, None)

    period = [(pe * T + t).astype(jnp.float32) for t in range(T)]
    pid = [jnp.full((1, Y), period[t]) for t in range(T)]
    disc = [jnp.exp(-RATE * pid[t]) for t in range(T)]
    tonr = ton[...] * (1.0 / root_blocks)
    for load in loads[1:]:
        load.wait()
    for t in range(T):
        tb[t] = 1.0 / (SLOPE * (total_periods - pid[t]) + tonr)
        for k in range(5):
            fa[k, t] = praw[k, t] * act[k]

    caps = jnp.zeros((R, Y), jnp.float32)
    climit = jnp.zeros((R, Y), jnp.float32)
    for t in range(T):
        caps = jnp.where(rows == t, cap_ref[t], caps)
        climit = jnp.where(rows == t, capacity_ref[t] * blocks_all, climit)
    w = jnp.full((1, Y), om_ref[0])

    for d in range(2):
        @pl.when(jnp.logical_not(gets[d]))
        def _():
            act[5 + d] = jnp.zeros((Z, Y), jnp.float32)
            ti[d] = jnp.zeros((Z, Y), jnp.float32)
            fa[5 + d] = jnp.zeros((T, Z, Y), jnp.float32)
            for s in range(STEPS):
                xr[d, s] = jnp.zeros((T, Z, Y), jnp.float32)

    def up_y(v):
        return pltpu.roll(v, 1, 1)

    def dn_y(v):
        return pltpu.roll(v, Y - 1, 1)

    def up_z(v):
        return pltpu.roll(v, 1, 0)

    def dn_z(v):
        return pltpu.roll(v, Z - 1, 0)

    def settle(first, cur, acc, at, j, new, old):
        if j == 0:
            cur[at] = new
            return new, None
        if j == 1:
            cur[at] = new
            acc[at] = old + new
            return new, None
        mean = (acc[at] + new) * (1.0 / INNER)
        diff = mean - first[at]
        first[at] = mean
        return mean, fold(diff * diff)

    def gradient_own(arcs, bounds):
        for t in range(T):
            p0, p3, p4 = arcs[0, t], arcs[3, t], arcs[4, t]
            back = p0 + (up_y(p3) + dn_y(p4))
            tl[t] = ((p0 + p3) + (p4 + bounds[t])) - dn_z(back)

    def gradient(s, arcs):
        tail = None
        for t in range(T - 1, -1, -1):
            g = (tl[t] + (arcs[1, t] + arcs[2, t])) - dn_z(arcs[5, t] + arcs[6, t])
            tail = g if tail is None else tail + g
            tl[t] = tail
        as_[s] = tail
        for k in range(1, NPD):
            start(pe >= k, a_copy(k, s))

    tail = None
    for t in range(T - 1, -1, -1):
        p = [fa[k, t] for k in range(5)]
        g = (((p[0] + p[1]) + (p[2] + p[3])) + p[4]) + bf[t]
        g = g - dn_z(p[0] + (up_y(p[3]) + dn_y(p[4])))
        tail = g if tail is None else tail + g
        tl[t] = tail
    for d in range(2):
        wait_recv(gets[d], ini_copy(d, 1))
        wait_recv(gets[d], ini_copy(d, 2))

        @pl.when(gets[d])
        def _():
            act[5 + d] = mask_of(slr[d], 1 + d, None)
    as_[0] = tl[0] - dn_z(ti[0] * act[5] + ti[1] * act[6])
    for k in range(1, NPD):
        start(pe >= k, a_copy(k, 0))
    for d in range(2):
        wait_recv(gets[d], ini_copy(d, 0))
        rest = ti[d]
        for t in range(1, T):
            plane = fa[5 + d, t]
            rest = rest - plane
            fa[5 + d, t] = plane * act[5 + d]
        fa[5 + d, 0] = rest * act[5 + d]
    tail = None
    for t in range(T - 1, -1, -1):
        back = fa[5, t] + fa[6, t]
        tail = back if tail is None else tail + back
        tl[t] = tl[t] - dn_z(tail)
    tons_all = jnp.sum(reduce_done(0), axis=1, keepdims=True)
    inv_tons = 1.0 / tons_all
    cap_first = cap_sum = None

    for s in range(STEPS):
        j = s % INNER
        u_src = uf if j == 0 else uc
        b_src = bf if j == 0 else bc
        p_src = fa if j == 0 else ca
        inv_w = 1.0 / w
        move_p = jnp.zeros((8, Y), jnp.float32)
        move_d = jnp.zeros((8, Y), jnp.float32)
        for k in range(1, NPD):
            @pl.when(pe + k < NPD)
            def _():
                a_copy(k, s).wait_recv()
                for t in range(T):
                    tl[t] = tl[t] + ar[s, k - 1]
        head = None
        row = jnp.zeros((R, Y), jnp.float32)
        for t in range(T):
            old = u_src[t]
            grad = tl[t] + (ton[...] * (1.0 / root_blocks)) * caps[t : t + 1, :]
            new = jnp.maximum(old - (tb[t] * inv_w) * (grad - bv_ref[0] * disc[t]), 0.0)
            ext = 2.0 * new - old
            _, moved = settle(uf, uc, us, t, j, new, old)
            if moved is not None:
                move_p = move_p + moved
            if t == 0:
                ex0[...] = ext
            else:
                xs[s, t] = ext
            head = ext if head is None else head + ext
            row = jnp.where(rows == t, jnp.sum(ton[...] * ext, axis=0, keepdims=True), row)
        es[s] = head
        for k in range(1, NPD):
            start(pe + k < NPD, e_copy(k, s))
        for d in range(2):
            start(has[d], x_copy(d, 0, s))
        for k in range(1, NPD):
            @pl.when(pe >= k)
            def _():
                e_copy(k, s).wait_recv()
                ex0[...] = ex0[...] + er[s, k - 1]
        xs[s, 0] = ex0[...]
        for d in range(2):
            start(has[d], x_copy(d, 1, s))
        reduce_start(1 + s, as_lanes(row))
        total = None
        for t in range(T):
            total = xs[s, t] if t == 0 else total + xs[s, t]
            cb[t] = total
        rate_b = [w / (pid[t] + 1.0) for t in range(T)]
        rate_p = [w / (2.0 * (pid[t] + 1.0)) for t in range(T)]

        def arc(k, t, diff, move):
            old = p_src[k, t]
            new = jnp.maximum(old + rate_p[t] * diff, 0.0) * act[k]
            _, moved = settle(fa, ca, sa, (k, t), j, new, old)
            if moved is not None and k < 5:
                move = move + moved
            return move

        for t in range(T):
            c = cb[t]
            old = b_src[t]
            new = jnp.maximum(old + rate_b[t] * (c - 1.0), 0.0)
            _, moved = settle(bf, bc, bs, t, j, new, old)
            if moved is not None:
                move_d = move_d + moved
            cz = up_z(c)
            move_d = arc(0, t, c - cz, move_d)
            move_d = arc(3, t, c - dn_y(cz), move_d)
            move_d = arc(4, t, c - up_y(cz), move_d)
        last = j == INNER - 1
        if s < STEPS - 1:
            gradient_own(fa if last else ca, bf if last else bc)
        for part in range(2):
            for d in range(2):
                wait_recv(gets[d], x_copy(d, part, s))
        total_m = total_p = None
        for t in range(T):
            total_m = xr[0, s, t] if t == 0 else total_m + xr[0, s, t]
            total_p = xr[1, s, t] if t == 0 else total_p + xr[1, s, t]
            c = cb[t]
            cz = up_z(c)
            move_d = arc(1, t, c - up_z(total_p), move_d)
            move_d = arc(2, t, c - up_z(total_m), move_d)
            if s < STEPS - 1:
                arc(5, t, total_m - cz, None)
                arc(6, t, total_p - cz, None)
        if s < STEPS - 1:
            gradient(s + 1, fa if last else ca)
        if last:
            cyc = s // INNER
            mp = jnp.sum(move_p, axis=0, keepdims=True)
            md = jnp.sum(move_d, axis=0, keepdims=True)
            reduce_start(1 + STEPS + cyc, as_lanes(jnp.where(rows == 0, mp, jnp.where(rows == 1, md, 0.0))))
        row_total = as_rows(reduce_done(1 + s))
        new_caps = jnp.maximum(caps + w * ((row_total - climit) * inv_tons), 0.0)
        new_caps = jnp.where(rows < T, new_caps, 0.0)
        if j == 0:
            cap_first = caps
            cap_sum = new_caps
        else:
            cap_sum = cap_sum + new_caps
        caps = new_caps
        if last:
            caps = cap_sum * (1.0 / INNER)
            cap_move = jnp.sum((caps - cap_first) ** 2, axis=0, keepdims=True)
            got = reduce_done(1 + STEPS + cyc)
            msg = got + jnp.where(lanes[0:1] == 1, cap_move, 0.0)
            ps[cyc] = msg
            pb[cyc, pe] = msg
            for k in range(1, NPD):
                start(None, p_copy(k, cyc))
            if s == STEPS - 1:
                for t in range(T):
                    u_out[0, t] = uf[t]
                    bound_out[0, t] = bf[t]
                    for k in range(5):
                        prec_out[k, 0, t] = fa[k, t]
                    cap_out[t] = caps[t, 0]
            for k in range(1, NPD):
                wait_recv(None, p_copy(k, cyc))
            tot = pb[cyc, 0]
            for k in range(1, NPD):
                tot = tot + pb[cyc, k]
            tot = as_rows(tot)
            moved = jnp.sqrt((tot[1:2, :] + EPS) / (tot[0:1, :] + EPS))
            w = jnp.sqrt(w * moved)
    w_out[0] = w[0, 0]
    for cond, copy in sends:
        if cond is None:
            copy.wait_send()
        else:
            pl.when(cond)(lambda copy=copy: copy.wait_send())


def pair_kernel(
    NS, NPD, T, Z, Y,
    u_ref, prec_ref, bound_ref, cap_ref, capacity_ref, bv_ref, tc_ref, dens_ref, slope_ref, om_ref,
    u_out, prec_out, bound_out, few_out,
    slope_own, cap_own, capacity_own, dens_own, om_own, cap_line, capb, praw, braw, gh, hh, pu, pb, pg, pp, hpr, nraw, hnr, bvb, tcb, slr,
    fa, ca, sa, fn, cn, sn, fh, ch, sh, bf, bc, bs, uf, uc, us,
    act, nact, hact, ton, tb, pr, tl, tt, rp, rh,
    xs, xr, hs, ls, zh, zl, dh, dl, rs, rb,
    token, loc, ini_s, ini_r, sl_s, sl_r, sm_s, sm_r, re_s, re_r,
    x_s, x_r, z_s, z_r, d_s, d_r, r_s, r_r, o_s, o_r,
):
    me = lax.axis_index("strip")
    pe = lax.axis_index("period")
    pairs, NP, NQ = NS // 2, NPD * T, 2 * NPD
    NT = NP // ROWS
    ND = NS * NPD
    a, h = me // 2, lax.rem(me, 2)
    q = jnp.where(h == 0, pe, NQ - 1 - pe)
    blocks_all = float(NS * Z * Y)
    inv_root = 1.0 / math.sqrt(blocks_all)
    sends = []

    def rows_of(block):
        return pl.ds(pl.multiple_of(ROWS * block, ROWS), ROWS)

    def block_of(hh_, pp_):
        return jnp.where(hh_ == 0, pp_, NQ - 1 - pp_)

    def device_at(pair, block):
        first = block < NPD
        return {
            "strip": 2 * pair + jnp.where(first, 0, 1),
            "period": jnp.where(first, block, NQ - 1 - block),
        }

    def remote(src, dst, ss, rr, dev):
        return pltpu.make_async_remote_copy(
            src_ref=src, dst_ref=dst, send_sem=ss, recv_sem=rr, device_id=dev, device_id_type=MESH
        )

    def start(cond, copy):
        if cond is None:
            copy.start()
        else:
            pl.when(cond)(lambda: copy.start())
        sends.append((cond, copy))

    def wait_recv(cond, copy):
        if cond is None:
            copy.wait_recv()
        else:
            pl.when(cond)(lambda: copy.wait_recv())

    mine = pl.ds(pe * T, T)
    unit = h * NPD + pe
    peers = pl.ds(0, NQ - 1)
    loads = (
        pltpu.make_async_copy(prec_ref.at[:, 0], praw, loc.at[0]),
        pltpu.make_async_copy(prec_ref.at[:, 0, :, rows_of(q)], pp.at[:, unit], loc.at[1]),
        pltpu.make_async_copy(bound_ref.at[0, :, rows_of(q)], pb.at[unit], loc.at[2]),
        pltpu.make_async_copy(u_ref.at[0, :, rows_of(q)], pu.at[unit], loc.at[3]),
        pltpu.make_async_copy(bound_ref.at[0], braw, loc.at[4]),
        pltpu.make_async_copy(slope_ref, slope_own, loc.at[5]),
        pltpu.make_async_copy(cap_ref, cap_own, loc.at[6]),
        pltpu.make_async_copy(capacity_ref, capacity_own, loc.at[7]),
        pltpu.make_async_copy(dens_ref, dens_own, loc.at[8]),
        pltpu.make_async_copy(om_ref, om_own, loc.at[9]),
        pltpu.make_async_copy(bv_ref.at[0, rows_of(q)], bvb.at[h], loc.at[10]),
        pltpu.make_async_copy(tc_ref.at[0, rows_of(q)], tcb.at[h], loc.at[11]),
    )
    for load in loads:
        load.start()
    barrier = pltpu.get_barrier_semaphore()
    others = [divmod(k, NPD) for k in range(1, ND)]
    others.sort(key=lambda o: -abs(o[0] - NS // 2) if o[0] else NS)

    def other(ks, kp):
        return {"strip": lax.rem(me + ks, NS), "period": lax.rem(pe + kp, NPD)}

    mates = [divmod(k, NPD) for k in range(1, NQ)]

    def mate(i):
        kh, kp = mates[i]
        return lax.rem(h + kh, 2), lax.rem(pe + kp, NPD)

    has = (a > 0, a < pairs - 1)
    up = (q > 0, q < NQ - 1)
    beside = [device_at(a - 1, q), device_at(a + 1, q)]
    for i in range(NQ - 1):
        th, tp = mate(i)
        pl.semaphore_signal(barrier, inc=1, device_id={"strip": 2 * a + th, "period": tp}, device_id_type=MESH)
    for d in range(2):
        pl.when(has[d])(
            lambda d=d: pl.semaphore_signal(barrier, inc=1, device_id=beside[d], device_id_type=MESH)
        )

    def in_ends(what, rows, block, at):
        if what == 1:
            return hh.at[block], hpr.at[at]
        if what == 2:
            return gh.at[:, rows], pg.at[at]
        if what == 7:
            return cap_line, capb.at[at]
        if what == 3:
            return u_ref.at[0, :, rows], pu.at[at]
        if what == 4:
            return bound_ref.at[0, :, rows], pb.at[at]
        arcs = {0: pl.ds(1, 2), 5: 0, 6: pl.ds(3, 2)}[what]
        return prec_ref.at[arcs, 0, :, rows], pp.at[arcs, at]

    def in_copy(i, what):
        th, tp = mate(i)
        block = block_of(th, tp)
        src, dst = in_ends(what, rows_of(block), block, unit)
        return remote(src, dst, ini_s.at[what], ini_r.at[what], {"strip": 2 * a + th, "period": tp})

    def in_all(what):
        dst = in_ends(what, rows_of(0), 0, peers)[1]
        return remote(dst, dst, ini_s.at[what], ini_r.at[what], other(0, 1))

    def partner_copy(what):
        rows = rows_of(block_of(1 - h, pe))
        dev = {"strip": 2 * a + 1 - h, "period": pe}
        if what == 0:
            return remote(tc_ref.at[0, rows], tcb.at[h], sm_s.at[0], sm_r.at[0], dev)
        return remote(bv_ref.at[0, rows], bvb.at[h], sm_s.at[1], sm_r.at[1], dev)

    def slope_copy(what):
        if what == 2:
            return remote(slope_ref, slr.at[1 + h], sl_s.at[2], sl_r.at[2], {"strip": 2 * a + 1 - h, "period": pe})
        return remote(slr.at[1 + what], slr.at[3 - 3 * what], sl_s.at[what], sl_r.at[1 - what], beside[what])

    def relay_copy(d, what):
        dev = beside[d]
        k, hs_ = (2, 0) if d == 0 else (1, 1)
        ss, rr = re_s.at[d, what], re_r.at[d, what]
        if what == 0:
            return remote(pp.at[k, pl.ds(hs_ * NPD, NPD)], nraw.at[1 - d], ss, rr, dev)
        return remote(hpr.at[pl.ds(hs_ * NPD, NPD), k], hnr.at[1 - d], ss, rr, dev)

    def reduce_sem(slot):
        return r_r.at[slot % 2 if slot < STEPS else 2]

    def reduce_start(slot, value):
        rs[slot] = value
        rb[slot, me * NPD + pe] = value
        for ks, kp in others:
            remote(
                rs.at[slot], rb.at[slot, me * NPD + pe], r_s.at[0], reduce_sem(slot), other(ks, kp)
            ).start()

    def reduce_done(slot):
        rest = rb.at[slot, pl.ds(0, ND - 1)]
        remote(rest, rest, r_s.at[0], reduce_sem(slot), other(0, 1)).wait_recv()
        parts = [rb[slot, i] for i in range(ND)]
        while len(parts) > 1:
            parts = [parts[i] + parts[i + 1] if i + 1 < len(parts) else parts[i] for i in range(0, len(parts), 2)]
        return parts[0]

    def x_copy(d, s):
        dev = beside[d]
        return remote(xs.at[s, d], xr.at[s, 1 - d], x_s.at[d], x_r.at[s % 2, 1 - d], dev)

    def z_copy(d, s):
        if d == 0:
            return remote(ls.at[s], zl.at[s], z_s.at[0], z_r.at[s % 2, 0], device_at(a, q - 1))
        return remote(hs.at[s], zh.at[s], z_s.at[1], z_r.at[s % 2, 1], device_at(a, q + 1))

    def d_copy(d, e, s):
        dev = device_at(a - 1 if d == 0 else a + 1, q - 1 if e == 0 else q + 1)
        src, dst = (ls, dl) if e == 0 else (hs, dh)
        return remote(src.at[s, d], dst.at[s, 1 - d], d_s.at[d, e], d_r.at[s % 2, 1 - d, e], dev)

    def out_ends(what, th, part, rows):
        if what == 0:
            return uf.at[th, part], u_out.at[0, :, rows]
        if what == 1:
            return bf.at[th, part], bound_out.at[0, :, rows]
        arcs = (0, pl.ds(3, 2), pl.ds(1, 2))[what - 2]
        return fa.at[arcs, th, part], prec_out.at[arcs, 0, :, rows]

    def out_start(what):
        for i in range(NQ - 1):
            th, tp = mate(i)
            src, dst = out_ends(what, th, pl.ds(tp * T, T), rows_of(q))
            remote(src, dst, o_s.at[what], o_r.at[what], {"strip": 2 * a + th, "period": tp}).start()

    def out_all(what):
        dst = out_ends(what, 0, mine, pl.ds(0, ROWS * (NQ - 1)))[1]
        return remote(dst, dst, o_s.at[what], o_r.at[what], other(0, 1))

    lanes1 = lax.broadcasted_iota(jnp.int32, (1, Y), 1)
    rows = lax.broadcasted_iota(jnp.int32, (NP, Y), 0)
    lanes = lax.broadcasted_iota(jnp.int32, (NP, Y), 1)

    def tons_of(cls):
        tons = jnp.zeros(cls.shape, jnp.float32)
        for c in range(dens_own.shape[0]):
            tons = jnp.where(cls == c, (1.0 + c) * dens_own[c], tons)
        return tons

    def as_lanes(value):
        sums = jnp.sum(value, axis=1, keepdims=True)
        return jnp.sum(jnp.where(lanes == rows, sums, 0.0), axis=0, keepdims=True)

    def as_rows(line, at=0):
        return jnp.broadcast_to(jnp.sum(jnp.where(lanes == rows + at, line, 0.0), axis=1, keepdims=True), (NP, Y))

    def roll(v, by, axis):
        return pltpu.roll(v, by % v.shape[axis], axis)

    def up_y(v):
        return roll(v, 1, v.ndim - 1)

    def dn_y(v):
        return roll(v, -1, v.ndim - 1)

    def mask_of(code, k, depth, inside):
        ok = (depth >= 1) & (depth < Z)
        y_ids = lax.broadcasted_iota(jnp.int32, depth.shape, 1)
        if k > 0:
            ok = ok & (jnp.broadcast_to((code >> (k - 1)) & 1, depth.shape) == 1)
        if k == 3:
            ok = ok & (y_ids < Y - 1)
        if k == 4:
            ok = ok & (y_ids >= 1)
        if inside is not None:
            ok = ok & (jnp.full(depth.shape, inside.astype(jnp.int32)) == 1)
        return ok.astype(jnp.float32)

    def send_all(*kinds):
        for what in kinds:
            for i in range(NQ - 1):
                in_copy(i, what).start()

    pl.semaphore_wait(barrier, NQ - 1 + has[0].astype(jnp.int32) + has[1].astype(jnp.int32))
    send_all(0)
    start(None, slope_copy(2))
    start(None, partner_copy(0))
    start(None, partner_copy(1))
    send_all(3)
    for load in loads[6:10]:
        load.wait()
    line = jnp.zeros((1, Y), jnp.float32)
    for t in range(T):
        line = jnp.where(lanes1 == pe * T + t, cap_own[t], line)
        line = jnp.where(lanes1 == NP + pe * T + t, capacity_own[t], line)
    cap_line[...] = line
    capb[unit] = line
    loads[0].wait()
    for b in range(NQ):
        if b + 1 < NQ:
            for k in range(5):
                for t in range(T):
                    hh[b, k, pl.ds(t, 1)] = praw[k, t, pl.ds(ROWS * (b + 1), 1)]
        else:
            hh[b] = jnp.zeros((5, T, Y), jnp.float32)
    hpr[unit] = hh[q]
    send_all(1, 7)
    z_ids = lax.broadcasted_iota(jnp.int32, (ROWS, Y), 0)
    low = z_ids == ROWS - 1
    depth = lax.broadcasted_iota(jnp.int32, (Z, Y), 0)
    loads[5].wait()
    home = {k: mask_of(slope_own[...], k, depth, None) for k in (0, 3, 4)}
    loads[4].wait()
    for t in range(T):
        p0, p3, p4 = (praw[k, t] * home[k] for k in (0, 3, 4))
        gh[t] = ((p0 + p3) + (p4 + braw[t])) - roll(p0 + (up_y(p3) + dn_y(p4)), -1, 0)
    pg[unit] = gh[:, rows_of(q)]
    send_all(2, 4, 5)
    slr[1 + h] = slope_own[...]
    for d in range(2):
        @pl.when(jnp.logical_not(has[d]))
        def _():
            for s in range(STEPS):
                xr[s, d] = jnp.zeros((NP, ROWS, Y), jnp.float32)
            nraw[d] = jnp.zeros((NPD, T, ROWS, Y), jnp.float32)
            hnr[d] = jnp.zeros((NPD, T, Y), jnp.float32)
            slr[3 * d] = jnp.zeros((1, Y), jnp.int32)
        for e in range(2):
            buf = (dh, dl)[e]

            @pl.when(jnp.logical_not(has[d] & up[e]))
            def _():
                for s in range(STEPS):
                    buf[s, d] = jnp.zeros((NT, ROWS, Y), jnp.float32)
    for e in range(2):
        buf = (zh, zl)[e]

        @pl.when(jnp.logical_not(up[e]))
        def _():
            for s in range(STEPS):
                buf[s] = jnp.zeros((2, NT, ROWS, Y), jnp.float32)

    wait_recv(None, slope_copy(2))
    for d in range(2):
        start(has[d], slope_copy(d))
    here, below = z_ids + ROWS * q, jnp.full((ROWS, Y), ROWS * (q + 1))
    for hh_ in range(2):
        code = slr[1 + hh_]
        for k in range(5):
            inside = None
            if k == 1 and hh_ == 1:
                inside = has[1]
            if k == 2 and hh_ == 0:
                inside = has[0]
            act[k, hh_] = mask_of(code, k, here, inside)
            hact[k, hh_] = mask_of(code, k, below, inside)
    for d in range(2):
        wait_recv(has[d], slope_copy(1 - d))
        nact[d] = mask_of(slr[3 * d], 1 + d, here + 1, has[d])

    wait_recv(None, partner_copy(0))
    wait_recv(None, partner_copy(1))
    loads[10].wait()
    loads[11].wait()
    for hh_ in range(2):
        tons = tons_of(tcb[hh_])
        ton[hh_] = tons
        for t in range(NP):
            tb[hh_, t] = 1.0 / (SLOPE * (NP - t) + tons * inv_root)
            pr[hh_, t] = bvb[hh_] * math.exp(-RATE * t)

    t_plane = lax.broadcasted_iota(jnp.int32, (NP, ROWS, Y), 0).astype(jnp.float32)
    t_rows = (
        lax.broadcasted_iota(jnp.int32, (NT, ROWS, Y), 0) * ROWS + lax.broadcasted_iota(jnp.int32, (NT, ROWS, Y), 1)
    ).astype(jnp.float32)

    w = jnp.full((1, Y), om_own[0])

    def set_rates(w):
        rp[...] = w[None] / (2.0 * (t_plane + 1.0))
        rh[...] = w[None] / (2.0 * (t_rows + 1.0))

    set_rates(w)

    for d in range(2):
        pl.when(has[1 - d])(lambda d=d: pl.semaphore_wait(token.at[d], 1))
        pl.when(has[d])(
            lambda d=d: pl.semaphore_signal(token.at[d], inc=1, device_id=beside[d], device_id_type=MESH)
        )
    loads[1].wait()
    in_all(0).wait_recv()
    for d in range(2):
        start(has[d], relay_copy(d, 0))
    in_all(1).wait_recv()
    for d in range(2):
        start(has[d], relay_copy(d, 1))

    chunks = [(lo, min(CHUNK, NP - lo)) for lo in range(0, NP, CHUNK)]

    def lines(ref, lo, size, *at):
        picked = [ref[(*at, t // ROWS, pl.ds(t % ROWS, 1))] for t in range(lo, lo + size)]
        return jnp.stack([jnp.broadcast_to(p, (ROWS, Y)) for p in picked])

    def from_above(v, line):
        return jnp.where(lax.broadcasted_iota(jnp.int32, v.shape, 1) == 0, line, roll(v, 1, 1))

    def from_below(v, line):
        return jnp.where(lax.broadcasted_iota(jnp.int32, v.shape, 1) == ROWS - 1, line, roll(v, -1, 1))

    def landed(ref, hh_, *at):
        return ref[(*at, pl.ds(hh_ * NPD, NPD))].reshape(NP, ROWS, Y)

    def mask_arcs(ks):
        for k in ks:
            for hh_ in range(2):
                fa[k, hh_] = landed(pp, hh_, k) * act[k, hh_][None]

    def mask_halo(ks):
        for k, hh_ in ks:
            for at in range(NP):
                line = hpr[hh_ * NPD + at // T, k, pl.ds(at % T, 1)]
                fh[k, hh_, at // ROWS, pl.ds(at % ROWS, 1)] = line * hact[k, hh_, 0:1]

    mask_arcs((1, 2))
    mask_halo(((1, 0), (2, 1)))
    for d in range(2):
        wait_recv(has[d], relay_copy(1 - d, 0))
        wait_recv(has[d], relay_copy(1 - d, 1))
        for t in range(NP):
            edge = jnp.broadcast_to(hnr[d, t // T, pl.ds(t % T, 1)], (ROWS, Y))
            fn[d, t] = jnp.where(low, edge, roll(nraw[d, t // T, t % T], -1, 0)) * nact[d]

    def settle(first, cur, acc, at, j, new, old):
        if j == 0:
            cur[at] = new
            return None
        if j == 1:
            cur[at] = new
            acc[at] = old + new
            return None
        mean = (acc[at] + new) * (1.0 / INNER)
        diff = mean - first[at]
        first[at] = mean
        return jnp.sum(diff * diff, axis=0)

    def rows_under(edge, lo, size):
        return jnp.stack([
            jnp.broadcast_to(edge[t // ROWS, t % ROWS : t % ROWS + 1], (ROWS, Y)) for t in range(lo, lo + size)
        ])

    def gradient(arcs, near, halo, bounds):
        for hh_ in range(2):
            k_in = 2 - hh_
            edge = (halo[0, hh_] + halo[k_in, 1 - hh_]) + (up_y(halo[3, hh_]) + dn_y(halo[4, hh_]))
            tail = None
            for lo, size in reversed(chunks):
                at = pl.ds(lo, size)
                p0, p3, p4 = arcs[0, hh_, at], arcs[3, hh_, at], arcs[4, hh_, at]
                back = (p0 + arcs[k_in, 1 - hh_, at]) + (up_y(p3) + dn_y(p4))
                g = ((p0 + p3) + (p4 + bounds[hh_, at])) + (arcs[1, hh_, at] + arcs[2, hh_, at])
                g = g - (from_below(back, rows_under(edge, lo, size)) + near[hh_, at])
                for t in range(lo + size - 1, lo - 1, -1):
                    tail = g[t - lo] if tail is None else tail + g[t - lo]
                    tl[hh_, t] = tail

    in_all(2).wait_recv()
    for hh_ in range(2):
        k_in = 2 - hh_
        edge = fh[k_in, 1 - hh_]
        tail = None
        for lo, size in reversed(chunks):
            at = pl.ds(lo, size)
            g = landed(pg, hh_)[lo : lo + size] + (fa[1, hh_, at] + fa[2, hh_, at])
            g = g - (from_below(fa[k_in, 1 - hh_, at], rows_under(edge, lo, size)) + fn[hh_, at])
            for t in range(lo + size - 1, lo - 1, -1):
                tail = g[t - lo] if tail is None else tail + g[t - lo]
                tl[hh_, t] = tail
    loads[3].wait()
    in_all(3).wait_recv()
    for hh_ in range(2):
        uf[hh_] = landed(pu, hh_)
    in_all(7).wait_recv()
    got = capb[0]
    for p in range(1, NPD):
        got = got + capb[p]
    caps = as_rows(got)
    climit = as_rows(got, NP) * blocks_all
    cap_first = cap_sum = inv_tons = None

    def totals(row, s):
        line = as_lanes(row)
        if s > 0:
            return line
        tons = jnp.sum(jnp.sum(ton[0] + ton[1], axis=0, keepdims=True), axis=1, keepdims=True)
        return jnp.where(lanes1 == NP, tons, line)

    for s in range(STEPS):
        j = s % INNER
        last, final = j == INNER - 1, s == STEPS - 1
        u_src = uf if j == 0 else uc
        b_src = bf if j == 0 else bc
        p_src, n_src, h_src = (fa, fn, fh) if j == 0 else (ca, cn, ch)
        inv_w = 1.0 / w
        move_p = jnp.zeros((ROWS, Y), jnp.float32)
        move_d = jnp.zeros((ROWS, Y), jnp.float32)
        if j == 0:
            for hh_ in range(2):
                for t in range(NP):
                    tau = tb[hh_, t] * inv_w
                    tt[hh_, t] = tau * (ton[hh_] * inv_root)
                    tl[hh_, t] = u_src[hh_, t] - tau * (tl[hh_, t] - pr[hh_, t])
        row = jnp.zeros((NP, Y), jnp.float32)
        heads = [None, None]
        for t in range(NP):
            mined = None
            for hh_ in range(2):
                old = u_src[hh_, t]
                new = jnp.maximum(tl[hh_, t] - tt[hh_, t] * caps[t : t + 1, :], 0.0)
                ext = 2.0 * new - old
                if j == 0:
                    uc[hh_, t] = new
                elif j == 1:
                    uc[hh_, t] = new
                    us[hh_, t] = old + new
                else:
                    mean = (us[hh_, t] + new) * (1.0 / INNER)
                    diff = mean - uf[hh_, t]
                    uf[hh_, t] = mean
                    move_p = move_p + diff * diff
                heads[hh_] = ext if t == 0 else heads[hh_] + ext
                xs[s, hh_, t] = heads[hh_]
                hs[s, hh_, t // ROWS, pl.ds(t % ROWS, 1)] = heads[hh_][ROWS - 1 : ROWS]
                if not final:
                    ls[s, hh_, t // ROWS, pl.ds(t % ROWS, 1)] = heads[hh_][0:1]
                part = ton[hh_] * ext
                mined = part if mined is None else mined + part
            row = jnp.where(rows == t, jnp.sum(mined, axis=0, keepdims=True), row)
        if not last:
            reduce_start(s, totals(row, s))
        if final:
            out_start(0)
        pl.when(up[1])(z_copy(1, s).start)
        for d in range(2):
            pl.when(has[d])(x_copy(d, s).start)
        for d in range(2):
            pl.when(has[d] & up[1])(d_copy(d, 1, s).start)
        if not final:
            pl.when(up[0])(z_copy(0, s).start)
            for d in range(2):
                pl.when(has[d] & up[0])(d_copy(d, 0, s).start)
        if s == 0:
            send_all(6)
            loads[2].wait()
            in_all(4).wait_recv()
            for hh_ in range(2):
                bf[hh_] = landed(pb, hh_)
        if last:
            reduce_start(s, totals(row, s))

        def arc(k, hh_, at, diff, move):
            old = p_src[k, hh_, at]
            new = jnp.maximum(old + rp[at] * diff, 0.0) * act[k, hh_][None]
            moved = settle(fa, ca, sa, (k, hh_, at), j, new, old)
            return move if moved is None else move + moved

        for hh_ in range(2):
            for lo, size in chunks:
                at = pl.ds(lo, size)
                old = b_src[hh_, at]
                new = jnp.maximum(old + 2.0 * rp[at] * (xs[s, hh_, at] - 1.0), 0.0)
                if j == 0:
                    bc[hh_, at] = new
                elif j == 1:
                    bc[hh_, at] = new
                    bs[hh_, at] = old + new
                else:
                    mean = (bs[hh_, at] + new) * (1.0 / INNER)
                    diff = mean - bf[hh_, at]
                    bf[hh_, at] = mean
                    move_d = move_d + jnp.sum(diff * diff, axis=0)
        if final:
            out_start(1)
        wait_recv(up[0], z_copy(1, s))

        def own_arcs(move):
            for lo, size in chunks:
                at = pl.ds(lo, size)
                for hh_ in range(2):
                    c = xs[s, hh_, at]
                    cz = from_above(c, lines(zh, lo, size, s, hh_))
                    move = arc(0, hh_, at, c - cz, move)
                    move = arc(3, hh_, at, c - dn_y(cz), move)
                    move = arc(4, hh_, at, c - up_y(cz), move)
            return move

        if s > 0:
            move_d = own_arcs(move_d)
        for lo, size in chunks:
            at = pl.ds(lo, size)
            c = [xs[s, hh_, at] for hh_ in range(2)]
            cz = [from_above(c[hh_], lines(zh, lo, size, s, hh_)) for hh_ in range(2)]
            move_d = arc(1, 0, at, c[0] - cz[1], move_d)
            move_d = arc(2, 1, at, c[1] - cz[0], move_d)
        if final:
            out_start(2)
        for d in range(2):
            wait_recv(has[d], x_copy(1 - d, s))
            wait_recv(has[d] & up[0], d_copy(1 - d, 1, s))
        for lo, size in chunks:
            at = pl.ds(lo, size)
            for d in range(2):
                cz = from_above(xr[s, d, at], lines(dh, lo, size, s, d))
                move_d = arc(2 - d, d, at, xs[s, d, at] - cz, move_d)
        if last:
            cyc = s // INNER
            mp = jnp.sum(move_p, axis=0, keepdims=True)
            md = jnp.sum(move_d, axis=0, keepdims=True)
            reduce_start(STEPS + cyc, as_lanes(jnp.where(rows == 0, mp, jnp.where(rows == 1, md, 0.0))))
        if final:
            out_start(3)
            out_start(4)
        else:
            wait_recv(up[1], z_copy(0, s))
            for d in range(2):
                wait_recv(has[d] & up[1], d_copy(1 - d, 0, s))
            for lo, size in chunks:
                at = pl.ds(lo, size)
                for d in range(2):
                    old = n_src[d, at]
                    diff = from_below(xr[s, d, at], lines(dl, lo, size, s, d)) - xs[s, d, at]
                    new = jnp.maximum(old + rp[at] * diff, 0.0) * nact[d][None]
                    settle(fn, cn, sn, (d, at), j, new, old)
            if s == 0:
                in_all(5).wait_recv()
                in_all(6).wait_recv()
                mask_arcs((0, 3, 4))
                mask_halo([(k, hh_) for k in (0, 3, 4) for hh_ in range(2)])
                own_arcs(move_d)
            for hh_ in range(2):
                c, cz = zl[s, hh_], hs[s, hh_]
                for k in (0, 3, 4, 1 + hh_):
                    ahead = (cz, hs[s, 1 - hh_], hs[s, 1 - hh_], dn_y(cz), up_y(cz))[k]
                    old = h_src[k, hh_]
                    new = jnp.maximum(old + rh[...] * (c - ahead), 0.0) * hact[k, hh_][None]
                    settle(fh, ch, sh, (k, hh_), j, new, old)
            if last:
                gradient(fa, fn, fh, bf)
            else:
                gradient(ca, cn, ch, bc)
                for hh_ in range(2):
                    for t in range(NP):
                        tau = tb[hh_, t] * inv_w
                        tl[hh_, t] = uc[hh_, t] - tau * (tl[hh_, t] - pr[hh_, t])
        got = reduce_done(s)
        if s == 0:
            inv_tons = 1.0 / jnp.sum(jnp.where(lanes1 == NP, got, 0.0), axis=1, keepdims=True)
        row_total = as_rows(got)
        new_caps = jnp.maximum(caps + w * ((row_total - climit) * inv_tons), 0.0)
        if j == 0:
            cap_first = caps
            cap_sum = new_caps
        else:
            cap_sum = cap_sum + new_caps
        caps = new_caps
        if last:
            caps = cap_sum * (1.0 / INNER)
            cap_move = jnp.sum((caps - cap_first) ** 2, axis=0, keepdims=True)
            if final:
                for t in range(T):
                    few_out[t] = jnp.sum(jnp.where(rows == pe * T + t, caps, 0.0), axis=0)
            tot = as_rows(reduce_done(STEPS + cyc))
            moved = jnp.sqrt((tot[1:2, :] + cap_move + EPS) / (tot[0:1, :] + EPS))
            w = jnp.sqrt(w * moved)
            if not final:
                set_rates(w)
    few_out[T] = w[0]
    u_out[0, :, rows_of(q)] = uf[h, mine]
    bound_out[0, :, rows_of(q)] = bf[h, mine]
    for k in range(5):
        prec_out[k, 0, :, rows_of(q)] = fa[k, h, mine]
    for what in range(5):
        out_all(what).wait_recv()
    for what in range(5):
        out_all(what).wait_send()
    for what in range(8):
        in_all(what).wait_send()
    rest = rb.at[:, pl.ds(0, ND - 1)]
    remote(rest, rest, r_s.at[0], r_r.at[0], other(0, 1)).wait_send()

    def wait_sent(cond, ref, sem):
        pl.when(cond)(lambda: remote(ref, ref, sem, sem, other(0, 1)).wait_send())

    rows_down, rows_up = ls.at[pl.ds(0, STEPS - 1)], hs
    wait_sent(up[0], rows_down, z_s.at[0])
    wait_sent(up[1], rows_up, z_s.at[1])
    for d in range(2):
        wait_sent(has[d], xs.at[:, d], x_s.at[d])
        wait_sent(has[d] & up[0], ls.at[pl.ds(0, STEPS - 1), d], d_s.at[d, 0])
        wait_sent(has[d] & up[1], hs.at[:, d], d_s.at[d, 1])
    for cond, copy in sends:
        if cond is None:
            copy.wait_send()
        else:
            pl.when(cond)(lambda copy=copy: copy.wait_send())


def store_kernel(u_ref, prec_ref, bound_ref, few_ref, u_out, prec_out, bound_out, cap_out, w_out, sem):
    stores = (
        pltpu.make_async_copy(prec_ref, prec_out, sem.at[0]),
        pltpu.make_async_copy(u_ref, u_out, sem.at[1]),
        pltpu.make_async_copy(bound_ref, bound_out, sem.at[2]),
    )
    for store in stores:
        store.start()
    T = cap_out.shape[0]
    for t in range(T):
        cap_out[t] = few_ref[t, 0]
    w_out[0] = few_ref[T, 0]
    for store in stores:
        store.wait()


def pair_call(NS, NPD, u, prec, bound, cap, capacity, bv, tc, dens, slope, om):
    _, T, Z, Y = u.shape
    f32 = jnp.float32
    NP, NQ, ND = NPD * T, 2 * NPD, NS * NPD
    NT = NP // ROWS
    vmem = pl.BlockSpec(memory_space=pltpu.VMEM)
    hbm = pl.BlockSpec(memory_space=pl.ANY)
    smem = pl.BlockSpec(memory_space=pltpu.SMEM)
    slots = STEPS + OUTER
    V = lambda *shape: pltpu.VMEM((*shape, Y), f32)
    unit = lambda *n: V(*n, NQ, T, ROWS)
    whole = lambda *n: V(*n, NP, ROWS)
    edge = lambda *n: V(*n, NT, ROWS)
    dma = pltpu.SemaphoreType.DMA
    ours = pl.pallas_call(
        functools.partial(pair_kernel, NS, NPD, T, Z, Y),
        out_shape=(
            pltpu.VMEM(u.shape, f32),
            pltpu.VMEM(prec.shape, f32),
            pltpu.VMEM(bound.shape, f32),
            pltpu.VMEM((T + 1, Y), f32),
        ),
        in_specs=[hbm] * 10,
        out_specs=(vmem, vmem, vmem, vmem),
        scratch_shapes=[
            pltpu.VMEM((1, Y), jnp.int32), pltpu.SMEM(cap.shape, f32), pltpu.SMEM(cap.shape, f32),
            pltpu.SMEM(dens.shape, f32), pltpu.SMEM(om.shape, f32), V(1), V(NQ, 1),
            V(5, T, Z), V(T, Z), V(T, Z), V(NQ, 5, T), unit(), unit(), unit(), unit(5), V(NQ, 5, T), V(2, NPD, T, ROWS), V(2, NPD, T),
            V(2, ROWS), pltpu.VMEM((2, ROWS, Y), jnp.int32), pltpu.VMEM((4, 1, Y), jnp.int32),
            whole(5, 2), whole(5, 2), whole(5, 2), whole(2), whole(2), whole(2),
            edge(5, 2), edge(5, 2), edge(5, 2), whole(2), whole(2), whole(2), whole(2), whole(2), whole(2),
            V(5, 2, ROWS), V(2, ROWS), V(5, 2, ROWS), V(2, ROWS), whole(2), whole(2), whole(2), whole(2),
            whole(), edge(),
            whole(STEPS, 2), whole(STEPS, 2), edge(STEPS, 2), edge(STEPS, 2), edge(STEPS, 2), edge(STEPS, 2),
            edge(STEPS, 2), edge(STEPS, 2), V(slots, 1), V(slots, ND, 1),
            pltpu.SemaphoreType.REGULAR((2,)), dma((12,)), dma((8,)), dma((8,)), dma((3,)), dma((3,)), dma((2,)), dma((2,)), dma((2, 2)), dma((2, 2)),
            dma((2,)), dma((2, 2)), dma((2,)), dma((2, 2)), dma((2, 2)), dma((2, 2, 2)), dma((1,)), dma((3,)),
            dma((5,)), dma((5,)),
        ],
        compiler_params=pltpu.CompilerParams(collective_id=1, has_side_effects=True),
    )(u, prec, bound, cap, capacity, bv, tc, dens, slope, om)
    return pl.pallas_call(
        store_kernel,
        out_shape=(
            jax.ShapeDtypeStruct(u.shape, f32),
            jax.ShapeDtypeStruct(prec.shape, f32),
            jax.ShapeDtypeStruct(bound.shape, f32),
            jax.ShapeDtypeStruct(cap.shape, f32),
            jax.ShapeDtypeStruct((1,), f32),
        ),
        in_specs=[vmem] * 4,
        out_specs=(hbm, hbm, hbm, smem, smem),
        scratch_shapes=[dma((3,))],
    )(*[pltpu.with_memory_space_constraint(x, pltpu.VMEM) for x in ours])


def solution(mesh):
    NS, NPD = mesh.shape["strip"], mesh.shape["period"]

    def per_device(u, prec, bound, cap, capacity, bv, tc, dens, slope, om):
        rows_here, T, Z, Y = u.shape
        assert rows_here == 1
        NP = NPD * T
        if NS % 2 == 0 and Z == 2 * NPD * ROWS and NP % ROWS == 0 and 2 * NP < Y:
            return pair_call(NS, NPD, u, prec, bound, cap, capacity, bv, tc, dens, slope, om)
        R = -(-T // 8) * 8
        f32 = jnp.float32
        vmem = pl.BlockSpec(memory_space=pltpu.VMEM)
        hbm = pl.BlockSpec(memory_space=pl.ANY)
        smem = pl.BlockSpec(memory_space=pltpu.SMEM)
        plane = lambda *n: pltpu.VMEM((*n, Z, Y), f32)
        dma = pltpu.SemaphoreType.DMA
        slots = 1 + STEPS + OUTER
        far = max(NPD - 1, 1)
        return pl.pallas_call(
            functools.partial(kernel, NS, NPD, T, Z, Y, R),
            out_shape=(
                pltpu.VMEM(u.shape, f32),
                pltpu.VMEM(prec.shape, f32),
                pltpu.VMEM(bound.shape, f32),
                jax.ShapeDtypeStruct(cap.shape, f32),
                jax.ShapeDtypeStruct((1,), f32),
            ),
            in_specs=[hbm, hbm, hbm, smem, smem, vmem, vmem, smem, vmem, smem],
            out_specs=(vmem, vmem, vmem, smem, smem),
            scratch_shapes=[
                plane(T), plane(T), plane(T), plane(T), plane(T), plane(T),
                plane(7, T), plane(7, T), plane(7, T), plane(7), plane(), plane(T), plane(T), plane(T), plane(),
                plane(STEPS, T), plane(2, STEPS, T), plane(STEPS), plane(STEPS, far),
                plane(STEPS), plane(STEPS, far),
                pltpu.VMEM((slots, 1, Y), f32), pltpu.VMEM((slots, NS, 1, Y), f32),
                pltpu.VMEM((OUTER, 1, Y), f32), pltpu.VMEM((OUTER, NPD, 1, Y), f32),
                pltpu.VMEM((2, 1, Y), jnp.int32),
                plane(5, T), plane(2), plane(2), dma((3,)),
                dma((2, 3)), dma((2, 3)), dma((2, 2, STEPS)), dma((2, 2, STEPS)),
                dma((STEPS, far)), dma((STEPS, far)), dma((STEPS, far)), dma((STEPS, far)),
                dma((slots, NS - 1)), dma((slots, NS - 1)), dma((OUTER, far)), dma((OUTER, far)),
            ],
            compiler_params=pltpu.CompilerParams(collective_id=0, has_side_effects=True),
        )(u, prec, bound, cap, capacity, bv, tc, dens, slope, om)

    in_specs = (
        P("strip", "period", None, None),
        P(None, "strip", "period", None, None),
        P("strip", "period", None, None),
        P("period"),
        P("period"),
        P("strip", None, None),
        P("strip", None, None),
        P(),
        P("strip", None),
        P(),
    )
    out_specs = (
        P("strip", "period", None, None),
        P(None, "strip", "period", None, None),
        P("strip", "period", None, None),
        P("period"),
        P(),
    )
    return jax.shard_map(
        per_device, mesh=mesh, in_specs=in_specs, out_specs=out_specs, check_vma=False
    )
```

```python
import functools
import math

import jax
import jax.numpy as jnp
from jax import lax
from jax.experimental import pallas as pl
from jax.experimental.pallas import tpu as pltpu
from jax.sharding import PartitionSpec as P

OUTER = 2
INNER = 3
STEPS = OUTER * INNER
RATE = math.log(1.1) / 12.0
EPS = 1e-06
SLOPE = 11.0
MESH = pl.DeviceIdType.MESH
ROWS = 8
CHUNK = 8


def kernel(
    NS, NPD, T, Z, Y, R,
    u_ref, prec_ref, bound_ref, cap_ref, capacity_ref, bv_ref, tc_ref, dens_ref, slope_ref, om_ref,
    u_out, prec_out, bound_out, cap_out, w_out,
    uf, uc, us, bf, bc, bs, fa, ca, sa, act, ton, tb, tl, cb, ex0,
    xs, xr, es, er, as_, ar, rs, rb, ps, pb, slr,
    praw, ti, to_sum, loc, ini_s, ini_r, xs_s, xs_r, e_s, e_r, a_s, a_r, r_s, r_r, p_s, p_r,
):
    me = lax.axis_index("strip")
    pe = lax.axis_index("period")
    total_rows = NS
    total_periods = NPD * T
    blocks_all = float(total_rows * Z * Y)
    root_blocks = math.sqrt(blocks_all)
    sends = []

    loads = (
        pltpu.make_async_copy(prec_ref.at[:, 0], praw, loc.at[0]),
        pltpu.make_async_copy(bound_ref.at[0], bf, loc.at[1]),
        pltpu.make_async_copy(u_ref.at[0], uf, loc.at[2]),
    )
    for load in loads:
        load.start()
    barrier = pltpu.get_barrier_semaphore()
    for k in range(1, NS):
        pl.semaphore_signal(barrier, inc=1, device_id={"strip": lax.rem(me + k, NS)}, device_id_type=MESH)
    for k in range(1, NPD):
        pl.semaphore_signal(barrier, inc=1, device_id={"period": lax.rem(pe + k, NPD)}, device_id_type=MESH)

    has = (me < NS - 1, me > 0)
    gets = (me > 0, me < NS - 1)
    to = (me + 1, me - 1)

    def remote(src, dst, ss, rr, dev):
        return pltpu.make_async_remote_copy(
            src_ref=src, dst_ref=dst, send_sem=ss, recv_sem=rr, device_id=dev, device_id_type=MESH
        )

    def ini_copy(d, what):
        if what == 2:
            return remote(to_sum.at[d], ti.at[d], ini_s.at[d, 2], ini_r.at[d, 2], {"strip": to[d]})
        if what == 0:
            rest = pl.ds(1, T - 1)
            return remote(praw.at[1 + d, rest], fa.at[5 + d, rest], ini_s.at[d, 0], ini_r.at[d, 0], {"strip": to[d]})
        return remote(slope_ref, slr.at[d], ini_s.at[d, 1], ini_r.at[d, 1], {"strip": to[d]})

    def x_copy(d, part, s):
        lo, size = (1, T - 1) if part == 0 else (0, 1)
        return remote(
            xs.at[s, pl.ds(lo, size)], xr.at[d, s, pl.ds(lo, size)],
            xs_s.at[d, part, s], xs_r.at[d, part, s], {"strip": to[d]},
        )

    def e_copy(k, s):
        return remote(es.at[s], er.at[s, k - 1], e_s.at[s, k - 1], e_r.at[s, k - 1], {"period": pe + k})

    def a_copy(k, s):
        return remote(as_.at[s], ar.at[s, k - 1], a_s.at[s, k - 1], a_r.at[s, k - 1], {"period": pe - k})

    def r_copy(k, slot):
        return remote(
            rs.at[slot], rb.at[slot, me], r_s.at[slot, k - 1], r_r.at[slot, k - 1],
            {"strip": lax.rem(me + k, NS)},
        )

    def p_copy(k, slot):
        return remote(
            ps.at[slot], pb.at[slot, pe], p_s.at[slot, k - 1], p_r.at[slot, k - 1],
            {"period": lax.rem(pe + k, NPD)},
        )

    def start(cond, copy):
        def go():
            copy.start()
        if cond is None:
            go()
        else:
            pl.when(cond)(go)
        sends.append((cond, copy))

    def wait_recv(cond, copy):
        if cond is None:
            copy.wait_recv()
        else:
            pl.when(cond)(lambda: copy.wait_recv())

    def reduce_start(slot, value):
        rs[slot] = value
        rb[slot, me] = value
        for k in range(1, NS):
            start(None, r_copy(k, slot))

    def reduce_done(slot):
        for k in range(1, NS):
            wait_recv(None, r_copy(k, slot))
        total = rb[slot, 0]
        for k in range(1, NS):
            total = total + rb[slot, k]
        return total

    loads[0].wait()
    for d in range(2):
        total = praw[1 + d, 0]
        for t in range(1, T):
            total = total + praw[1 + d, t]
        to_sum[d] = total
    pl.semaphore_wait(barrier, NS + NPD - 2)
    for d in range(2):
        start(has[d], ini_copy(d, 1))
        start(has[d], ini_copy(d, 2))
    for d in range(2):
        start(has[d], ini_copy(d, 0))

    rows = lax.broadcasted_iota(jnp.int32, (R, Y), 0)
    lanes = lax.broadcasted_iota(jnp.int32, (R, Y), 1)

    def as_lanes(value):
        sums = jnp.sum(value, axis=1, keepdims=True)
        return jnp.sum(jnp.where(lanes == rows, sums, 0.0), axis=0, keepdims=True)

    def as_rows(line):
        return jnp.sum(jnp.where(lanes == rows, line, 0.0), axis=1, keepdims=True)

    def fold(v):
        return jnp.sum(v.reshape(Z // 8, 8, Y), axis=0)

    cls = tc_ref[0]
    tons = jnp.zeros((Z, Y), jnp.float32)
    for c in range(dens_ref.shape[0]):
        tons = jnp.where(cls == c, (1.0 + c) * dens_ref[c], tons)
    ton[...] = tons
    part = jnp.sum(tons, axis=0, keepdims=True)
    reduce_start(0, part)

    z_ids = lax.broadcasted_iota(jnp.int32, (Z, Y), 0)
    y_ids = lax.broadcasted_iota(jnp.int32, (Z, Y), 1)

    def mask_of(codes, k, inside):
        ok = z_ids >= 1
        if k > 0:
            ok = ok & (jnp.broadcast_to((codes >> (k - 1)) & 1, (Z, Y)) == 1)
        if k == 3:
            ok = ok & (y_ids < Y - 1)
        if k == 4:
            ok = ok & (y_ids >= 1)
        if inside is not None:
            ok = ok & (jnp.full((Z, Y), inside.astype(jnp.int32)) == 1)
        return ok.astype(jnp.float32)

    own = slope_ref[...]
    act[0] = mask_of(own, 0, None)
    act[1] = mask_of(own, 1, me < NS - 1)
    act[2] = mask_of(own, 2, me > 0)
    act[3] = mask_of(own, 3, None)
    act[4] = mask_of(own, 4, None)

    period = [(pe * T + t).astype(jnp.float32) for t in range(T)]
    pid = [jnp.full((1, Y), period[t]) for t in range(T)]
    disc = [jnp.exp(-RATE * pid[t]) for t in range(T)]
    tonr = ton[...] * (1.0 / root_blocks)
    for load in loads[1:]:
        load.wait()
    for t in range(T):
        tb[t] = 1.0 / (SLOPE * (total_periods - pid[t]) + tonr)
        for k in range(5):
            fa[k, t] = praw[k, t] * act[k]

    caps = jnp.zeros((R, Y), jnp.float32)
    climit = jnp.zeros((R, Y), jnp.float32)
    for t in range(T):
        caps = jnp.where(rows == t, cap_ref[t], caps)
        climit = jnp.where(rows == t, capacity_ref[t] * blocks_all, climit)
    w = jnp.full((1, Y), om_ref[0])

    for d in range(2):
        @pl.when(jnp.logical_not(gets[d]))
        def _():
            act[5 + d] = jnp.zeros((Z, Y), jnp.float32)
            ti[d] = jnp.zeros((Z, Y), jnp.float32)
            fa[5 + d] = jnp.zeros((T, Z, Y), jnp.float32)
            for s in range(STEPS):
                xr[d, s] = jnp.zeros((T, Z, Y), jnp.float32)

    def up_y(v):
        return pltpu.roll(v, 1, 1)

    def dn_y(v):
        return pltpu.roll(v, Y - 1, 1)

    def up_z(v):
        return pltpu.roll(v, 1, 0)

    def dn_z(v):
        return pltpu.roll(v, Z - 1, 0)

    def settle(first, cur, acc, at, j, new, old):
        if j == 0:
            cur[at] = new
            return new, None
        if j == 1:
            cur[at] = new
            acc[at] = old + new
            return new, None
        mean = (acc[at] + new) * (1.0 / INNER)
        diff = mean - first[at]
        first[at] = mean
        return mean, fold(diff * diff)

    def gradient_own(arcs, bounds):
        for t in range(T):
            p0, p3, p4 = arcs[0, t], arcs[3, t], arcs[4, t]
            back = p0 + (up_y(p3) + dn_y(p4))
            tl[t] = ((p0 + p3) + (p4 + bounds[t])) - dn_z(back)

    def gradient(s, arcs):
        tail = None
        for t in range(T - 1, -1, -1):
            g = (tl[t] + (arcs[1, t] + arcs[2, t])) - dn_z(arcs[5, t] + arcs[6, t])
            tail = g if tail is None else tail + g
            tl[t] = tail
        as_[s] = tail
        for k in range(1, NPD):
            start(pe >= k, a_copy(k, s))

    tail = None
    for t in range(T - 1, -1, -1):
        p = [fa[k, t] for k in range(5)]
        g = (((p[0] + p[1]) + (p[2] + p[3])) + p[4]) + bf[t]
        g = g - dn_z(p[0] + (up_y(p[3]) + dn_y(p[4])))
        tail = g if tail is None else tail + g
        tl[t] = tail
    for d in range(2):
        wait_recv(gets[d], ini_copy(d, 1))
        wait_recv(gets[d], ini_copy(d, 2))

        @pl.when(gets[d])
        def _():
            act[5 + d] = mask_of(slr[d], 1 + d, None)
    as_[0] = tl[0] - dn_z(ti[0] * act[5] + ti[1] * act[6])
    for k in range(1, NPD):
        start(pe >= k, a_copy(k, 0))
    for d in range(2):
        wait_recv(gets[d], ini_copy(d, 0))
        rest = ti[d]
        for t in range(1, T):
            plane = fa[5 + d, t]
            rest = rest - plane
            fa[5 + d, t] = plane * act[5 + d]
        fa[5 + d, 0] = rest * act[5 + d]
    tail = None
    for t in range(T - 1, -1, -1):
        back = fa[5, t] + fa[6, t]
        tail = back if tail is None else tail + back
        tl[t] = tl[t] - dn_z(tail)
    tons_all = jnp.sum(reduce_done(0), axis=1, keepdims=True)
    inv_tons = 1.0 / tons_all
    cap_first = cap_sum = None

    for s in range(STEPS):
        j = s % INNER
        u_src = uf if j == 0 else uc
        b_src = bf if j == 0 else bc
        p_src = fa if j == 0 else ca
        inv_w = 1.0 / w
        move_p = jnp.zeros((8, Y), jnp.float32)
        move_d = jnp.zeros((8, Y), jnp.float32)
        for k in range(1, NPD):
            @pl.when(pe + k < NPD)
            def _():
                a_copy(k, s).wait_recv()
                for t in range(T):
                    tl[t] = tl[t] + ar[s, k - 1]
        head = None
        row = jnp.zeros((R, Y), jnp.float32)
        for t in range(T):
            old = u_src[t]
            grad = tl[t] + (ton[...] * (1.0 / root_blocks)) * caps[t : t + 1, :]
            new = jnp.maximum(old - (tb[t] * inv_w) * (grad - bv_ref[0] * disc[t]), 0.0)
            ext = 2.0 * new - old
            _, moved = settle(uf, uc, us, t, j, new, old)
            if moved is not None:
                move_p = move_p + moved
            if t == 0:
                ex0[...] = ext
            else:
                xs[s, t] = ext
            head = ext if head is None else head + ext
            row = jnp.where(rows == t, jnp.sum(ton[...] * ext, axis=0, keepdims=True), row)
        es[s] = head
        for k in range(1, NPD):
            start(pe + k < NPD, e_copy(k, s))
        for d in range(2):
            start(has[d], x_copy(d, 0, s))
        for k in range(1, NPD):
            @pl.when(pe >= k)
            def _():
                e_copy(k, s).wait_recv()
                ex0[...] = ex0[...] + er[s, k - 1]
        xs[s, 0] = ex0[...]
        for d in range(2):
            start(has[d], x_copy(d, 1, s))
        reduce_start(1 + s, as_lanes(row))
        total = None
        for t in range(T):
            total = xs[s, t] if t == 0 else total + xs[s, t]
            cb[t] = total
        rate_b = [w / (pid[t] + 1.0) for t in range(T)]
        rate_p = [w / (2.0 * (pid[t] + 1.0)) for t in range(T)]

        def arc(k, t, diff, move):
            old = p_src[k, t]
            new = jnp.maximum(old + rate_p[t] * diff, 0.0) * act[k]
            _, moved = settle(fa, ca, sa, (k, t), j, new, old)
            if moved is not None and k < 5:
                move = move + moved
            return move

        for t in range(T):
            c = cb[t]
            old = b_src[t]
            new = jnp.maximum(old + rate_b[t] * (c - 1.0), 0.0)
            _, moved = settle(bf, bc, bs, t, j, new, old)
            if moved is not None:
                move_d = move_d + moved
            cz = up_z(c)
            move_d = arc(0, t, c - cz, move_d)
            move_d = arc(3, t, c - dn_y(cz), move_d)
            move_d = arc(4, t, c - up_y(cz), move_d)
        last = j == INNER - 1
        if s < STEPS - 1:
            gradient_own(fa if last else ca, bf if last else bc)
        for part in range(2):
            for d in range(2):
                wait_recv(gets[d], x_copy(d, part, s))
        total_m = total_p = None
        for t in range(T):
            total_m = xr[0, s, t] if t == 0 else total_m + xr[0, s, t]
            total_p = xr[1, s, t] if t == 0 else total_p + xr[1, s, t]
            c = cb[t]
            cz = up_z(c)
            move_d = arc(1, t, c - up_z(total_p), move_d)
            move_d = arc(2, t, c - up_z(total_m), move_d)
            if s < STEPS - 1:
                arc(5, t, total_m - cz, None)
                arc(6, t, total_p - cz, None)
        if s < STEPS - 1:
            gradient(s + 1, fa if last else ca)
        if last:
            cyc = s // INNER
            mp = jnp.sum(move_p, axis=0, keepdims=True)
            md = jnp.sum(move_d, axis=0, keepdims=True)
            reduce_start(1 + STEPS + cyc, as_lanes(jnp.where(rows == 0, mp, jnp.where(rows == 1, md, 0.0))))
        row_total = as_rows(reduce_done(1 + s))
        new_caps = jnp.maximum(caps + w * ((row_total - climit) * inv_tons), 0.0)
        new_caps = jnp.where(rows < T, new_caps, 0.0)
        if j == 0:
            cap_first = caps
            cap_sum = new_caps
        else:
            cap_sum = cap_sum + new_caps
        caps = new_caps
        if last:
            caps = cap_sum * (1.0 / INNER)
            cap_move = jnp.sum((caps - cap_first) ** 2, axis=0, keepdims=True)
            got = reduce_done(1 + STEPS + cyc)
            msg = got + jnp.where(lanes[0:1] == 1, cap_move, 0.0)
            ps[cyc] = msg
            pb[cyc, pe] = msg
            for k in range(1, NPD):
                start(None, p_copy(k, cyc))
            if s == STEPS - 1:
                for t in range(T):
                    u_out[0, t] = uf[t]
                    bound_out[0, t] = bf[t]
                    for k in range(5):
                        prec_out[k, 0, t] = fa[k, t]
                    cap_out[t] = caps[t, 0]
            for k in range(1, NPD):
                wait_recv(None, p_copy(k, cyc))
            tot = pb[cyc, 0]
            for k in range(1, NPD):
                tot = tot + pb[cyc, k]
            tot = as_rows(tot)
            moved = jnp.sqrt((tot[1:2, :] + EPS) / (tot[0:1, :] + EPS))
            w = jnp.sqrt(w * moved)
    w_out[0] = w[0, 0]
    for cond, copy in sends:
        if cond is None:
            copy.wait_send()
        else:
            pl.when(cond)(lambda copy=copy: copy.wait_send())


def pair_kernel(
    NS, NPD, T, Z, Y,
    u_ref, prec_ref, bound_ref, cap_ref, capacity_ref, bv_ref, tc_ref, dens_ref, slope_ref, om_ref,
    u_out, prec_out, bound_out, few_out,
    slope_own, cap_own, capacity_own, dens_own, om_own, cap_line, capb, praw, braw, gh, hh, pu, pb, pg, pp, hpr, nraw, hnr, bvb, tcb, slr,
    fa, ca, sa, fn, cn, sn, fh, ch, sh, bf, bc, bs, uf, uc, us,
    act, nact, hact, ton, tb, pr, tl, tt, rp, rh,
    xs, xr, hs, ls, zh, zl, dh, dl, rs, rb,
    token, loc, ini_s, ini_r, sl_s, sl_r, sm_s, sm_r, re_s, re_r,
    x_s, x_r, z_s, z_r, d_s, d_r, r_s, r_r, o_s, o_r,
):
    me = lax.axis_index("strip")
    pe = lax.axis_index("period")
    pairs, NP, NQ = NS // 2, NPD * T, 2 * NPD
    NT = NP // ROWS
    ND = NS * NPD
    a, h = me // 2, lax.rem(me, 2)
    q = jnp.where(h == 0, pe, NQ - 1 - pe)
    blocks_all = float(NS * Z * Y)
    inv_root = 1.0 / math.sqrt(blocks_all)
    sends = []

    def rows_of(block):
        return pl.ds(pl.multiple_of(ROWS * block, ROWS), ROWS)

    def block_of(hh_, pp_):
        return jnp.where(hh_ == 0, pp_, NQ - 1 - pp_)

    def device_at(pair, block):
        first = block < NPD
        return {
            "strip": 2 * pair + jnp.where(first, 0, 1),
            "period": jnp.where(first, block, NQ - 1 - block),
        }

    def remote(src, dst, ss, rr, dev):
        return pltpu.make_async_remote_copy(
            src_ref=src, dst_ref=dst, send_sem=ss, recv_sem=rr, device_id=dev, device_id_type=MESH
        )

    def start(cond, copy):
        if cond is None:
            copy.start()
        else:
            pl.when(cond)(lambda: copy.start())
        sends.append((cond, copy))

    def wait_recv(cond, copy):
        if cond is None:
            copy.wait_recv()
        else:
            pl.when(cond)(lambda: copy.wait_recv())

    mine = pl.ds(pe * T, T)
    unit = h * NPD + pe
    peers = pl.ds(0, NQ - 1)
    loads = (
        pltpu.make_async_copy(prec_ref.at[:, 0], praw, loc.at[0]),
        pltpu.make_async_copy(prec_ref.at[:, 0, :, rows_of(q)], pp.at[:, unit], loc.at[1]),
        pltpu.make_async_copy(bound_ref.at[0, :, rows_of(q)], pb.at[unit], loc.at[2]),
        pltpu.make_async_copy(u_ref.at[0, :, rows_of(q)], pu.at[unit], loc.at[3]),
        pltpu.make_async_copy(bound_ref.at[0], braw, loc.at[4]),
        pltpu.make_async_copy(slope_ref, slope_own, loc.at[5]),
        pltpu.make_async_copy(cap_ref, cap_own, loc.at[6]),
        pltpu.make_async_copy(capacity_ref, capacity_own, loc.at[7]),
        pltpu.make_async_copy(dens_ref, dens_own, loc.at[8]),
        pltpu.make_async_copy(om_ref, om_own, loc.at[9]),
        pltpu.make_async_copy(bv_ref.at[0, rows_of(q)], bvb.at[h], loc.at[10]),
        pltpu.make_async_copy(tc_ref.at[0, rows_of(q)], tcb.at[h], loc.at[11]),
    )
    for load in loads:
        load.start()
    barrier = pltpu.get_barrier_semaphore()
    others = [divmod(k, NPD) for k in range(1, ND)]
    others.sort(key=lambda o: -abs(o[0] - NS // 2) if o[0] else NS)

    def other(ks, kp):
        return {"strip": lax.rem(me + ks, NS), "period": lax.rem(pe + kp, NPD)}

    mates = [divmod(k, NPD) for k in range(1, NQ)]

    def mate(i):
        kh, kp = mates[i]
        return lax.rem(h + kh, 2), lax.rem(pe + kp, NPD)

    has = (a > 0, a < pairs - 1)
    up = (q > 0, q < NQ - 1)
    beside = [device_at(a - 1, q), device_at(a + 1, q)]
    for i in range(NQ - 1):
        th, tp = mate(i)
        pl.semaphore_signal(barrier, inc=1, device_id={"strip": 2 * a + th, "period": tp}, device_id_type=MESH)
    column = [device_at(lax.rem(a + k, pairs), q) for k in range(1, pairs)]
    for there in column:
        pl.semaphore_signal(barrier, inc=1, device_id=there, device_id_type=MESH)

    def in_ends(what, rows, block, at):
        if what == 1:
            return hh.at[block], hpr.at[at]
        if what == 2:
            return gh.at[:, rows], pg.at[at]
        if what == 7:
            return cap_line, capb.at[at]
        if what == 3:
            return u_ref.at[0, :, rows], pu.at[at]
        if what == 4:
            return bound_ref.at[0, :, rows], pb.at[at]
        arcs = {0: pl.ds(1, 2), 5: 0, 6: pl.ds(3, 2)}[what]
        return prec_ref.at[arcs, 0, :, rows], pp.at[arcs, at]

    def in_copy(i, what):
        th, tp = mate(i)
        block = block_of(th, tp)
        src, dst = in_ends(what, rows_of(block), block, unit)
        return remote(src, dst, ini_s.at[what], ini_r.at[what], {"strip": 2 * a + th, "period": tp})

    def in_all(what):
        dst = in_ends(what, rows_of(0), 0, peers)[1]
        return remote(dst, dst, ini_s.at[what], ini_r.at[what], other(0, 1))

    def partner_copy(what):
        rows = rows_of(block_of(1 - h, pe))
        dev = {"strip": 2 * a + 1 - h, "period": pe}
        if what == 0:
            return remote(tc_ref.at[0, rows], tcb.at[h], sm_s.at[0], sm_r.at[0], dev)
        return remote(bv_ref.at[0, rows], bvb.at[h], sm_s.at[1], sm_r.at[1], dev)

    def slope_copy(what):
        if what == 2:
            return remote(slope_ref, slr.at[1 + h], sl_s.at[2], sl_r.at[2], {"strip": 2 * a + 1 - h, "period": pe})
        return remote(slr.at[1 + what], slr.at[3 - 3 * what], sl_s.at[what], sl_r.at[1 - what], beside[what])

    def relay_copy(d, what):
        dev = beside[d]
        k, hs_ = (2, 0) if d == 0 else (1, 1)
        ss, rr = re_s.at[d, what], re_r.at[d, what]
        if what == 0:
            return remote(pp.at[k, pl.ds(hs_ * NPD, NPD)], nraw.at[1 - d], ss, rr, dev)
        return remote(hpr.at[pl.ds(hs_ * NPD, NPD), k], hnr.at[1 - d], ss, rr, dev)

    def reduce_sem(slot):
        return r_r.at[slot % 2 if slot < STEPS else 2]

    def reduce_start(slot, value):
        rs[slot] = value
        rb[slot, me * NPD + pe] = value
        for ks, kp in others:
            remote(
                rs.at[slot], rb.at[slot, me * NPD + pe], r_s.at[0], reduce_sem(slot), other(ks, kp)
            ).start()

    def reduce_done(slot):
        rest = rb.at[slot, pl.ds(0, ND - 1)]
        remote(rest, rest, r_s.at[0], reduce_sem(slot), other(0, 1)).wait_recv()
        parts = [rb[slot, i] for i in range(ND)]
        while len(parts) > 1:
            parts = [parts[i] + parts[i + 1] if i + 1 < len(parts) else parts[i] for i in range(0, len(parts), 2)]
        return parts[0]

    def x_copy(d, s):
        dev = beside[d]
        return remote(xs.at[s, d], xr.at[s, 1 - d], x_s.at[d], x_r.at[s % 2, 1 - d], dev)

    def z_copy(d, s):
        if d == 0:
            return remote(ls.at[s], zl.at[s], z_s.at[0], z_r.at[s % 2, 0], device_at(a, q - 1))
        return remote(hs.at[s], zh.at[s], z_s.at[1], z_r.at[s % 2, 1], device_at(a, q + 1))

    def d_copy(d, e, s):
        dev = device_at(a - 1 if d == 0 else a + 1, q - 1 if e == 0 else q + 1)
        src, dst = (ls, dl) if e == 0 else (hs, dh)
        return remote(src.at[s, d], dst.at[s, 1 - d], d_s.at[d, e], d_r.at[s % 2, 1 - d, e], dev)

    def out_ends(what, th, part, rows):
        if what == 0:
            return uf.at[th, part], u_out.at[0, :, rows]
        if what == 1:
            return bf.at[th, part], bound_out.at[0, :, rows]
        arcs = (0, pl.ds(3, 2), pl.ds(1, 2))[what - 2]
        return fa.at[arcs, th, part], prec_out.at[arcs, 0, :, rows]

    def out_start(what):
        for i in range(NQ - 1):
            th, tp = mate(i)
            src, dst = out_ends(what, th, pl.ds(tp * T, T), rows_of(q))
            remote(src, dst, o_s.at[what], o_r.at[what], {"strip": 2 * a + th, "period": tp}).start()

    def out_all(what):
        dst = out_ends(what, 0, mine, pl.ds(0, ROWS * (NQ - 1)))[1]
        return remote(dst, dst, o_s.at[what], o_r.at[what], other(0, 1))

    lanes1 = lax.broadcasted_iota(jnp.int32, (1, Y), 1)
    rows = lax.broadcasted_iota(jnp.int32, (NP, Y), 0)
    lanes = lax.broadcasted_iota(jnp.int32, (NP, Y), 1)

    def tons_of(cls):
        tons = jnp.zeros(cls.shape, jnp.float32)
        for c in range(dens_own.shape[0]):
            tons = jnp.where(cls == c, (1.0 + c) * dens_own[c], tons)
        return tons

    def as_lanes(value):
        sums = jnp.sum(value, axis=1, keepdims=True)
        return jnp.sum(jnp.where(lanes == rows, sums, 0.0), axis=0, keepdims=True)

    def as_rows(line, at=0):
        return jnp.broadcast_to(jnp.sum(jnp.where(lanes == rows + at, line, 0.0), axis=1, keepdims=True), (NP, Y))

    def roll(v, by, axis):
        return pltpu.roll(v, by % v.shape[axis], axis)

    def up_y(v):
        return roll(v, 1, v.ndim - 1)

    def dn_y(v):
        return roll(v, -1, v.ndim - 1)

    def mask_of(code, k, depth, inside):
        ok = (depth >= 1) & (depth < Z)
        y_ids = lax.broadcasted_iota(jnp.int32, depth.shape, 1)
        if k > 0:
            ok = ok & (jnp.broadcast_to((code >> (k - 1)) & 1, depth.shape) == 1)
        if k == 3:
            ok = ok & (y_ids < Y - 1)
        if k == 4:
            ok = ok & (y_ids >= 1)
        if inside is not None:
            ok = ok & (jnp.full(depth.shape, inside.astype(jnp.int32)) == 1)
        return ok.astype(jnp.float32)

    def send_all(*kinds):
        for what in kinds:
            for i in range(NQ - 1):
                in_copy(i, what).start()

    pl.semaphore_wait(barrier, NQ - 1 + pairs - 1)
    send_all(0)
    for there in column:
        pl.semaphore_signal(token.at[0], inc=1, device_id=there, device_id_type=MESH)
    start(None, slope_copy(2))
    start(None, partner_copy(0))
    start(None, partner_copy(1))
    send_all(3)
    for load in loads[6:10]:
        load.wait()
    line = jnp.zeros((1, Y), jnp.float32)
    for t in range(T):
        line = jnp.where(lanes1 == pe * T + t, cap_own[t], line)
        line = jnp.where(lanes1 == NP + pe * T + t, capacity_own[t], line)
    cap_line[...] = line
    capb[unit] = line
    loads[0].wait()
    for b in range(NQ):
        if b + 1 < NQ:
            for k in range(5):
                for t in range(T):
                    hh[b, k, pl.ds(t, 1)] = praw[k, t, pl.ds(ROWS * (b + 1), 1)]
        else:
            hh[b] = jnp.zeros((5, T, Y), jnp.float32)
    hpr[unit] = hh[q]
    send_all(1, 7)
    z_ids = lax.broadcasted_iota(jnp.int32, (ROWS, Y), 0)
    low = z_ids == ROWS - 1
    depth = lax.broadcasted_iota(jnp.int32, (Z, Y), 0)
    loads[5].wait()
    home = {k: mask_of(slope_own[...], k, depth, None) for k in (0, 3, 4)}
    loads[4].wait()
    for t in range(T):
        p0, p3, p4 = (praw[k, t] * home[k] for k in (0, 3, 4))
        gh[t] = ((p0 + p3) + (p4 + braw[t])) - roll(p0 + (up_y(p3) + dn_y(p4)), -1, 0)
    pg[unit] = gh[:, rows_of(q)]
    send_all(2, 4, 5)
    slr[1 + h] = slope_own[...]
    for d in range(2):
        @pl.when(jnp.logical_not(has[d]))
        def _():
            for s in range(STEPS):
                xr[s, d] = jnp.zeros((NP, ROWS, Y), jnp.float32)
            nraw[d] = jnp.zeros((NPD, T, ROWS, Y), jnp.float32)
            hnr[d] = jnp.zeros((NPD, T, Y), jnp.float32)
            slr[3 * d] = jnp.zeros((1, Y), jnp.int32)
        for e in range(2):
            buf = (dh, dl)[e]

            @pl.when(jnp.logical_not(has[d] & up[e]))
            def _():
                for s in range(STEPS):
                    buf[s, d] = jnp.zeros((NT, ROWS, Y), jnp.float32)
    for e in range(2):
        buf = (zh, zl)[e]

        @pl.when(jnp.logical_not(up[e]))
        def _():
            for s in range(STEPS):
                buf[s] = jnp.zeros((2, NT, ROWS, Y), jnp.float32)

    wait_recv(None, slope_copy(2))
    for d in range(2):
        start(has[d], slope_copy(d))
    here, below = z_ids + ROWS * q, jnp.full((ROWS, Y), ROWS * (q + 1))
    for hh_ in range(2):
        code = slr[1 + hh_]
        for k in range(5):
            inside = None
            if k == 1 and hh_ == 1:
                inside = has[1]
            if k == 2 and hh_ == 0:
                inside = has[0]
            act[k, hh_] = mask_of(code, k, here, inside)
            hact[k, hh_] = mask_of(code, k, below, inside)
    for d in range(2):
        wait_recv(has[d], slope_copy(1 - d))
        nact[d] = mask_of(slr[3 * d], 1 + d, here + 1, has[d])

    wait_recv(None, partner_copy(0))
    wait_recv(None, partner_copy(1))
    loads[10].wait()
    loads[11].wait()
    for hh_ in range(2):
        tons = tons_of(tcb[hh_])
        ton[hh_] = tons
        for t in range(NP):
            tb[hh_, t] = 1.0 / (SLOPE * (NP - t) + tons * inv_root)
            pr[hh_, t] = bvb[hh_] * math.exp(-RATE * t)

    t_plane = lax.broadcasted_iota(jnp.int32, (NP, ROWS, Y), 0).astype(jnp.float32)
    t_rows = (
        lax.broadcasted_iota(jnp.int32, (NT, ROWS, Y), 0) * ROWS + lax.broadcasted_iota(jnp.int32, (NT, ROWS, Y), 1)
    ).astype(jnp.float32)

    w = jnp.full((1, Y), om_own[0])

    def set_rates(w):
        rp[...] = w[None] / (2.0 * (t_plane + 1.0))
        rh[...] = w[None] / (2.0 * (t_rows + 1.0))

    set_rates(w)

    loads[1].wait()
    in_all(0).wait_recv()
    for d in range(2):
        start(has[d], relay_copy(d, 0))
    in_all(1).wait_recv()
    for d in range(2):
        start(has[d], relay_copy(d, 1))

    chunks = [(lo, min(CHUNK, NP - lo)) for lo in range(0, NP, CHUNK)]

    def lines(ref, lo, size, *at):
        picked = [ref[(*at, t // ROWS, pl.ds(t % ROWS, 1))] for t in range(lo, lo + size)]
        return jnp.stack([jnp.broadcast_to(p, (ROWS, Y)) for p in picked])

    def from_above(v, line):
        return jnp.where(lax.broadcasted_iota(jnp.int32, v.shape, 1) == 0, line, roll(v, 1, 1))

    def from_below(v, line):
        return jnp.where(lax.broadcasted_iota(jnp.int32, v.shape, 1) == ROWS - 1, line, roll(v, -1, 1))

    def landed(ref, hh_, *at):
        return ref[(*at, pl.ds(hh_ * NPD, NPD))].reshape(NP, ROWS, Y)

    def mask_arcs(ks):
        for k in ks:
            for hh_ in range(2):
                fa[k, hh_] = landed(pp, hh_, k) * act[k, hh_][None]

    def mask_halo(ks):
        for k, hh_ in ks:
            for at in range(NP):
                line = hpr[hh_ * NPD + at // T, k, pl.ds(at % T, 1)]
                fh[k, hh_, at // ROWS, pl.ds(at % ROWS, 1)] = line * hact[k, hh_, 0:1]

    mask_arcs((1, 2))
    mask_halo(((1, 0), (2, 1)))
    for d in range(2):
        wait_recv(has[d], relay_copy(1 - d, 0))
        wait_recv(has[d], relay_copy(1 - d, 1))
        for t in range(NP):
            edge = jnp.broadcast_to(hnr[d, t // T, pl.ds(t % T, 1)], (ROWS, Y))
            fn[d, t] = jnp.where(low, edge, roll(nraw[d, t // T, t % T], -1, 0)) * nact[d]

    def settle(first, cur, acc, at, j, new, old):
        if j == 0:
            cur[at] = new
            return None
        if j == 1:
            cur[at] = new
            acc[at] = old + new
            return None
        mean = (acc[at] + new) * (1.0 / INNER)
        diff = mean - first[at]
        first[at] = mean
        return jnp.sum(diff * diff, axis=0)

    def rows_under(edge, lo, size):
        return jnp.stack([
            jnp.broadcast_to(edge[t // ROWS, t % ROWS : t % ROWS + 1], (ROWS, Y)) for t in range(lo, lo + size)
        ])

    def gradient(arcs, near, halo, bounds):
        for hh_ in range(2):
            k_in = 2 - hh_
            edge = (halo[0, hh_] + halo[k_in, 1 - hh_]) + (up_y(halo[3, hh_]) + dn_y(halo[4, hh_]))
            tail = None
            for lo, size in reversed(chunks):
                at = pl.ds(lo, size)
                p0, p3, p4 = arcs[0, hh_, at], arcs[3, hh_, at], arcs[4, hh_, at]
                back = (p0 + arcs[k_in, 1 - hh_, at]) + (up_y(p3) + dn_y(p4))
                g = ((p0 + p3) + (p4 + bounds[hh_, at])) + (arcs[1, hh_, at] + arcs[2, hh_, at])
                g = g - (from_below(back, rows_under(edge, lo, size)) + near[hh_, at])
                for t in range(lo + size - 1, lo - 1, -1):
                    tail = g[t - lo] if tail is None else tail + g[t - lo]
                    tl[hh_, t] = tail

    in_all(2).wait_recv()
    for hh_ in range(2):
        k_in = 2 - hh_
        edge = fh[k_in, 1 - hh_]
        tail = None
        for lo, size in reversed(chunks):
            at = pl.ds(lo, size)
            g = landed(pg, hh_)[lo : lo + size] + (fa[1, hh_, at] + fa[2, hh_, at])
            g = g - (from_below(fa[k_in, 1 - hh_, at], rows_under(edge, lo, size)) + fn[hh_, at])
            for t in range(lo + size - 1, lo - 1, -1):
                tail = g[t - lo] if tail is None else tail + g[t - lo]
                tl[hh_, t] = tail
    loads[3].wait()
    in_all(3).wait_recv()
    for hh_ in range(2):
        uf[hh_] = landed(pu, hh_)
    in_all(7).wait_recv()
    if pairs > 1:
        pl.semaphore_wait(token.at[0], pairs - 1)
    got = capb[0]
    for p in range(1, NPD):
        got = got + capb[p]
    caps = as_rows(got)
    climit = as_rows(got, NP) * blocks_all
    cap_first = cap_sum = inv_tons = None

    def totals(row, s):
        line = as_lanes(row)
        if s > 0:
            return line
        tons = jnp.sum(jnp.sum(ton[0] + ton[1], axis=0, keepdims=True), axis=1, keepdims=True)
        return jnp.where(lanes1 == NP, tons, line)

    for s in range(STEPS):
        j = s % INNER
        last, final = j == INNER - 1, s == STEPS - 1
        u_src = uf if j == 0 else uc
        b_src = bf if j == 0 else bc
        p_src, n_src, h_src = (fa, fn, fh) if j == 0 else (ca, cn, ch)
        inv_w = 1.0 / w
        move_p = jnp.zeros((ROWS, Y), jnp.float32)
        move_d = jnp.zeros((ROWS, Y), jnp.float32)
        if j == 0:
            for hh_ in range(2):
                for t in range(NP):
                    tau = tb[hh_, t] * inv_w
                    tt[hh_, t] = tau * (ton[hh_] * inv_root)
                    tl[hh_, t] = u_src[hh_, t] - tau * (tl[hh_, t] - pr[hh_, t])
        row = jnp.zeros((NP, Y), jnp.float32)
        heads = [None, None]
        for t in range(NP):
            mined = None
            for hh_ in range(2):
                old = u_src[hh_, t]
                new = jnp.maximum(tl[hh_, t] - tt[hh_, t] * caps[t : t + 1, :], 0.0)
                ext = 2.0 * new - old
                if j == 0:
                    uc[hh_, t] = new
                elif j == 1:
                    uc[hh_, t] = new
                    us[hh_, t] = old + new
                else:
                    mean = (us[hh_, t] + new) * (1.0 / INNER)
                    diff = mean - uf[hh_, t]
                    uf[hh_, t] = mean
                    move_p = move_p + diff * diff
                heads[hh_] = ext if t == 0 else heads[hh_] + ext
                xs[s, hh_, t] = heads[hh_]
                hs[s, hh_, t // ROWS, pl.ds(t % ROWS, 1)] = heads[hh_][ROWS - 1 : ROWS]
                if not final:
                    ls[s, hh_, t // ROWS, pl.ds(t % ROWS, 1)] = heads[hh_][0:1]
                part = ton[hh_] * ext
                mined = part if mined is None else mined + part
            row = jnp.where(rows == t, jnp.sum(mined, axis=0, keepdims=True), row)
        if not last:
            reduce_start(s, totals(row, s))
        if final:
            out_start(0)
        pl.when(up[1])(z_copy(1, s).start)
        for d in range(2):
            pl.when(has[d])(x_copy(d, s).start)
        for d in range(2):
            pl.when(has[d] & up[1])(d_copy(d, 1, s).start)
        if not final:
            pl.when(up[0])(z_copy(0, s).start)
            for d in range(2):
                pl.when(has[d] & up[0])(d_copy(d, 0, s).start)
        if s == 0:
            send_all(6)
            loads[2].wait()
            in_all(4).wait_recv()
            for hh_ in range(2):
                bf[hh_] = landed(pb, hh_)
        if last:
            reduce_start(s, totals(row, s))

        def arc(k, hh_, at, diff, move):
            old = p_src[k, hh_, at]
            new = jnp.maximum(old + rp[at] * diff, 0.0) * act[k, hh_][None]
            moved = settle(fa, ca, sa, (k, hh_, at), j, new, old)
            return move if moved is None else move + moved

        for hh_ in range(2):
            for lo, size in chunks:
                at = pl.ds(lo, size)
                old = b_src[hh_, at]
                new = jnp.maximum(old + 2.0 * rp[at] * (xs[s, hh_, at] - 1.0), 0.0)
                if j == 0:
                    bc[hh_, at] = new
                elif j == 1:
                    bc[hh_, at] = new
                    bs[hh_, at] = old + new
                else:
                    mean = (bs[hh_, at] + new) * (1.0 / INNER)
                    diff = mean - bf[hh_, at]
                    bf[hh_, at] = mean
                    move_d = move_d + jnp.sum(diff * diff, axis=0)
        if final:
            out_start(1)
        wait_recv(up[0], z_copy(1, s))

        def own_arcs(move):
            for lo, size in chunks:
                at = pl.ds(lo, size)
                for hh_ in range(2):
                    c = xs[s, hh_, at]
                    cz = from_above(c, lines(zh, lo, size, s, hh_))
                    move = arc(0, hh_, at, c - cz, move)
                    move = arc(3, hh_, at, c - dn_y(cz), move)
                    move = arc(4, hh_, at, c - up_y(cz), move)
            return move

        if s > 0:
            move_d = own_arcs(move_d)
        for lo, size in chunks:
            at = pl.ds(lo, size)
            c = [xs[s, hh_, at] for hh_ in range(2)]
            cz = [from_above(c[hh_], lines(zh, lo, size, s, hh_)) for hh_ in range(2)]
            move_d = arc(1, 0, at, c[0] - cz[1], move_d)
            move_d = arc(2, 1, at, c[1] - cz[0], move_d)
        if final:
            out_start(2)
        for d in range(2):
            wait_recv(has[d], x_copy(1 - d, s))
            wait_recv(has[d] & up[0], d_copy(1 - d, 1, s))
        for lo, size in chunks:
            at = pl.ds(lo, size)
            for d in range(2):
                cz = from_above(xr[s, d, at], lines(dh, lo, size, s, d))
                move_d = arc(2 - d, d, at, xs[s, d, at] - cz, move_d)
        if last:
            cyc = s // INNER
            mp = jnp.sum(move_p, axis=0, keepdims=True)
            md = jnp.sum(move_d, axis=0, keepdims=True)
            reduce_start(STEPS + cyc, as_lanes(jnp.where(rows == 0, mp, jnp.where(rows == 1, md, 0.0))))
        if final:
            out_start(3)
            out_start(4)
        else:
            wait_recv(up[1], z_copy(0, s))
            for d in range(2):
                wait_recv(has[d] & up[1], d_copy(1 - d, 0, s))
            for lo, size in chunks:
                at = pl.ds(lo, size)
                for d in range(2):
                    old = n_src[d, at]
                    diff = from_below(xr[s, d, at], lines(dl, lo, size, s, d)) - xs[s, d, at]
                    new = jnp.maximum(old + rp[at] * diff, 0.0) * nact[d][None]
                    settle(fn, cn, sn, (d, at), j, new, old)
            if s == 0:
                in_all(5).wait_recv()
                in_all(6).wait_recv()
                mask_arcs((0, 3, 4))
                mask_halo([(k, hh_) for k in (0, 3, 4) for hh_ in range(2)])
                own_arcs(move_d)
            for hh_ in range(2):
                c, cz = zl[s, hh_], hs[s, hh_]
                for k in (0, 3, 4, 1 + hh_):
                    ahead = (cz, hs[s, 1 - hh_], hs[s, 1 - hh_], dn_y(cz), up_y(cz))[k]
                    old = h_src[k, hh_]
                    new = jnp.maximum(old + rh[...] * (c - ahead), 0.0) * hact[k, hh_][None]
                    settle(fh, ch, sh, (k, hh_), j, new, old)
            if last:
                gradient(fa, fn, fh, bf)
            else:
                gradient(ca, cn, ch, bc)
                for hh_ in range(2):
                    for t in range(NP):
                        tau = tb[hh_, t] * inv_w
                        tl[hh_, t] = uc[hh_, t] - tau * (tl[hh_, t] - pr[hh_, t])
        got = reduce_done(s)
        if s == 0:
            inv_tons = 1.0 / jnp.sum(jnp.where(lanes1 == NP, got, 0.0), axis=1, keepdims=True)
        row_total = as_rows(got)
        new_caps = jnp.maximum(caps + w * ((row_total - climit) * inv_tons), 0.0)
        if j == 0:
            cap_first = caps
            cap_sum = new_caps
        else:
            cap_sum = cap_sum + new_caps
        caps = new_caps
        if last:
            caps = cap_sum * (1.0 / INNER)
            cap_move = jnp.sum((caps - cap_first) ** 2, axis=0, keepdims=True)
            if final:
                for t in range(T):
                    few_out[t] = jnp.sum(jnp.where(rows == pe * T + t, caps, 0.0), axis=0)
            tot = as_rows(reduce_done(STEPS + cyc))
            moved = jnp.sqrt((tot[1:2, :] + cap_move + EPS) / (tot[0:1, :] + EPS))
            w = jnp.sqrt(w * moved)
            if not final:
                set_rates(w)
    few_out[T] = w[0]
    u_out[0, :, rows_of(q)] = uf[h, mine]
    bound_out[0, :, rows_of(q)] = bf[h, mine]
    for k in range(5):
        prec_out[k, 0, :, rows_of(q)] = fa[k, h, mine]
    for what in range(5):
        out_all(what).wait_recv()
    for what in range(5):
        out_all(what).wait_send()
    for what in range(8):
        in_all(what).wait_send()
    rest = rb.at[:, pl.ds(0, ND - 1)]
    remote(rest, rest, r_s.at[0], r_r.at[0], other(0, 1)).wait_send()

    def wait_sent(cond, ref, sem):
        pl.when(cond)(lambda: remote(ref, ref, sem, sem, other(0, 1)).wait_send())

    rows_down, rows_up = ls.at[pl.ds(0, STEPS - 1)], hs
    wait_sent(up[0], rows_down, z_s.at[0])
    wait_sent(up[1], rows_up, z_s.at[1])
    for d in range(2):
        wait_sent(has[d], xs.at[:, d], x_s.at[d])
        wait_sent(has[d] & up[0], ls.at[pl.ds(0, STEPS - 1), d], d_s.at[d, 0])
        wait_sent(has[d] & up[1], hs.at[:, d], d_s.at[d, 1])
    for cond, copy in sends:
        if cond is None:
            copy.wait_send()
        else:
            pl.when(cond)(lambda copy=copy: copy.wait_send())


def store_kernel(u_ref, prec_ref, bound_ref, few_ref, u_out, prec_out, bound_out, cap_out, w_out, sem):
    stores = (
        pltpu.make_async_copy(prec_ref, prec_out, sem.at[0]),
        pltpu.make_async_copy(u_ref, u_out, sem.at[1]),
        pltpu.make_async_copy(bound_ref, bound_out, sem.at[2]),
    )
    for store in stores:
        store.start()
    T = cap_out.shape[0]
    for t in range(T):
        cap_out[t] = few_ref[t, 0]
    w_out[0] = few_ref[T, 0]
    for store in stores:
        store.wait()


def pair_call(NS, NPD, u, prec, bound, cap, capacity, bv, tc, dens, slope, om):
    _, T, Z, Y = u.shape
    f32 = jnp.float32
    NP, NQ, ND = NPD * T, 2 * NPD, NS * NPD
    NT = NP // ROWS
    vmem = pl.BlockSpec(memory_space=pltpu.VMEM)
    hbm = pl.BlockSpec(memory_space=pl.ANY)
    smem = pl.BlockSpec(memory_space=pltpu.SMEM)
    slots = STEPS + OUTER
    V = lambda *shape: pltpu.VMEM((*shape, Y), f32)
    unit = lambda *n: V(*n, NQ, T, ROWS)
    whole = lambda *n: V(*n, NP, ROWS)
    edge = lambda *n: V(*n, NT, ROWS)
    dma = pltpu.SemaphoreType.DMA
    ours = pl.pallas_call(
        functools.partial(pair_kernel, NS, NPD, T, Z, Y),
        out_shape=(
            pltpu.VMEM(u.shape, f32),
            pltpu.VMEM(prec.shape, f32),
            pltpu.VMEM(bound.shape, f32),
            pltpu.VMEM((T + 1, Y), f32),
        ),
        in_specs=[hbm] * 10,
        out_specs=(vmem, vmem, vmem, vmem),
        scratch_shapes=[
            pltpu.VMEM((1, Y), jnp.int32), pltpu.SMEM(cap.shape, f32), pltpu.SMEM(cap.shape, f32),
            pltpu.SMEM(dens.shape, f32), pltpu.SMEM(om.shape, f32), V(1), V(NQ, 1),
            V(5, T, Z), V(T, Z), V(T, Z), V(NQ, 5, T), unit(), unit(), unit(), unit(5), V(NQ, 5, T), V(2, NPD, T, ROWS), V(2, NPD, T),
            V(2, ROWS), pltpu.VMEM((2, ROWS, Y), jnp.int32), pltpu.VMEM((4, 1, Y), jnp.int32),
            whole(5, 2), whole(5, 2), whole(5, 2), whole(2), whole(2), whole(2),
            edge(5, 2), edge(5, 2), edge(5, 2), whole(2), whole(2), whole(2), whole(2), whole(2), whole(2),
            V(5, 2, ROWS), V(2, ROWS), V(5, 2, ROWS), V(2, ROWS), whole(2), whole(2), whole(2), whole(2),
            whole(), edge(),
            whole(STEPS, 2), whole(STEPS, 2), edge(STEPS, 2), edge(STEPS, 2), edge(STEPS, 2), edge(STEPS, 2),
            edge(STEPS, 2), edge(STEPS, 2), V(slots, 1), V(slots, ND, 1),
            pltpu.SemaphoreType.REGULAR((1,)), dma((12,)), dma((8,)), dma((8,)), dma((3,)), dma((3,)), dma((2,)), dma((2,)), dma((2, 2)), dma((2, 2)),
            dma((2,)), dma((2, 2)), dma((2,)), dma((2, 2)), dma((2, 2)), dma((2, 2, 2)), dma((1,)), dma((3,)),
            dma((5,)), dma((5,)),
        ],
        compiler_params=pltpu.CompilerParams(collective_id=1, has_side_effects=True),
    )(u, prec, bound, cap, capacity, bv, tc, dens, slope, om)
    return pl.pallas_call(
        store_kernel,
        out_shape=(
            jax.ShapeDtypeStruct(u.shape, f32),
            jax.ShapeDtypeStruct(prec.shape, f32),
            jax.ShapeDtypeStruct(bound.shape, f32),
            jax.ShapeDtypeStruct(cap.shape, f32),
            jax.ShapeDtypeStruct((1,), f32),
        ),
        in_specs=[vmem] * 4,
        out_specs=(hbm, hbm, hbm, smem, smem),
        scratch_shapes=[dma((3,))],
    )(*[pltpu.with_memory_space_constraint(x, pltpu.VMEM) for x in ours])


def solution(mesh):
    NS, NPD = mesh.shape["strip"], mesh.shape["period"]

    def per_device(u, prec, bound, cap, capacity, bv, tc, dens, slope, om):
        rows_here, T, Z, Y = u.shape
        assert rows_here == 1
        NP = NPD * T
        if NS % 2 == 0 and Z == 2 * NPD * ROWS and NP % ROWS == 0 and 2 * NP < Y:
            return pair_call(NS, NPD, u, prec, bound, cap, capacity, bv, tc, dens, slope, om)
        R = -(-T // 8) * 8
        f32 = jnp.float32
        vmem = pl.BlockSpec(memory_space=pltpu.VMEM)
        hbm = pl.BlockSpec(memory_space=pl.ANY)
        smem = pl.BlockSpec(memory_space=pltpu.SMEM)
        plane = lambda *n: pltpu.VMEM((*n, Z, Y), f32)
        dma = pltpu.SemaphoreType.DMA
        slots = 1 + STEPS + OUTER
        far = max(NPD - 1, 1)
        return pl.pallas_call(
            functools.partial(kernel, NS, NPD, T, Z, Y, R),
            out_shape=(
                pltpu.VMEM(u.shape, f32),
                pltpu.VMEM(prec.shape, f32),
                pltpu.VMEM(bound.shape, f32),
                jax.ShapeDtypeStruct(cap.shape, f32),
                jax.ShapeDtypeStruct((1,), f32),
            ),
            in_specs=[hbm, hbm, hbm, smem, smem, vmem, vmem, smem, vmem, smem],
            out_specs=(vmem, vmem, vmem, smem, smem),
            scratch_shapes=[
                plane(T), plane(T), plane(T), plane(T), plane(T), plane(T),
                plane(7, T), plane(7, T), plane(7, T), plane(7), plane(), plane(T), plane(T), plane(T), plane(),
                plane(STEPS, T), plane(2, STEPS, T), plane(STEPS), plane(STEPS, far),
                plane(STEPS), plane(STEPS, far),
                pltpu.VMEM((slots, 1, Y), f32), pltpu.VMEM((slots, NS, 1, Y), f32),
                pltpu.VMEM((OUTER, 1, Y), f32), pltpu.VMEM((OUTER, NPD, 1, Y), f32),
                pltpu.VMEM((2, 1, Y), jnp.int32),
                plane(5, T), plane(2), plane(2), dma((3,)),
                dma((2, 3)), dma((2, 3)), dma((2, 2, STEPS)), dma((2, 2, STEPS)),
                dma((STEPS, far)), dma((STEPS, far)), dma((STEPS, far)), dma((STEPS, far)),
                dma((slots, NS - 1)), dma((slots, NS - 1)), dma((OUTER, far)), dma((OUTER, far)),
            ],
            compiler_params=pltpu.CompilerParams(collective_id=0, has_side_effects=True),
        )(u, prec, bound, cap, capacity, bv, tc, dens, slope, om)

    in_specs = (
        P("strip", "period", None, None),
        P(None, "strip", "period", None, None),
        P("strip", "period", None, None),
        P("period"),
        P("period"),
        P("strip", None, None),
        P("strip", None, None),
        P(),
        P("strip", None),
        P(),
    )
    out_specs = (
        P("strip", "period", None, None),
        P(None, "strip", "period", None, None),
        P("strip", "period", None, None),
        P("period"),
        P(),
    )
    return jax.shard_map(
        per_device, mesh=mesh, in_specs=in_specs, out_specs=out_specs, check_vma=False
    )
```

```python
import functools
import math

import jax
import jax.numpy as jnp
from jax import lax
from jax.experimental import pallas as pl
from jax.experimental.pallas import tpu as pltpu
from jax.sharding import PartitionSpec as P

OUTER = 2
INNER = 3
STEPS = OUTER * INNER
RATE = math.log(1.1) / 12.0
EPS = 1e-06
SLOPE = 11.0
MESH = pl.DeviceIdType.MESH
ROWS = 8
CHUNK = 8


def kernel(
    NS, NPD, T, Z, Y, R,
    u_ref, prec_ref, bound_ref, cap_ref, capacity_ref, bv_ref, tc_ref, dens_ref, slope_ref, om_ref,
    u_out, prec_out, bound_out, cap_out, w_out,
    uf, uc, us, bf, bc, bs, fa, ca, sa, act, ton, tb, tl, cb, ex0,
    xs, xr, es, er, as_, ar, rs, rb, ps, pb, slr,
    praw, ti, to_sum, loc, ini_s, ini_r, xs_s, xs_r, e_s, e_r, a_s, a_r, r_s, r_r, p_s, p_r,
):
    me = lax.axis_index("strip")
    pe = lax.axis_index("period")
    total_rows = NS
    total_periods = NPD * T
    blocks_all = float(total_rows * Z * Y)
    root_blocks = math.sqrt(blocks_all)
    sends = []

    loads = (
        pltpu.make_async_copy(prec_ref.at[:, 0], praw, loc.at[0]),
        pltpu.make_async_copy(bound_ref.at[0], bf, loc.at[1]),
        pltpu.make_async_copy(u_ref.at[0], uf, loc.at[2]),
    )
    for load in loads:
        load.start()
    barrier = pltpu.get_barrier_semaphore()
    for k in range(1, NS):
        pl.semaphore_signal(barrier, inc=1, device_id={"strip": lax.rem(me + k, NS)}, device_id_type=MESH)
    for k in range(1, NPD):
        pl.semaphore_signal(barrier, inc=1, device_id={"period": lax.rem(pe + k, NPD)}, device_id_type=MESH)

    has = (me < NS - 1, me > 0)
    gets = (me > 0, me < NS - 1)
    to = (me + 1, me - 1)

    def remote(src, dst, ss, rr, dev):
        return pltpu.make_async_remote_copy(
            src_ref=src, dst_ref=dst, send_sem=ss, recv_sem=rr, device_id=dev, device_id_type=MESH
        )

    def ini_copy(d, what):
        if what == 2:
            return remote(to_sum.at[d], ti.at[d], ini_s.at[d, 2], ini_r.at[d, 2], {"strip": to[d]})
        if what == 0:
            rest = pl.ds(1, T - 1)
            return remote(praw.at[1 + d, rest], fa.at[5 + d, rest], ini_s.at[d, 0], ini_r.at[d, 0], {"strip": to[d]})
        return remote(slope_ref, slr.at[d], ini_s.at[d, 1], ini_r.at[d, 1], {"strip": to[d]})

    def x_copy(d, part, s):
        lo, size = (1, T - 1) if part == 0 else (0, 1)
        return remote(
            xs.at[s, pl.ds(lo, size)], xr.at[d, s, pl.ds(lo, size)],
            xs_s.at[d, part, s], xs_r.at[d, part, s], {"strip": to[d]},
        )

    def e_copy(k, s):
        return remote(es.at[s], er.at[s, k - 1], e_s.at[s, k - 1], e_r.at[s, k - 1], {"period": pe + k})

    def a_copy(k, s):
        return remote(as_.at[s], ar.at[s, k - 1], a_s.at[s, k - 1], a_r.at[s, k - 1], {"period": pe - k})

    def r_copy(k, slot):
        return remote(
            rs.at[slot], rb.at[slot, me], r_s.at[slot, k - 1], r_r.at[slot, k - 1],
            {"strip": lax.rem(me + k, NS)},
        )

    def p_copy(k, slot):
        return remote(
            ps.at[slot], pb.at[slot, pe], p_s.at[slot, k - 1], p_r.at[slot, k - 1],
            {"period": lax.rem(pe + k, NPD)},
        )

    def start(cond, copy):
        def go():
            copy.start()
        if cond is None:
            go()
        else:
            pl.when(cond)(go)
        sends.append((cond, copy))

    def wait_recv(cond, copy):
        if cond is None:
            copy.wait_recv()
        else:
            pl.when(cond)(lambda: copy.wait_recv())

    def reduce_start(slot, value):
        rs[slot] = value
        rb[slot, me] = value
        for k in range(1, NS):
            start(None, r_copy(k, slot))

    def reduce_done(slot):
        for k in range(1, NS):
            wait_recv(None, r_copy(k, slot))
        total = rb[slot, 0]
        for k in range(1, NS):
            total = total + rb[slot, k]
        return total

    loads[0].wait()
    for d in range(2):
        total = praw[1 + d, 0]
        for t in range(1, T):
            total = total + praw[1 + d, t]
        to_sum[d] = total
    pl.semaphore_wait(barrier, NS + NPD - 2)
    for d in range(2):
        start(has[d], ini_copy(d, 1))
        start(has[d], ini_copy(d, 2))
    for d in range(2):
        start(has[d], ini_copy(d, 0))

    rows = lax.broadcasted_iota(jnp.int32, (R, Y), 0)
    lanes = lax.broadcasted_iota(jnp.int32, (R, Y), 1)

    def as_lanes(value):
        sums = jnp.sum(value, axis=1, keepdims=True)
        return jnp.sum(jnp.where(lanes == rows, sums, 0.0), axis=0, keepdims=True)

    def as_rows(line):
        return jnp.sum(jnp.where(lanes == rows, line, 0.0), axis=1, keepdims=True)

    def fold(v):
        return jnp.sum(v.reshape(Z // 8, 8, Y), axis=0)

    cls = tc_ref[0]
    tons = jnp.zeros((Z, Y), jnp.float32)
    for c in range(dens_ref.shape[0]):
        tons = jnp.where(cls == c, (1.0 + c) * dens_ref[c], tons)
    ton[...] = tons
    part = jnp.sum(tons, axis=0, keepdims=True)
    reduce_start(0, part)

    z_ids = lax.broadcasted_iota(jnp.int32, (Z, Y), 0)
    y_ids = lax.broadcasted_iota(jnp.int32, (Z, Y), 1)

    def mask_of(codes, k, inside):
        ok = z_ids >= 1
        if k > 0:
            ok = ok & (jnp.broadcast_to((codes >> (k - 1)) & 1, (Z, Y)) == 1)
        if k == 3:
            ok = ok & (y_ids < Y - 1)
        if k == 4:
            ok = ok & (y_ids >= 1)
        if inside is not None:
            ok = ok & (jnp.full((Z, Y), inside.astype(jnp.int32)) == 1)
        return ok.astype(jnp.float32)

    own = slope_ref[...]
    act[0] = mask_of(own, 0, None)
    act[1] = mask_of(own, 1, me < NS - 1)
    act[2] = mask_of(own, 2, me > 0)
    act[3] = mask_of(own, 3, None)
    act[4] = mask_of(own, 4, None)

    period = [(pe * T + t).astype(jnp.float32) for t in range(T)]
    pid = [jnp.full((1, Y), period[t]) for t in range(T)]
    disc = [jnp.exp(-RATE * pid[t]) for t in range(T)]
    tonr = ton[...] * (1.0 / root_blocks)
    for load in loads[1:]:
        load.wait()
    for t in range(T):
        tb[t] = 1.0 / (SLOPE * (total_periods - pid[t]) + tonr)
        for k in range(5):
            fa[k, t] = praw[k, t] * act[k]

    caps = jnp.zeros((R, Y), jnp.float32)
    climit = jnp.zeros((R, Y), jnp.float32)
    for t in range(T):
        caps = jnp.where(rows == t, cap_ref[t], caps)
        climit = jnp.where(rows == t, capacity_ref[t] * blocks_all, climit)
    w = jnp.full((1, Y), om_ref[0])

    for d in range(2):
        @pl.when(jnp.logical_not(gets[d]))
        def _():
            act[5 + d] = jnp.zeros((Z, Y), jnp.float32)
            ti[d] = jnp.zeros((Z, Y), jnp.float32)
            fa[5 + d] = jnp.zeros((T, Z, Y), jnp.float32)
            for s in range(STEPS):
                xr[d, s] = jnp.zeros((T, Z, Y), jnp.float32)

    def up_y(v):
        return pltpu.roll(v, 1, 1)

    def dn_y(v):
        return pltpu.roll(v, Y - 1, 1)

    def up_z(v):
        return pltpu.roll(v, 1, 0)

    def dn_z(v):
        return pltpu.roll(v, Z - 1, 0)

    def settle(first, cur, acc, at, j, new, old):
        if j == 0:
            cur[at] = new
            return new, None
        if j == 1:
            cur[at] = new
            acc[at] = old + new
            return new, None
        mean = (acc[at] + new) * (1.0 / INNER)
        diff = mean - first[at]
        first[at] = mean
        return mean, fold(diff * diff)

    def gradient_own(arcs, bounds):
        for t in range(T):
            p0, p3, p4 = arcs[0, t], arcs[3, t], arcs[4, t]
            back = p0 + (up_y(p3) + dn_y(p4))
            tl[t] = ((p0 + p3) + (p4 + bounds[t])) - dn_z(back)

    def gradient(s, arcs):
        tail = None
        for t in range(T - 1, -1, -1):
            g = (tl[t] + (arcs[1, t] + arcs[2, t])) - dn_z(arcs[5, t] + arcs[6, t])
            tail = g if tail is None else tail + g
            tl[t] = tail
        as_[s] = tail
        for k in range(1, NPD):
            start(pe >= k, a_copy(k, s))

    tail = None
    for t in range(T - 1, -1, -1):
        p = [fa[k, t] for k in range(5)]
        g = (((p[0] + p[1]) + (p[2] + p[3])) + p[4]) + bf[t]
        g = g - dn_z(p[0] + (up_y(p[3]) + dn_y(p[4])))
        tail = g if tail is None else tail + g
        tl[t] = tail
    for d in range(2):
        wait_recv(gets[d], ini_copy(d, 1))
        wait_recv(gets[d], ini_copy(d, 2))

        @pl.when(gets[d])
        def _():
            act[5 + d] = mask_of(slr[d], 1 + d, None)
    as_[0] = tl[0] - dn_z(ti[0] * act[5] + ti[1] * act[6])
    for k in range(1, NPD):
        start(pe >= k, a_copy(k, 0))
    for d in range(2):
        wait_recv(gets[d], ini_copy(d, 0))
        rest = ti[d]
        for t in range(1, T):
            plane = fa[5 + d, t]
            rest = rest - plane
            fa[5 + d, t] = plane * act[5 + d]
        fa[5 + d, 0] = rest * act[5 + d]
    tail = None
    for t in range(T - 1, -1, -1):
        back = fa[5, t] + fa[6, t]
        tail = back if tail is None else tail + back
        tl[t] = tl[t] - dn_z(tail)
    tons_all = jnp.sum(reduce_done(0), axis=1, keepdims=True)
    inv_tons = 1.0 / tons_all
    cap_first = cap_sum = None

    for s in range(STEPS):
        j = s % INNER
        u_src = uf if j == 0 else uc
        b_src = bf if j == 0 else bc
        p_src = fa if j == 0 else ca
        inv_w = 1.0 / w
        move_p = jnp.zeros((8, Y), jnp.float32)
        move_d = jnp.zeros((8, Y), jnp.float32)
        for k in range(1, NPD):
            @pl.when(pe + k < NPD)
            def _():
                a_copy(k, s).wait_recv()
                for t in range(T):
                    tl[t] = tl[t] + ar[s, k - 1]
        head = None
        row = jnp.zeros((R, Y), jnp.float32)
        for t in range(T):
            old = u_src[t]
            grad = tl[t] + (ton[...] * (1.0 / root_blocks)) * caps[t : t + 1, :]
            new = jnp.maximum(old - (tb[t] * inv_w) * (grad - bv_ref[0] * disc[t]), 0.0)
            ext = 2.0 * new - old
            _, moved = settle(uf, uc, us, t, j, new, old)
            if moved is not None:
                move_p = move_p + moved
            if t == 0:
                ex0[...] = ext
            else:
                xs[s, t] = ext
            head = ext if head is None else head + ext
            row = jnp.where(rows == t, jnp.sum(ton[...] * ext, axis=0, keepdims=True), row)
        es[s] = head
        for k in range(1, NPD):
            start(pe + k < NPD, e_copy(k, s))
        for d in range(2):
            start(has[d], x_copy(d, 0, s))
        for k in range(1, NPD):
            @pl.when(pe >= k)
            def _():
                e_copy(k, s).wait_recv()
                ex0[...] = ex0[...] + er[s, k - 1]
        xs[s, 0] = ex0[...]
        for d in range(2):
            start(has[d], x_copy(d, 1, s))
        reduce_start(1 + s, as_lanes(row))
        total = None
        for t in range(T):
            total = xs[s, t] if t == 0 else total + xs[s, t]
            cb[t] = total
        rate_b = [w / (pid[t] + 1.0) for t in range(T)]
        rate_p = [w / (2.0 * (pid[t] + 1.0)) for t in range(T)]

        def arc(k, t, diff, move):
            old = p_src[k, t]
            new = jnp.maximum(old + rate_p[t] * diff, 0.0) * act[k]
            _, moved = settle(fa, ca, sa, (k, t), j, new, old)
            if moved is not None and k < 5:
                move = move + moved
            return move

        for t in range(T):
            c = cb[t]
            old = b_src[t]
            new = jnp.maximum(old + rate_b[t] * (c - 1.0), 0.0)
            _, moved = settle(bf, bc, bs, t, j, new, old)
            if moved is not None:
                move_d = move_d + moved
            cz = up_z(c)
            move_d = arc(0, t, c - cz, move_d)
            move_d = arc(3, t, c - dn_y(cz), move_d)
            move_d = arc(4, t, c - up_y(cz), move_d)
        last = j == INNER - 1
        if s < STEPS - 1:
            gradient_own(fa if last else ca, bf if last else bc)
        for part in range(2):
            for d in range(2):
                wait_recv(gets[d], x_copy(d, part, s))
        total_m = total_p = None
        for t in range(T):
            total_m = xr[0, s, t] if t == 0 else total_m + xr[0, s, t]
            total_p = xr[1, s, t] if t == 0 else total_p + xr[1, s, t]
            c = cb[t]
            cz = up_z(c)
            move_d = arc(1, t, c - up_z(total_p), move_d)
            move_d = arc(2, t, c - up_z(total_m), move_d)
            if s < STEPS - 1:
                arc(5, t, total_m - cz, None)
                arc(6, t, total_p - cz, None)
        if s < STEPS - 1:
            gradient(s + 1, fa if last else ca)
        if last:
            cyc = s // INNER
            mp = jnp.sum(move_p, axis=0, keepdims=True)
            md = jnp.sum(move_d, axis=0, keepdims=True)
            reduce_start(1 + STEPS + cyc, as_lanes(jnp.where(rows == 0, mp, jnp.where(rows == 1, md, 0.0))))
        row_total = as_rows(reduce_done(1 + s))
        new_caps = jnp.maximum(caps + w * ((row_total - climit) * inv_tons), 0.0)
        new_caps = jnp.where(rows < T, new_caps, 0.0)
        if j == 0:
            cap_first = caps
            cap_sum = new_caps
        else:
            cap_sum = cap_sum + new_caps
        caps = new_caps
        if last:
            caps = cap_sum * (1.0 / INNER)
            cap_move = jnp.sum((caps - cap_first) ** 2, axis=0, keepdims=True)
            got = reduce_done(1 + STEPS + cyc)
            msg = got + jnp.where(lanes[0:1] == 1, cap_move, 0.0)
            ps[cyc] = msg
            pb[cyc, pe] = msg
            for k in range(1, NPD):
                start(None, p_copy(k, cyc))
            if s == STEPS - 1:
                for t in range(T):
                    u_out[0, t] = uf[t]
                    bound_out[0, t] = bf[t]
                    for k in range(5):
                        prec_out[k, 0, t] = fa[k, t]
                    cap_out[t] = caps[t, 0]
            for k in range(1, NPD):
                wait_recv(None, p_copy(k, cyc))
            tot = pb[cyc, 0]
            for k in range(1, NPD):
                tot = tot + pb[cyc, k]
            tot = as_rows(tot)
            moved = jnp.sqrt((tot[1:2, :] + EPS) / (tot[0:1, :] + EPS))
            w = jnp.sqrt(w * moved)
    w_out[0] = w[0, 0]
    for cond, copy in sends:
        if cond is None:
            copy.wait_send()
        else:
            pl.when(cond)(lambda copy=copy: copy.wait_send())


def pair_kernel(
    NS, NPD, T, Z, Y,
    u_ref, prec_ref, bound_ref, cap_ref, capacity_ref, bv_ref, tc_ref, dens_ref, slope_ref, om_ref,
    u_out, prec_out, bound_out, few_out,
    slope_own, cap_own, capacity_own, dens_own, om_own, cap_line, capb, hm, hf, hcur, hacc, hc, praw, braw, gh, hh, pu, pb, pg, pp, hpr, nraw, hnr, bvb, tcb, slr,
    fa, ca, sa, fn, cn, sn, fh, ch, sh, bf, bc, bs, uf, uc, us,
    act, nact, hact, ton, tb, pr, tl, tt, rp, rh,
    xs, xr, hs, ls, zh, zl, dh, dl, rs, rb,
    token, loc, ini_s, ini_r, sl_s, sl_r, sm_s, sm_r, re_s, re_r,
    x_s, x_r, z_s, z_r, d_s, d_r, r_s, r_r, o_s, o_r, f_s, f_r, c_s, c_r,
):
    me = lax.axis_index("strip")
    pe = lax.axis_index("period")
    pairs, NP, NQ = NS // 2, NPD * T, 2 * NPD
    NT = NP // ROWS
    ND = NS * NPD
    a, h = me // 2, lax.rem(me, 2)
    q = jnp.where(h == 0, pe, NQ - 1 - pe)
    blocks_all = float(NS * Z * Y)
    inv_root = 1.0 / math.sqrt(blocks_all)
    sends = []

    def rows_of(block):
        return pl.ds(pl.multiple_of(ROWS * block, ROWS), ROWS)

    def block_of(hh_, pp_):
        return jnp.where(hh_ == 0, pp_, NQ - 1 - pp_)

    def device_at(pair, block):
        first = block < NPD
        return {
            "strip": 2 * pair + jnp.where(first, 0, 1),
            "period": jnp.where(first, block, NQ - 1 - block),
        }

    def remote(src, dst, ss, rr, dev):
        return pltpu.make_async_remote_copy(
            src_ref=src, dst_ref=dst, send_sem=ss, recv_sem=rr, device_id=dev, device_id_type=MESH
        )

    def start(cond, copy):
        if cond is None:
            copy.start()
        else:
            pl.when(cond)(lambda: copy.start())
        sends.append((cond, copy))

    def wait_recv(cond, copy):
        if cond is None:
            copy.wait_recv()
        else:
            pl.when(cond)(lambda: copy.wait_recv())

    mine = pl.ds(pe * T, T)
    unit = h * NPD + pe
    peers = pl.ds(0, NQ - 1)
    loads = (
        pltpu.make_async_copy(prec_ref.at[:, 0], praw, loc.at[0]),
        pltpu.make_async_copy(prec_ref.at[:, 0, :, rows_of(q)], pp.at[:, unit], loc.at[1]),
        pltpu.make_async_copy(bound_ref.at[0, :, rows_of(q)], pb.at[unit], loc.at[2]),
        pltpu.make_async_copy(u_ref.at[0, :, rows_of(q)], pu.at[unit], loc.at[3]),
        pltpu.make_async_copy(bound_ref.at[0], braw, loc.at[4]),
        pltpu.make_async_copy(slope_ref, slope_own, loc.at[5]),
        pltpu.make_async_copy(cap_ref, cap_own, loc.at[6]),
        pltpu.make_async_copy(capacity_ref, capacity_own, loc.at[7]),
        pltpu.make_async_copy(dens_ref, dens_own, loc.at[8]),
        pltpu.make_async_copy(om_ref, om_own, loc.at[9]),
        pltpu.make_async_copy(bv_ref.at[0, rows_of(q)], bvb.at[h], loc.at[10]),
        pltpu.make_async_copy(tc_ref.at[0, rows_of(q)], tcb.at[h], loc.at[11]),
    )
    for load in loads:
        load.start()
    barrier = pltpu.get_barrier_semaphore()
    others = [divmod(k, NPD) for k in range(1, ND)]
    others.sort(key=lambda o: -abs(o[0] - NS // 2) if o[0] else NS)

    def other(ks, kp):
        return {"strip": lax.rem(me + ks, NS), "period": lax.rem(pe + kp, NPD)}

    mates = [divmod(k, NPD) for k in range(1, NQ)]

    def mate(i):
        kh, kp = mates[i]
        return lax.rem(h + kh, 2), lax.rem(pe + kp, NPD)

    has = (a > 0, a < pairs - 1)
    up = (q > 0, q < NQ - 1)
    beside = [device_at(a - 1, q), device_at(a + 1, q)]
    for i in range(NQ - 1):
        th, tp = mate(i)
        pl.semaphore_signal(barrier, inc=1, device_id={"strip": 2 * a + th, "period": tp}, device_id_type=MESH)
    column = [device_at(lax.rem(a + k, pairs), q) for k in range(1, pairs)]
    for there in column:
        pl.semaphore_signal(barrier, inc=1, device_id=there, device_id_type=MESH)

    def in_ends(what, rows, block, at):
        if what == 1:
            return hh.at[block], hpr.at[at]
        if what == 2:
            return gh.at[:, rows], pg.at[at]
        if what == 7:
            return cap_line, capb.at[at]
        if what == 3:
            return u_ref.at[0, :, rows], pu.at[at]
        if what == 4:
            return bound_ref.at[0, :, rows], pb.at[at]
        arcs = {0: pl.ds(1, 2), 5: 0, 6: pl.ds(3, 2)}[what]
        return prec_ref.at[arcs, 0, :, rows], pp.at[arcs, at]

    def in_copy(i, what):
        th, tp = mate(i)
        block = block_of(th, tp)
        src, dst = in_ends(what, rows_of(block), block, unit)
        return remote(src, dst, ini_s.at[what], ini_r.at[what], {"strip": 2 * a + th, "period": tp})

    def in_all(what):
        dst = in_ends(what, rows_of(0), 0, peers)[1]
        return remote(dst, dst, ini_s.at[what], ini_r.at[what], other(0, 1))

    def partner_copy(what):
        rows = rows_of(block_of(1 - h, pe))
        dev = {"strip": 2 * a + 1 - h, "period": pe}
        if what == 0:
            return remote(tc_ref.at[0, rows], tcb.at[h], sm_s.at[0], sm_r.at[0], dev)
        return remote(bv_ref.at[0, rows], bvb.at[h], sm_s.at[1], sm_r.at[1], dev)

    def slope_copy(what):
        if what == 2:
            return remote(slope_ref, slr.at[1 + h], sl_s.at[2], sl_r.at[2], {"strip": 2 * a + 1 - h, "period": pe})
        return remote(slr.at[1 + what], slr.at[3 - 3 * what], sl_s.at[what], sl_r.at[1 - what], beside[what])

    def relay_copy(d, what):
        dev = beside[d]
        k, hs_ = (2, 0) if d == 0 else (1, 1)
        ss, rr = re_s.at[d, what], re_r.at[d, what]
        if what == 0:
            return remote(pp.at[k, pl.ds(hs_ * NPD, NPD)], nraw.at[1 - d], ss, rr, dev)
        return remote(hpr.at[pl.ds(hs_ * NPD, NPD), k], hnr.at[1 - d], ss, rr, dev)

    def reduce_sem(slot):
        return r_r.at[slot % 2 if slot < STEPS else 2]

    def reduce_start(slot, value):
        rs[slot] = value
        rb[slot, me * NPD + pe] = value
        for ks, kp in others:
            remote(
                rs.at[slot], rb.at[slot, me * NPD + pe], r_s.at[0], reduce_sem(slot), other(ks, kp)
            ).start()

    def reduce_done(slot):
        rest = rb.at[slot, pl.ds(0, ND - 1)]
        remote(rest, rest, r_s.at[0], reduce_sem(slot), other(0, 1)).wait_recv()
        parts = [rb[slot, i] for i in range(ND)]
        while len(parts) > 1:
            parts = [parts[i] + parts[i + 1] if i + 1 < len(parts) else parts[i] for i in range(0, len(parts), 2)]
        return parts[0]

    def x_copy(d, s):
        dev = beside[d]
        return remote(xs.at[s, d], xr.at[s, 1 - d], x_s.at[d], x_r.at[s % 2, 1 - d], dev)

    def z_copy(d, s):
        if d == 0:
            return remote(ls.at[s], zl.at[s], z_s.at[0], z_r.at[s % 2, 0], device_at(a, q - 1))
        return remote(hs.at[s], zh.at[s], z_s.at[1], z_r.at[s % 2, 1], device_at(a, q + 1))

    def d_copy(d, e, s):
        dev = device_at(a - 1 if d == 0 else a + 1, q - 1 if e == 0 else q + 1)
        src, dst = (ls, dl) if e == 0 else (hs, dh)
        return remote(src.at[s, d], dst.at[s, 1 - d], d_s.at[d, e], d_r.at[s % 2, 1 - d, e], dev)

    def out_ends(what, th, part, rows):
        if what == 0:
            return uf.at[th, part], u_out.at[0, :, rows]
        return fa.at[pl.ds(1, 2), th, part], prec_out.at[pl.ds(1, 2), 0, :, rows]

    def to_mates(src_of, dst, ss, rr):
        for i in range(NQ - 1):
            th, tp = mate(i)
            remote(src_of(th, pl.ds(tp * T, T)), dst, ss, rr, {"strip": 2 * a + th, "period": tp}).start()

    def out_start(what):
        dst = out_ends(what, 0, mine, rows_of(q))[1]
        to_mates(lambda th, part: out_ends(what, th, part, rows_of(q))[0], dst, o_s.at[what], o_r.at[what])

    def home_start():
        here = rows_of(q)
        for src, at in ((fa.at[0], 0), (fa.at[pl.ds(3, 2)], pl.ds(1, 2)), (bf, 3)):
            pick = lambda th, part: src.at[:, th, part] if src is not bf and at != 0 else src.at[th, part]
            to_mates(pick, hf.at[at, :, here], f_s.at[0], f_r.at[0])
        hf[0, :, here] = fa[0, h, mine]
        hf[1, :, here] = fa[3, h, mine]
        hf[2, :, here] = fa[4, h, mine]
        hf[3, :, here] = bf[h, mine]

    def sums_start(s, j):
        here = rows_of(q)
        to_mates(lambda th, part: xs.at[s, th, part], hc.at[j, :, here], c_s.at[0], c_r.at[j])
        hc[j, :, here] = xs[s, h, mine]

    def all_rows(ref):
        return ref.at[:, :, pl.ds(0, ROWS * (NQ - 1))]

    def home_step(j, w):
        if j == 0:
            remote(all_rows(hf), all_rows(hf), f_s.at[0], f_r.at[0], other(0, 1)).wait_recv()
        got = hc.at[j, :, pl.ds(0, ROWS * (NQ - 1))]
        remote(got, got, c_s.at[0], c_r.at[j], other(0, 1)).wait_recv()
        old_ref = hf if j == 0 else hcur
        for t in range(T):
            rate = w / (2.0 * (jnp.full((1, Y), (pe * T + t).astype(jnp.float32)) + 1.0))
            c = hc[j, t]
            cz = roll(c, 1, 0)
            for i, ahead in enumerate((cz, dn_y(cz), up_y(cz), None)):
                old = old_ref[i, t]
                if ahead is None:
                    new = jnp.maximum(old + 2.0 * rate * (c - 1.0), 0.0)
                else:
                    new = jnp.maximum(old + rate * (c - ahead), 0.0) * hm[i]
                if j < INNER - 1:
                    hcur[i, t] = new
                    hacc[i, t] = new if j == 0 else hacc[i, t] + new
                else:
                    mean = (hacc[i, t] + new) * (1.0 / INNER)
                    if ahead is None:
                        bound_out[0, t] = mean
                    else:
                        prec_out[(0, 3, 4)[i], 0, t] = mean

    def out_all(what):
        dst = out_ends(what, 0, mine, pl.ds(0, ROWS * (NQ - 1)))[1]
        return remote(dst, dst, o_s.at[what], o_r.at[what], other(0, 1))

    lanes1 = lax.broadcasted_iota(jnp.int32, (1, Y), 1)
    rows = lax.broadcasted_iota(jnp.int32, (NP, Y), 0)
    lanes = lax.broadcasted_iota(jnp.int32, (NP, Y), 1)

    def tons_of(cls):
        tons = jnp.zeros(cls.shape, jnp.float32)
        for c in range(dens_own.shape[0]):
            tons = jnp.where(cls == c, (1.0 + c) * dens_own[c], tons)
        return tons

    def as_lanes(value):
        sums = jnp.sum(value, axis=1, keepdims=True)
        return jnp.sum(jnp.where(lanes == rows, sums, 0.0), axis=0, keepdims=True)

    def as_rows(line, at=0):
        return jnp.broadcast_to(jnp.sum(jnp.where(lanes == rows + at, line, 0.0), axis=1, keepdims=True), (NP, Y))

    def roll(v, by, axis):
        return pltpu.roll(v, by % v.shape[axis], axis)

    def up_y(v):
        return roll(v, 1, v.ndim - 1)

    def dn_y(v):
        return roll(v, -1, v.ndim - 1)

    def mask_of(code, k, depth, inside):
        ok = (depth >= 1) & (depth < Z)
        y_ids = lax.broadcasted_iota(jnp.int32, depth.shape, 1)
        if k > 0:
            ok = ok & (jnp.broadcast_to((code >> (k - 1)) & 1, depth.shape) == 1)
        if k == 3:
            ok = ok & (y_ids < Y - 1)
        if k == 4:
            ok = ok & (y_ids >= 1)
        if inside is not None:
            ok = ok & (jnp.full(depth.shape, inside.astype(jnp.int32)) == 1)
        return ok.astype(jnp.float32)

    def send_all(*kinds):
        for what in kinds:
            for i in range(NQ - 1):
                in_copy(i, what).start()

    pl.semaphore_wait(barrier, NQ - 1 + pairs - 1)
    send_all(0)
    for there in column:
        pl.semaphore_signal(token.at[0], inc=1, device_id=there, device_id_type=MESH)
    start(None, slope_copy(2))
    start(None, partner_copy(0))
    start(None, partner_copy(1))
    send_all(3)
    for load in loads[6:10]:
        load.wait()
    line = jnp.zeros((1, Y), jnp.float32)
    for t in range(T):
        line = jnp.where(lanes1 == pe * T + t, cap_own[t], line)
        line = jnp.where(lanes1 == NP + pe * T + t, capacity_own[t], line)
    cap_line[...] = line
    capb[unit] = line
    loads[0].wait()
    for b in range(NQ):
        if b + 1 < NQ:
            for k in range(5):
                for t in range(T):
                    hh[b, k, pl.ds(t, 1)] = praw[k, t, pl.ds(ROWS * (b + 1), 1)]
        else:
            hh[b] = jnp.zeros((5, T, Y), jnp.float32)
    hpr[unit] = hh[q]
    send_all(1, 7)
    z_ids = lax.broadcasted_iota(jnp.int32, (ROWS, Y), 0)
    low = z_ids == ROWS - 1
    depth = lax.broadcasted_iota(jnp.int32, (Z, Y), 0)
    loads[5].wait()
    home = {k: mask_of(slope_own[...], k, depth, None) for k in (0, 3, 4)}
    loads[4].wait()
    for i, k in enumerate((0, 3, 4)):
        hm[i] = home[k]
    for t in range(T):
        p0, p3, p4 = (praw[k, t] * home[k] for k in (0, 3, 4))
        gh[t] = ((p0 + p3) + (p4 + braw[t])) - roll(p0 + (up_y(p3) + dn_y(p4)), -1, 0)
    pg[unit] = gh[:, rows_of(q)]
    send_all(2, 4, 5)
    slr[1 + h] = slope_own[...]
    for d in range(2):
        @pl.when(jnp.logical_not(has[d]))
        def _():
            for s in range(STEPS):
                xr[s, d] = jnp.zeros((NP, ROWS, Y), jnp.float32)
            nraw[d] = jnp.zeros((NPD, T, ROWS, Y), jnp.float32)
            hnr[d] = jnp.zeros((NPD, T, Y), jnp.float32)
            slr[3 * d] = jnp.zeros((1, Y), jnp.int32)
        for e in range(2):
            buf = (dh, dl)[e]

            @pl.when(jnp.logical_not(has[d] & up[e]))
            def _():
                for s in range(STEPS):
                    buf[s, d] = jnp.zeros((NT, ROWS, Y), jnp.float32)
    for e in range(2):
        buf = (zh, zl)[e]

        @pl.when(jnp.logical_not(up[e]))
        def _():
            for s in range(STEPS):
                buf[s] = jnp.zeros((2, NT, ROWS, Y), jnp.float32)

    wait_recv(None, slope_copy(2))
    for d in range(2):
        start(has[d], slope_copy(d))
    here, below = z_ids + ROWS * q, jnp.full((ROWS, Y), ROWS * (q + 1))
    for hh_ in range(2):
        code = slr[1 + hh_]
        for k in range(5):
            inside = None
            if k == 1 and hh_ == 1:
                inside = has[1]
            if k == 2 and hh_ == 0:
                inside = has[0]
            act[k, hh_] = mask_of(code, k, here, inside)
            hact[k, hh_] = mask_of(code, k, below, inside)
    for d in range(2):
        wait_recv(has[d], slope_copy(1 - d))
        nact[d] = mask_of(slr[3 * d], 1 + d, here + 1, has[d])

    wait_recv(None, partner_copy(0))
    wait_recv(None, partner_copy(1))
    loads[10].wait()
    loads[11].wait()
    for hh_ in range(2):
        tons = tons_of(tcb[hh_])
        ton[hh_] = tons
        for t in range(NP):
            tb[hh_, t] = 1.0 / (SLOPE * (NP - t) + tons * inv_root)
            pr[hh_, t] = bvb[hh_] * math.exp(-RATE * t)

    t_plane = lax.broadcasted_iota(jnp.int32, (NP, ROWS, Y), 0).astype(jnp.float32)
    t_rows = (
        lax.broadcasted_iota(jnp.int32, (NT, ROWS, Y), 0) * ROWS + lax.broadcasted_iota(jnp.int32, (NT, ROWS, Y), 1)
    ).astype(jnp.float32)

    w = jnp.full((1, Y), om_own[0])

    def set_rates(w):
        rp[...] = w[None] / (2.0 * (t_plane + 1.0))
        rh[...] = w[None] / (2.0 * (t_rows + 1.0))

    set_rates(w)

    loads[1].wait()
    in_all(0).wait_recv()
    for d in range(2):
        start(has[d], relay_copy(d, 0))
    in_all(1).wait_recv()
    for d in range(2):
        start(has[d], relay_copy(d, 1))

    chunks = [(lo, min(CHUNK, NP - lo)) for lo in range(0, NP, CHUNK)]

    def lines(ref, lo, size, *at):
        picked = [ref[(*at, t // ROWS, pl.ds(t % ROWS, 1))] for t in range(lo, lo + size)]
        return jnp.stack([jnp.broadcast_to(p, (ROWS, Y)) for p in picked])

    def from_above(v, line):
        return jnp.where(lax.broadcasted_iota(jnp.int32, v.shape, 1) == 0, line, roll(v, 1, 1))

    def from_below(v, line):
        return jnp.where(lax.broadcasted_iota(jnp.int32, v.shape, 1) == ROWS - 1, line, roll(v, -1, 1))

    def landed(ref, hh_, *at):
        return ref[(*at, pl.ds(hh_ * NPD, NPD))].reshape(NP, ROWS, Y)

    def mask_arcs(ks):
        for k in ks:
            for hh_ in range(2):
                fa[k, hh_] = landed(pp, hh_, k) * act[k, hh_][None]

    def mask_halo(ks):
        for k, hh_ in ks:
            for at in range(NP):
                line = hpr[hh_ * NPD + at // T, k, pl.ds(at % T, 1)]
                fh[k, hh_, at // ROWS, pl.ds(at % ROWS, 1)] = line * hact[k, hh_, 0:1]

    mask_arcs((1, 2))
    mask_halo(((1, 0), (2, 1)))
    for d in range(2):
        wait_recv(has[d], relay_copy(1 - d, 0))
        wait_recv(has[d], relay_copy(1 - d, 1))
        for t in range(NP):
            edge = jnp.broadcast_to(hnr[d, t // T, pl.ds(t % T, 1)], (ROWS, Y))
            fn[d, t] = jnp.where(low, edge, roll(nraw[d, t // T, t % T], -1, 0)) * nact[d]

    def settle(first, cur, acc, at, j, new, old, keep=True):
        if j == 0:
            cur[at] = new
            return None
        if j == 1:
            cur[at] = new
            acc[at] = old + new
            return None
        mean = (acc[at] + new) * (1.0 / INNER)
        diff = mean - first[at]
        if keep:
            first[at] = mean
        return jnp.sum(diff * diff, axis=0)

    def rows_under(edge, lo, size):
        return jnp.stack([
            jnp.broadcast_to(edge[t // ROWS, t % ROWS : t % ROWS + 1], (ROWS, Y)) for t in range(lo, lo + size)
        ])

    def gradient(arcs, near, halo, bounds):
        for hh_ in range(2):
            k_in = 2 - hh_
            edge = (halo[0, hh_] + halo[k_in, 1 - hh_]) + (up_y(halo[3, hh_]) + dn_y(halo[4, hh_]))
            tail = None
            for lo, size in reversed(chunks):
                at = pl.ds(lo, size)
                p0, p3, p4 = arcs[0, hh_, at], arcs[3, hh_, at], arcs[4, hh_, at]
                back = (p0 + arcs[k_in, 1 - hh_, at]) + (up_y(p3) + dn_y(p4))
                g = ((p0 + p3) + (p4 + bounds[hh_, at])) + (arcs[1, hh_, at] + arcs[2, hh_, at])
                g = g - (from_below(back, rows_under(edge, lo, size)) + near[hh_, at])
                for t in range(lo + size - 1, lo - 1, -1):
                    tail = g[t - lo] if tail is None else tail + g[t - lo]
                    tl[hh_, t] = tail

    in_all(2).wait_recv()
    for hh_ in range(2):
        k_in = 2 - hh_
        edge = fh[k_in, 1 - hh_]
        tail = None
        for lo, size in reversed(chunks):
            at = pl.ds(lo, size)
            g = landed(pg, hh_)[lo : lo + size] + (fa[1, hh_, at] + fa[2, hh_, at])
            g = g - (from_below(fa[k_in, 1 - hh_, at], rows_under(edge, lo, size)) + fn[hh_, at])
            for t in range(lo + size - 1, lo - 1, -1):
                tail = g[t - lo] if tail is None else tail + g[t - lo]
                tl[hh_, t] = tail
    loads[3].wait()
    in_all(3).wait_recv()
    for hh_ in range(2):
        uf[hh_] = landed(pu, hh_)
    in_all(7).wait_recv()
    if pairs > 1:
        pl.semaphore_wait(token.at[0], pairs - 1)
    got = capb[0]
    for p in range(1, NPD):
        got = got + capb[p]
    caps = as_rows(got)
    climit = as_rows(got, NP) * blocks_all
    cap_first = cap_sum = inv_tons = None

    def totals(row, s):
        line = as_lanes(row)
        if s > 0:
            return line
        tons = jnp.sum(jnp.sum(ton[0] + ton[1], axis=0, keepdims=True), axis=1, keepdims=True)
        return jnp.where(lanes1 == NP, tons, line)

    for s in range(STEPS):
        j = s % INNER
        last, final = j == INNER - 1, s == STEPS - 1
        u_src = uf if j == 0 else uc
        b_src = bf if j == 0 else bc
        p_src, n_src, h_src = (fa, fn, fh) if j == 0 else (ca, cn, ch)
        inv_w = 1.0 / w
        move_p = jnp.zeros((ROWS, Y), jnp.float32)
        move_d = jnp.zeros((ROWS, Y), jnp.float32)
        if j == 0:
            for hh_ in range(2):
                for t in range(NP):
                    tau = tb[hh_, t] * inv_w
                    tt[hh_, t] = tau * (ton[hh_] * inv_root)
                    tl[hh_, t] = u_src[hh_, t] - tau * (tl[hh_, t] - pr[hh_, t])
        row = jnp.zeros((NP, Y), jnp.float32)
        heads = [None, None]
        for t in range(NP):
            mined = None
            for hh_ in range(2):
                old = u_src[hh_, t]
                new = jnp.maximum(tl[hh_, t] - tt[hh_, t] * caps[t : t + 1, :], 0.0)
                ext = 2.0 * new - old
                if j == 0:
                    uc[hh_, t] = new
                elif j == 1:
                    uc[hh_, t] = new
                    us[hh_, t] = old + new
                else:
                    mean = (us[hh_, t] + new) * (1.0 / INNER)
                    diff = mean - uf[hh_, t]
                    uf[hh_, t] = mean
                    move_p = move_p + diff * diff
                heads[hh_] = ext if t == 0 else heads[hh_] + ext
                xs[s, hh_, t] = heads[hh_]
                hs[s, hh_, t // ROWS, pl.ds(t % ROWS, 1)] = heads[hh_][ROWS - 1 : ROWS]
                if not final:
                    ls[s, hh_, t // ROWS, pl.ds(t % ROWS, 1)] = heads[hh_][0:1]
                part = ton[hh_] * ext
                mined = part if mined is None else mined + part
            row = jnp.where(rows == t, jnp.sum(mined, axis=0, keepdims=True), row)
        if not last:
            reduce_start(s, totals(row, s))
        if final:
            out_start(0)
        pl.when(up[1])(z_copy(1, s).start)
        for d in range(2):
            pl.when(has[d])(x_copy(d, s).start)
        for d in range(2):
            pl.when(has[d] & up[1])(d_copy(d, 1, s).start)
        if not final:
            pl.when(up[0])(z_copy(0, s).start)
            for d in range(2):
                pl.when(has[d] & up[0])(d_copy(d, 0, s).start)
        if s >= STEPS - INNER:
            sums_start(s, j)
        if s == 0:
            send_all(6)
            loads[2].wait()
            in_all(4).wait_recv()
            for hh_ in range(2):
                bf[hh_] = landed(pb, hh_)
        if last:
            reduce_start(s, totals(row, s))

        def arc(k, hh_, at, diff, move):
            old = p_src[k, hh_, at]
            new = jnp.maximum(old + rp[at] * diff, 0.0) * act[k, hh_][None]
            moved = settle(fa, ca, sa, (k, hh_, at), j, new, old, not final or k in (1, 2))
            return move if moved is None else move + moved

        for hh_ in range(2):
            for lo, size in chunks:
                at = pl.ds(lo, size)
                old = b_src[hh_, at]
                new = jnp.maximum(old + 2.0 * rp[at] * (xs[s, hh_, at] - 1.0), 0.0)
                if j == 0:
                    bc[hh_, at] = new
                elif j == 1:
                    bc[hh_, at] = new
                    bs[hh_, at] = old + new
                else:
                    mean = (bs[hh_, at] + new) * (1.0 / INNER)
                    diff = mean - bf[hh_, at]
                    if not final:
                        bf[hh_, at] = mean
                    move_d = move_d + jnp.sum(diff * diff, axis=0)
        if s > STEPS - INNER:
            home_step(j - 1, w)
        wait_recv(up[0], z_copy(1, s))

        def own_arcs(move):
            for lo, size in chunks:
                at = pl.ds(lo, size)
                for hh_ in range(2):
                    c = xs[s, hh_, at]
                    cz = from_above(c, lines(zh, lo, size, s, hh_))
                    move = arc(0, hh_, at, c - cz, move)
                    move = arc(3, hh_, at, c - dn_y(cz), move)
                    move = arc(4, hh_, at, c - up_y(cz), move)
            return move

        if s > 0:
            move_d = own_arcs(move_d)
        for lo, size in chunks:
            at = pl.ds(lo, size)
            c = [xs[s, hh_, at] for hh_ in range(2)]
            cz = [from_above(c[hh_], lines(zh, lo, size, s, hh_)) for hh_ in range(2)]
            move_d = arc(1, 0, at, c[0] - cz[1], move_d)
            move_d = arc(2, 1, at, c[1] - cz[0], move_d)
        for d in range(2):
            wait_recv(has[d], x_copy(1 - d, s))
            wait_recv(has[d] & up[0], d_copy(1 - d, 1, s))
        for lo, size in chunks:
            at = pl.ds(lo, size)
            for d in range(2):
                cz = from_above(xr[s, d, at], lines(dh, lo, size, s, d))
                move_d = arc(2 - d, d, at, xs[s, d, at] - cz, move_d)
        if last:
            cyc = s // INNER
            mp = jnp.sum(move_p, axis=0, keepdims=True)
            md = jnp.sum(move_d, axis=0, keepdims=True)
            reduce_start(STEPS + cyc, as_lanes(jnp.where(rows == 0, mp, jnp.where(rows == 1, md, 0.0))))
        if s == STEPS - INNER - 1:
            home_start()
        if final:
            out_start(1)
            home_step(j, w)
        else:
            wait_recv(up[1], z_copy(0, s))
            for d in range(2):
                wait_recv(has[d] & up[1], d_copy(1 - d, 0, s))
            for lo, size in chunks:
                at = pl.ds(lo, size)
                for d in range(2):
                    old = n_src[d, at]
                    diff = from_below(xr[s, d, at], lines(dl, lo, size, s, d)) - xs[s, d, at]
                    new = jnp.maximum(old + rp[at] * diff, 0.0) * nact[d][None]
                    settle(fn, cn, sn, (d, at), j, new, old)
            if s == 0:
                in_all(5).wait_recv()
                in_all(6).wait_recv()
                mask_arcs((0, 3, 4))
                mask_halo([(k, hh_) for k in (0, 3, 4) for hh_ in range(2)])
                own_arcs(move_d)
            for hh_ in range(2):
                c, cz = zl[s, hh_], hs[s, hh_]
                for k in (0, 3, 4, 1 + hh_):
                    ahead = (cz, hs[s, 1 - hh_], hs[s, 1 - hh_], dn_y(cz), up_y(cz))[k]
                    old = h_src[k, hh_]
                    new = jnp.maximum(old + rh[...] * (c - ahead), 0.0) * hact[k, hh_][None]
                    settle(fh, ch, sh, (k, hh_), j, new, old)
            if last:
                gradient(fa, fn, fh, bf)
            else:
                gradient(ca, cn, ch, bc)
                for hh_ in range(2):
                    for t in range(NP):
                        tau = tb[hh_, t] * inv_w
                        tl[hh_, t] = uc[hh_, t] - tau * (tl[hh_, t] - pr[hh_, t])
        got = reduce_done(s)
        if s == 0:
            inv_tons = 1.0 / jnp.sum(jnp.where(lanes1 == NP, got, 0.0), axis=1, keepdims=True)
        row_total = as_rows(got)
        new_caps = jnp.maximum(caps + w * ((row_total - climit) * inv_tons), 0.0)
        if j == 0:
            cap_first = caps
            cap_sum = new_caps
        else:
            cap_sum = cap_sum + new_caps
        caps = new_caps
        if last:
            caps = cap_sum * (1.0 / INNER)
            cap_move = jnp.sum((caps - cap_first) ** 2, axis=0, keepdims=True)
            if final:
                for t in range(T):
                    few_out[t] = jnp.sum(jnp.where(rows == pe * T + t, caps, 0.0), axis=0)
            tot = as_rows(reduce_done(STEPS + cyc))
            moved = jnp.sqrt((tot[1:2, :] + cap_move + EPS) / (tot[0:1, :] + EPS))
            w = jnp.sqrt(w * moved)
            if not final:
                set_rates(w)
    few_out[T] = w[0]
    u_out[0, :, rows_of(q)] = uf[h, mine]
    for k in (1, 2):
        prec_out[k, 0, :, rows_of(q)] = fa[k, h, mine]
    for what in range(2):
        out_all(what).wait_recv()
    for what in range(2):
        out_all(what).wait_send()
    remote(all_rows(hf), all_rows(hf), f_s.at[0], f_r.at[0], other(0, 1)).wait_send()
    remote(all_rows(hc), all_rows(hc), c_s.at[0], c_r.at[0], other(0, 1)).wait_send()
    for what in range(8):
        in_all(what).wait_send()
    rest = rb.at[:, pl.ds(0, ND - 1)]
    remote(rest, rest, r_s.at[0], r_r.at[0], other(0, 1)).wait_send()

    def wait_sent(cond, ref, sem):
        pl.when(cond)(lambda: remote(ref, ref, sem, sem, other(0, 1)).wait_send())

    rows_down, rows_up = ls.at[pl.ds(0, STEPS - 1)], hs
    wait_sent(up[0], rows_down, z_s.at[0])
    wait_sent(up[1], rows_up, z_s.at[1])
    for d in range(2):
        wait_sent(has[d], xs.at[:, d], x_s.at[d])
        wait_sent(has[d] & up[0], ls.at[pl.ds(0, STEPS - 1), d], d_s.at[d, 0])
        wait_sent(has[d] & up[1], hs.at[:, d], d_s.at[d, 1])
    for cond, copy in sends:
        if cond is None:
            copy.wait_send()
        else:
            pl.when(cond)(lambda copy=copy: copy.wait_send())


def store_kernel(u_ref, prec_ref, bound_ref, few_ref, u_out, prec_out, bound_out, cap_out, w_out, sem):
    stores = (
        pltpu.make_async_copy(prec_ref, prec_out, sem.at[0]),
        pltpu.make_async_copy(u_ref, u_out, sem.at[1]),
        pltpu.make_async_copy(bound_ref, bound_out, sem.at[2]),
    )
    for store in stores:
        store.start()
    T = cap_out.shape[0]
    for t in range(T):
        cap_out[t] = few_ref[t, 0]
    w_out[0] = few_ref[T, 0]
    for store in stores:
        store.wait()


def pair_call(NS, NPD, u, prec, bound, cap, capacity, bv, tc, dens, slope, om):
    _, T, Z, Y = u.shape
    f32 = jnp.float32
    NP, NQ, ND = NPD * T, 2 * NPD, NS * NPD
    NT = NP // ROWS
    vmem = pl.BlockSpec(memory_space=pltpu.VMEM)
    hbm = pl.BlockSpec(memory_space=pl.ANY)
    smem = pl.BlockSpec(memory_space=pltpu.SMEM)
    slots = STEPS + OUTER
    V = lambda *shape: pltpu.VMEM((*shape, Y), f32)
    unit = lambda *n: V(*n, NQ, T, ROWS)
    whole = lambda *n: V(*n, NP, ROWS)
    edge = lambda *n: V(*n, NT, ROWS)
    dma = pltpu.SemaphoreType.DMA
    ours = pl.pallas_call(
        functools.partial(pair_kernel, NS, NPD, T, Z, Y),
        out_shape=(
            pltpu.VMEM(u.shape, f32),
            pltpu.VMEM(prec.shape, f32),
            pltpu.VMEM(bound.shape, f32),
            pltpu.VMEM((T + 1, Y), f32),
        ),
        in_specs=[hbm] * 10,
        out_specs=(vmem, vmem, vmem, vmem),
        scratch_shapes=[
            pltpu.VMEM((1, Y), jnp.int32), pltpu.SMEM(cap.shape, f32), pltpu.SMEM(cap.shape, f32),
            pltpu.SMEM(dens.shape, f32), pltpu.SMEM(om.shape, f32), V(1), V(NQ, 1),
            V(3, Z), V(4, T, Z), V(4, T, Z), V(4, T, Z), V(INNER, T, Z),
            V(5, T, Z), V(T, Z), V(T, Z), V(NQ, 5, T), unit(), unit(), unit(), unit(5), V(NQ, 5, T), V(2, NPD, T, ROWS), V(2, NPD, T),
            V(2, ROWS), pltpu.VMEM((2, ROWS, Y), jnp.int32), pltpu.VMEM((4, 1, Y), jnp.int32),
            whole(5, 2), whole(5, 2), whole(5, 2), whole(2), whole(2), whole(2),
            edge(5, 2), edge(5, 2), edge(5, 2), whole(2), whole(2), whole(2), whole(2), whole(2), whole(2),
            V(5, 2, ROWS), V(2, ROWS), V(5, 2, ROWS), V(2, ROWS), whole(2), whole(2), whole(2), whole(2),
            whole(), edge(),
            whole(STEPS, 2), whole(STEPS, 2), edge(STEPS, 2), edge(STEPS, 2), edge(STEPS, 2), edge(STEPS, 2),
            edge(STEPS, 2), edge(STEPS, 2), V(slots, 1), V(slots, ND, 1),
            pltpu.SemaphoreType.REGULAR((1,)), dma((12,)), dma((8,)), dma((8,)), dma((3,)), dma((3,)), dma((2,)), dma((2,)), dma((2, 2)), dma((2, 2)),
            dma((2,)), dma((2, 2)), dma((2,)), dma((2, 2)), dma((2, 2)), dma((2, 2, 2)), dma((1,)), dma((3,)),
            dma((2,)), dma((2,)), dma((1,)), dma((1,)), dma((1,)), dma((INNER,)),
        ],
        compiler_params=pltpu.CompilerParams(collective_id=1, has_side_effects=True),
    )(u, prec, bound, cap, capacity, bv, tc, dens, slope, om)
    return pl.pallas_call(
        store_kernel,
        out_shape=(
            jax.ShapeDtypeStruct(u.shape, f32),
            jax.ShapeDtypeStruct(prec.shape, f32),
            jax.ShapeDtypeStruct(bound.shape, f32),
            jax.ShapeDtypeStruct(cap.shape, f32),
            jax.ShapeDtypeStruct((1,), f32),
        ),
        in_specs=[vmem] * 4,
        out_specs=(hbm, hbm, hbm, smem, smem),
        scratch_shapes=[dma((3,))],
    )(*[pltpu.with_memory_space_constraint(x, pltpu.VMEM) for x in ours])


def solution(mesh):
    NS, NPD = mesh.shape["strip"], mesh.shape["period"]

    def per_device(u, prec, bound, cap, capacity, bv, tc, dens, slope, om):
        rows_here, T, Z, Y = u.shape
        assert rows_here == 1
        NP = NPD * T
        if NS % 2 == 0 and Z == 2 * NPD * ROWS and NP % ROWS == 0 and 2 * NP < Y:
            return pair_call(NS, NPD, u, prec, bound, cap, capacity, bv, tc, dens, slope, om)
        R = -(-T // 8) * 8
        f32 = jnp.float32
        vmem = pl.BlockSpec(memory_space=pltpu.VMEM)
        hbm = pl.BlockSpec(memory_space=pl.ANY)
        smem = pl.BlockSpec(memory_space=pltpu.SMEM)
        plane = lambda *n: pltpu.VMEM((*n, Z, Y), f32)
        dma = pltpu.SemaphoreType.DMA
        slots = 1 + STEPS + OUTER
        far = max(NPD - 1, 1)
        return pl.pallas_call(
            functools.partial(kernel, NS, NPD, T, Z, Y, R),
            out_shape=(
                pltpu.VMEM(u.shape, f32),
                pltpu.VMEM(prec.shape, f32),
                pltpu.VMEM(bound.shape, f32),
                jax.ShapeDtypeStruct(cap.shape, f32),
                jax.ShapeDtypeStruct((1,), f32),
            ),
            in_specs=[hbm, hbm, hbm, smem, smem, vmem, vmem, smem, vmem, smem],
            out_specs=(vmem, vmem, vmem, smem, smem),
            scratch_shapes=[
                plane(T), plane(T), plane(T), plane(T), plane(T), plane(T),
                plane(7, T), plane(7, T), plane(7, T), plane(7), plane(), plane(T), plane(T), plane(T), plane(),
                plane(STEPS, T), plane(2, STEPS, T), plane(STEPS), plane(STEPS, far),
                plane(STEPS), plane(STEPS, far),
                pltpu.VMEM((slots, 1, Y), f32), pltpu.VMEM((slots, NS, 1, Y), f32),
                pltpu.VMEM((OUTER, 1, Y), f32), pltpu.VMEM((OUTER, NPD, 1, Y), f32),
                pltpu.VMEM((2, 1, Y), jnp.int32),
                plane(5, T), plane(2), plane(2), dma((3,)),
                dma((2, 3)), dma((2, 3)), dma((2, 2, STEPS)), dma((2, 2, STEPS)),
                dma((STEPS, far)), dma((STEPS, far)), dma((STEPS, far)), dma((STEPS, far)),
                dma((slots, NS - 1)), dma((slots, NS - 1)), dma((OUTER, far)), dma((OUTER, far)),
            ],
            compiler_params=pltpu.CompilerParams(collective_id=0, has_side_effects=True),
        )(u, prec, bound, cap, capacity, bv, tc, dens, slope, om)

    in_specs = (
        P("strip", "period", None, None),
        P(None, "strip", "period", None, None),
        P("strip", "period", None, None),
        P("period"),
        P("period"),
        P("strip", None, None),
        P("strip", None, None),
        P(),
        P("strip", None),
        P(),
    )
    out_specs = (
        P("strip", "period", None, None),
        P(None, "strip", "period", None, None),
        P("strip", "period", None, None),
        P("period"),
        P(),
    )
    return jax.shard_map(
        per_device, mesh=mesh, in_specs=in_specs, out_specs=out_specs, check_vma=False
    )
```

```python
import functools
import math

import jax
import jax.numpy as jnp
from jax import lax
from jax.experimental import pallas as pl
from jax.experimental.pallas import tpu as pltpu
from jax.sharding import PartitionSpec as P

OUTER = 2
INNER = 3
STEPS = OUTER * INNER
RATE = math.log(1.1) / 12.0
EPS = 1e-06
SLOPE = 11.0
MESH = pl.DeviceIdType.MESH
ROWS = 8
CHUNK = 4


def kernel(
    NS, NPD, T, Z, Y, R,
    u_ref, prec_ref, bound_ref, cap_ref, capacity_ref, bv_ref, tc_ref, dens_ref, slope_ref, om_ref,
    u_out, prec_out, bound_out, cap_out, w_out,
    uf, uc, us, bf, bc, bs, fa, ca, sa, act, ton, tb, tl, cb, ex0,
    xs, xr, es, er, as_, ar, rs, rb, ps, pb, slr,
    praw, ti, to_sum, loc, ini_s, ini_r, xs_s, xs_r, e_s, e_r, a_s, a_r, r_s, r_r, p_s, p_r,
):
    me = lax.axis_index("strip")
    pe = lax.axis_index("period")
    total_rows = NS
    total_periods = NPD * T
    blocks_all = float(total_rows * Z * Y)
    root_blocks = math.sqrt(blocks_all)
    sends = []

    loads = (
        pltpu.make_async_copy(prec_ref.at[:, 0], praw, loc.at[0]),
        pltpu.make_async_copy(bound_ref.at[0], bf, loc.at[1]),
        pltpu.make_async_copy(u_ref.at[0], uf, loc.at[2]),
    )
    for load in loads:
        load.start()
    barrier = pltpu.get_barrier_semaphore()
    for k in range(1, NS):
        pl.semaphore_signal(barrier, inc=1, device_id={"strip": lax.rem(me + k, NS)}, device_id_type=MESH)
    for k in range(1, NPD):
        pl.semaphore_signal(barrier, inc=1, device_id={"period": lax.rem(pe + k, NPD)}, device_id_type=MESH)

    has = (me < NS - 1, me > 0)
    gets = (me > 0, me < NS - 1)
    to = (me + 1, me - 1)

    def remote(src, dst, ss, rr, dev):
        return pltpu.make_async_remote_copy(
            src_ref=src, dst_ref=dst, send_sem=ss, recv_sem=rr, device_id=dev, device_id_type=MESH
        )

    def ini_copy(d, what):
        if what == 2:
            return remote(to_sum.at[d], ti.at[d], ini_s.at[d, 2], ini_r.at[d, 2], {"strip": to[d]})
        if what == 0:
            rest = pl.ds(1, T - 1)
            return remote(praw.at[1 + d, rest], fa.at[5 + d, rest], ini_s.at[d, 0], ini_r.at[d, 0], {"strip": to[d]})
        return remote(slope_ref, slr.at[d], ini_s.at[d, 1], ini_r.at[d, 1], {"strip": to[d]})

    def x_copy(d, part, s):
        lo, size = (1, T - 1) if part == 0 else (0, 1)
        return remote(
            xs.at[s, pl.ds(lo, size)], xr.at[d, s, pl.ds(lo, size)],
            xs_s.at[d, part, s], xs_r.at[d, part, s], {"strip": to[d]},
        )

    def e_copy(k, s):
        return remote(es.at[s], er.at[s, k - 1], e_s.at[s, k - 1], e_r.at[s, k - 1], {"period": pe + k})

    def a_copy(k, s):
        return remote(as_.at[s], ar.at[s, k - 1], a_s.at[s, k - 1], a_r.at[s, k - 1], {"period": pe - k})

    def r_copy(k, slot):
        return remote(
            rs.at[slot], rb.at[slot, me], r_s.at[slot, k - 1], r_r.at[slot, k - 1],
            {"strip": lax.rem(me + k, NS)},
        )

    def p_copy(k, slot):
        return remote(
            ps.at[slot], pb.at[slot, pe], p_s.at[slot, k - 1], p_r.at[slot, k - 1],
            {"period": lax.rem(pe + k, NPD)},
        )

    def start(cond, copy):
        def go():
            copy.start()
        if cond is None:
            go()
        else:
            pl.when(cond)(go)
        sends.append((cond, copy))

    def wait_recv(cond, copy):
        if cond is None:
            copy.wait_recv()
        else:
            pl.when(cond)(lambda: copy.wait_recv())

    def reduce_start(slot, value):
        rs[slot] = value
        rb[slot, me] = value
        for k in range(1, NS):
            start(None, r_copy(k, slot))

    def reduce_done(slot):
        for k in range(1, NS):
            wait_recv(None, r_copy(k, slot))
        total = rb[slot, 0]
        for k in range(1, NS):
            total = total + rb[slot, k]
        return total

    loads[0].wait()
    for d in range(2):
        total = praw[1 + d, 0]
        for t in range(1, T):
            total = total + praw[1 + d, t]
        to_sum[d] = total
    pl.semaphore_wait(barrier, NS + NPD - 2)
    for d in range(2):
        start(has[d], ini_copy(d, 1))
        start(has[d], ini_copy(d, 2))
    for d in range(2):
        start(has[d], ini_copy(d, 0))

    rows = lax.broadcasted_iota(jnp.int32, (R, Y), 0)
    lanes = lax.broadcasted_iota(jnp.int32, (R, Y), 1)

    def as_lanes(value):
        sums = jnp.sum(value, axis=1, keepdims=True)
        return jnp.sum(jnp.where(lanes == rows, sums, 0.0), axis=0, keepdims=True)

    def as_rows(line):
        return jnp.sum(jnp.where(lanes == rows, line, 0.0), axis=1, keepdims=True)

    def fold(v):
        return jnp.sum(v.reshape(Z // 8, 8, Y), axis=0)

    cls = tc_ref[0]
    tons = jnp.zeros((Z, Y), jnp.float32)
    for c in range(dens_ref.shape[0]):
        tons = jnp.where(cls == c, (1.0 + c) * dens_ref[c], tons)
    ton[...] = tons
    part = jnp.sum(tons, axis=0, keepdims=True)
    reduce_start(0, part)

    z_ids = lax.broadcasted_iota(jnp.int32, (Z, Y), 0)
    y_ids = lax.broadcasted_iota(jnp.int32, (Z, Y), 1)

    def mask_of(codes, k, inside):
        ok = z_ids >= 1
        if k > 0:
            ok = ok & (jnp.broadcast_to((codes >> (k - 1)) & 1, (Z, Y)) == 1)
        if k == 3:
            ok = ok & (y_ids < Y - 1)
        if k == 4:
            ok = ok & (y_ids >= 1)
        if inside is not None:
            ok = ok & (jnp.full((Z, Y), inside.astype(jnp.int32)) == 1)
        return ok.astype(jnp.float32)

    own = slope_ref[...]
    act[0] = mask_of(own, 0, None)
    act[1] = mask_of(own, 1, me < NS - 1)
    act[2] = mask_of(own, 2, me > 0)
    act[3] = mask_of(own, 3, None)
    act[4] = mask_of(own, 4, None)

    period = [(pe * T + t).astype(jnp.float32) for t in range(T)]
    pid = [jnp.full((1, Y), period[t]) for t in range(T)]
    disc = [jnp.exp(-RATE * pid[t]) for t in range(T)]
    tonr = ton[...] * (1.0 / root_blocks)
    for load in loads[1:]:
        load.wait()
    for t in range(T):
        tb[t] = 1.0 / (SLOPE * (total_periods - pid[t]) + tonr)
        for k in range(5):
            fa[k, t] = praw[k, t] * act[k]

    caps = jnp.zeros((R, Y), jnp.float32)
    climit = jnp.zeros((R, Y), jnp.float32)
    for t in range(T):
        caps = jnp.where(rows == t, cap_ref[t], caps)
        climit = jnp.where(rows == t, capacity_ref[t] * blocks_all, climit)
    w = jnp.full((1, Y), om_ref[0])

    for d in range(2):
        @pl.when(jnp.logical_not(gets[d]))
        def _():
            act[5 + d] = jnp.zeros((Z, Y), jnp.float32)
            ti[d] = jnp.zeros((Z, Y), jnp.float32)
            fa[5 + d] = jnp.zeros((T, Z, Y), jnp.float32)
            for s in range(STEPS):
                xr[d, s] = jnp.zeros((T, Z, Y), jnp.float32)

    def up_y(v):
        return pltpu.roll(v, 1, 1)

    def dn_y(v):
        return pltpu.roll(v, Y - 1, 1)

    def up_z(v):
        return pltpu.roll(v, 1, 0)

    def dn_z(v):
        return pltpu.roll(v, Z - 1, 0)

    def settle(first, cur, acc, at, j, new, old):
        if j == 0:
            cur[at] = new
            return new, None
        if j == 1:
            cur[at] = new
            acc[at] = old + new
            return new, None
        mean = (acc[at] + new) * (1.0 / INNER)
        diff = mean - first[at]
        first[at] = mean
        return mean, fold(diff * diff)

    def gradient_own(arcs, bounds):
        for t in range(T):
            p0, p3, p4 = arcs[0, t], arcs[3, t], arcs[4, t]
            back = p0 + (up_y(p3) + dn_y(p4))
            tl[t] = ((p0 + p3) + (p4 + bounds[t])) - dn_z(back)

    def gradient(s, arcs):
        tail = None
        for t in range(T - 1, -1, -1):
            g = (tl[t] + (arcs[1, t] + arcs[2, t])) - dn_z(arcs[5, t] + arcs[6, t])
            tail = g if tail is None else tail + g
            tl[t] = tail
        as_[s] = tail
        for k in range(1, NPD):
            start(pe >= k, a_copy(k, s))

    tail = None
    for t in range(T - 1, -1, -1):
        p = [fa[k, t] for k in range(5)]
        g = (((p[0] + p[1]) + (p[2] + p[3])) + p[4]) + bf[t]
        g = g - dn_z(p[0] + (up_y(p[3]) + dn_y(p[4])))
        tail = g if tail is None else tail + g
        tl[t] = tail
    for d in range(2):
        wait_recv(gets[d], ini_copy(d, 1))
        wait_recv(gets[d], ini_copy(d, 2))

        @pl.when(gets[d])
        def _():
            act[5 + d] = mask_of(slr[d], 1 + d, None)
    as_[0] = tl[0] - dn_z(ti[0] * act[5] + ti[1] * act[6])
    for k in range(1, NPD):
        start(pe >= k, a_copy(k, 0))
    for d in range(2):
        wait_recv(gets[d], ini_copy(d, 0))
        rest = ti[d]
        for t in range(1, T):
            plane = fa[5 + d, t]
            rest = rest - plane
            fa[5 + d, t] = plane * act[5 + d]
        fa[5 + d, 0] = rest * act[5 + d]
    tail = None
    for t in range(T - 1, -1, -1):
        back = fa[5, t] + fa[6, t]
        tail = back if tail is None else tail + back
        tl[t] = tl[t] - dn_z(tail)
    tons_all = jnp.sum(reduce_done(0), axis=1, keepdims=True)
    inv_tons = 1.0 / tons_all
    cap_first = cap_sum = None

    for s in range(STEPS):
        j = s % INNER
        u_src = uf if j == 0 else uc
        b_src = bf if j == 0 else bc
        p_src = fa if j == 0 else ca
        inv_w = 1.0 / w
        move_p = jnp.zeros((8, Y), jnp.float32)
        move_d = jnp.zeros((8, Y), jnp.float32)
        for k in range(1, NPD):
            @pl.when(pe + k < NPD)
            def _():
                a_copy(k, s).wait_recv()
                for t in range(T):
                    tl[t] = tl[t] + ar[s, k - 1]
        head = None
        row = jnp.zeros((R, Y), jnp.float32)
        for t in range(T):
            old = u_src[t]
            grad = tl[t] + (ton[...] * (1.0 / root_blocks)) * caps[t : t + 1, :]
            new = jnp.maximum(old - (tb[t] * inv_w) * (grad - bv_ref[0] * disc[t]), 0.0)
            ext = 2.0 * new - old
            _, moved = settle(uf, uc, us, t, j, new, old)
            if moved is not None:
                move_p = move_p + moved
            if t == 0:
                ex0[...] = ext
            else:
                xs[s, t] = ext
            head = ext if head is None else head + ext
            row = jnp.where(rows == t, jnp.sum(ton[...] * ext, axis=0, keepdims=True), row)
        es[s] = head
        for k in range(1, NPD):
            start(pe + k < NPD, e_copy(k, s))
        for d in range(2):
            start(has[d], x_copy(d, 0, s))
        for k in range(1, NPD):
            @pl.when(pe >= k)
            def _():
                e_copy(k, s).wait_recv()
                ex0[...] = ex0[...] + er[s, k - 1]
        xs[s, 0] = ex0[...]
        for d in range(2):
            start(has[d], x_copy(d, 1, s))
        reduce_start(1 + s, as_lanes(row))
        total = None
        for t in range(T):
            total = xs[s, t] if t == 0 else total + xs[s, t]
            cb[t] = total
        rate_b = [w / (pid[t] + 1.0) for t in range(T)]
        rate_p = [w / (2.0 * (pid[t] + 1.0)) for t in range(T)]

        def arc(k, t, diff, move):
            old = p_src[k, t]
            new = jnp.maximum(old + rate_p[t] * diff, 0.0) * act[k]
            _, moved = settle(fa, ca, sa, (k, t), j, new, old)
            if moved is not None and k < 5:
                move = move + moved
            return move

        for t in range(T):
            c = cb[t]
            old = b_src[t]
            new = jnp.maximum(old + rate_b[t] * (c - 1.0), 0.0)
            _, moved = settle(bf, bc, bs, t, j, new, old)
            if moved is not None:
                move_d = move_d + moved
            cz = up_z(c)
            move_d = arc(0, t, c - cz, move_d)
            move_d = arc(3, t, c - dn_y(cz), move_d)
            move_d = arc(4, t, c - up_y(cz), move_d)
        last = j == INNER - 1
        if s < STEPS - 1:
            gradient_own(fa if last else ca, bf if last else bc)
        for part in range(2):
            for d in range(2):
                wait_recv(gets[d], x_copy(d, part, s))
        total_m = total_p = None
        for t in range(T):
            total_m = xr[0, s, t] if t == 0 else total_m + xr[0, s, t]
            total_p = xr[1, s, t] if t == 0 else total_p + xr[1, s, t]
            c = cb[t]
            cz = up_z(c)
            move_d = arc(1, t, c - up_z(total_p), move_d)
            move_d = arc(2, t, c - up_z(total_m), move_d)
            if s < STEPS - 1:
                arc(5, t, total_m - cz, None)
                arc(6, t, total_p - cz, None)
        if s < STEPS - 1:
            gradient(s + 1, fa if last else ca)
        if last:
            cyc = s // INNER
            mp = jnp.sum(move_p, axis=0, keepdims=True)
            md = jnp.sum(move_d, axis=0, keepdims=True)
            reduce_start(1 + STEPS + cyc, as_lanes(jnp.where(rows == 0, mp, jnp.where(rows == 1, md, 0.0))))
        row_total = as_rows(reduce_done(1 + s))
        new_caps = jnp.maximum(caps + w * ((row_total - climit) * inv_tons), 0.0)
        new_caps = jnp.where(rows < T, new_caps, 0.0)
        if j == 0:
            cap_first = caps
            cap_sum = new_caps
        else:
            cap_sum = cap_sum + new_caps
        caps = new_caps
        if last:
            caps = cap_sum * (1.0 / INNER)
            cap_move = jnp.sum((caps - cap_first) ** 2, axis=0, keepdims=True)
            got = reduce_done(1 + STEPS + cyc)
            msg = got + jnp.where(lanes[0:1] == 1, cap_move, 0.0)
            ps[cyc] = msg
            pb[cyc, pe] = msg
            for k in range(1, NPD):
                start(None, p_copy(k, cyc))
            if s == STEPS - 1:
                for t in range(T):
                    u_out[0, t] = uf[t]
                    bound_out[0, t] = bf[t]
                    for k in range(5):
                        prec_out[k, 0, t] = fa[k, t]
                    cap_out[t] = caps[t, 0]
            for k in range(1, NPD):
                wait_recv(None, p_copy(k, cyc))
            tot = pb[cyc, 0]
            for k in range(1, NPD):
                tot = tot + pb[cyc, k]
            tot = as_rows(tot)
            moved = jnp.sqrt((tot[1:2, :] + EPS) / (tot[0:1, :] + EPS))
            w = jnp.sqrt(w * moved)
    w_out[0] = w[0, 0]
    for cond, copy in sends:
        if cond is None:
            copy.wait_send()
        else:
            pl.when(cond)(lambda copy=copy: copy.wait_send())


def pair_kernel(
    NS, NPD, T, Z, Y,
    u_ref, prec_ref, bound_ref, cap_ref, capacity_ref, bv_ref, tc_ref, dens_ref, slope_ref, om_ref,
    u_out, prec_out, bound_out, few_out,
    slope_own, cap_own, capacity_own, dens_own, om_own, cap_line, capb, hm, hf, hcur, hacc, hc, praw, braw, gh, hh, pu, pb, pg, pp, hpr, nraw, hnr, bvb, tcb, slr,
    fa, ca, sa, fn, cn, sn, fh, ch, sh, bf, bc, bs, uf, uc, us,
    act, nact, hact, ton, tb, pr, tl, tt, rp, rh,
    xs, xr, hs, ls, zh, zl, dh, dl, rs, rb,
    token, loc, ini_s, ini_r, sl_s, sl_r, sm_s, sm_r, re_s, re_r,
    x_s, x_r, z_s, z_r, d_s, d_r, r_s, r_r, o_s, o_r, f_s, f_r, c_s, c_r,
):
    me = lax.axis_index("strip")
    pe = lax.axis_index("period")
    pairs, NP, NQ = NS // 2, NPD * T, 2 * NPD
    NT = NP // ROWS
    ND = NS * NPD
    a, h = me // 2, lax.rem(me, 2)
    q = jnp.where(h == 0, pe, NQ - 1 - pe)
    blocks_all = float(NS * Z * Y)
    inv_root = 1.0 / math.sqrt(blocks_all)
    sends = []

    def rows_of(block):
        return pl.ds(pl.multiple_of(ROWS * block, ROWS), ROWS)

    def block_of(hh_, pp_):
        return jnp.where(hh_ == 0, pp_, NQ - 1 - pp_)

    def device_at(pair, block):
        first = block < NPD
        return {
            "strip": 2 * pair + jnp.where(first, 0, 1),
            "period": jnp.where(first, block, NQ - 1 - block),
        }

    def remote(src, dst, ss, rr, dev):
        return pltpu.make_async_remote_copy(
            src_ref=src, dst_ref=dst, send_sem=ss, recv_sem=rr, device_id=dev, device_id_type=MESH
        )

    def start(cond, copy):
        if cond is None:
            copy.start()
        else:
            pl.when(cond)(lambda: copy.start())
        sends.append((cond, copy))

    def wait_recv(cond, copy):
        if cond is None:
            copy.wait_recv()
        else:
            pl.when(cond)(lambda: copy.wait_recv())

    mine = pl.ds(pe * T, T)
    unit = h * NPD + pe
    peers = pl.ds(0, NQ - 1)
    loads = (
        pltpu.make_async_copy(prec_ref.at[:, 0], praw, loc.at[0]),
        pltpu.make_async_copy(prec_ref.at[:, 0, :, rows_of(q)], pp.at[:, unit], loc.at[1]),
        pltpu.make_async_copy(bound_ref.at[0, :, rows_of(q)], pb.at[unit], loc.at[2]),
        pltpu.make_async_copy(u_ref.at[0, :, rows_of(q)], pu.at[unit], loc.at[3]),
        pltpu.make_async_copy(bound_ref.at[0], braw, loc.at[4]),
        pltpu.make_async_copy(slope_ref, slope_own, loc.at[5]),
        pltpu.make_async_copy(cap_ref, cap_own, loc.at[6]),
        pltpu.make_async_copy(capacity_ref, capacity_own, loc.at[7]),
        pltpu.make_async_copy(dens_ref, dens_own, loc.at[8]),
        pltpu.make_async_copy(om_ref, om_own, loc.at[9]),
        pltpu.make_async_copy(bv_ref.at[0, rows_of(q)], bvb.at[h], loc.at[10]),
        pltpu.make_async_copy(tc_ref.at[0, rows_of(q)], tcb.at[h], loc.at[11]),
    )
    for load in loads:
        load.start()
    barrier = pltpu.get_barrier_semaphore()
    others = [divmod(k, NPD) for k in range(1, ND)]
    others.sort(key=lambda o: -abs(o[0] - NS // 2) if o[0] else NS)

    def other(ks, kp):
        return {"strip": lax.rem(me + ks, NS), "period": lax.rem(pe + kp, NPD)}

    mates = [divmod(k, NPD) for k in range(1, NQ)]

    def mate(i):
        kh, kp = mates[i]
        return lax.rem(h + kh, 2), lax.rem(pe + kp, NPD)

    has = (a > 0, a < pairs - 1)
    up = (q > 0, q < NQ - 1)
    beside = [device_at(a - 1, q), device_at(a + 1, q)]
    for i in range(NQ - 1):
        th, tp = mate(i)
        pl.semaphore_signal(barrier, inc=1, device_id={"strip": 2 * a + th, "period": tp}, device_id_type=MESH)
    column = [device_at(lax.rem(a + k, pairs), q) for k in range(1, pairs)]
    for there in column:
        pl.semaphore_signal(barrier, inc=1, device_id=there, device_id_type=MESH)

    def in_ends(what, rows, block, at):
        if what == 1:
            return hh.at[block], hpr.at[at]
        if what == 2:
            return gh.at[:, rows], pg.at[at]
        if what == 7:
            return cap_line, capb.at[at]
        if what == 3:
            return u_ref.at[0, :, rows], pu.at[at]
        if what == 4:
            return bound_ref.at[0, :, rows], pb.at[at]
        arcs = {0: pl.ds(1, 2), 5: 0, 6: pl.ds(3, 2)}[what]
        return prec_ref.at[arcs, 0, :, rows], pp.at[arcs, at]

    def in_copy(i, what):
        th, tp = mate(i)
        block = block_of(th, tp)
        src, dst = in_ends(what, rows_of(block), block, unit)
        return remote(src, dst, ini_s.at[what], ini_r.at[what], {"strip": 2 * a + th, "period": tp})

    def in_all(what):
        dst = in_ends(what, rows_of(0), 0, peers)[1]
        return remote(dst, dst, ini_s.at[what], ini_r.at[what], other(0, 1))

    def partner_copy(what):
        rows = rows_of(block_of(1 - h, pe))
        dev = {"strip": 2 * a + 1 - h, "period": pe}
        if what == 0:
            return remote(tc_ref.at[0, rows], tcb.at[h], sm_s.at[0], sm_r.at[0], dev)
        return remote(bv_ref.at[0, rows], bvb.at[h], sm_s.at[1], sm_r.at[1], dev)

    def slope_copy(what):
        if what == 2:
            return remote(slope_ref, slr.at[1 + h], sl_s.at[2], sl_r.at[2], {"strip": 2 * a + 1 - h, "period": pe})
        return remote(slr.at[1 + what], slr.at[3 - 3 * what], sl_s.at[what], sl_r.at[1 - what], beside[what])

    def relay_copy(d, what):
        dev = beside[d]
        k, hs_ = (2, 0) if d == 0 else (1, 1)
        ss, rr = re_s.at[d, what], re_r.at[d, what]
        if what == 0:
            return remote(pp.at[k, pl.ds(hs_ * NPD, NPD)], nraw.at[1 - d], ss, rr, dev)
        return remote(hpr.at[pl.ds(hs_ * NPD, NPD), k], hnr.at[1 - d], ss, rr, dev)

    def reduce_sem(slot):
        return r_r.at[slot % 2 if slot < STEPS else 2]

    def reduce_start(slot, value):
        rs[slot] = value
        rb[slot, me * NPD + pe] = value
        for ks, kp in others:
            remote(
                rs.at[slot], rb.at[slot, me * NPD + pe], r_s.at[0], reduce_sem(slot), other(ks, kp)
            ).start()

    def reduce_done(slot):
        rest = rb.at[slot, pl.ds(0, ND - 1)]
        remote(rest, rest, r_s.at[0], reduce_sem(slot), other(0, 1)).wait_recv()
        parts = [rb[slot, i] for i in range(ND)]
        while len(parts) > 1:
            parts = [parts[i] + parts[i + 1] if i + 1 < len(parts) else parts[i] for i in range(0, len(parts), 2)]
        return parts[0]

    def x_copy(d, s):
        dev = beside[d]
        return remote(xs.at[s, d], xr.at[s, 1 - d], x_s.at[d], x_r.at[s % 2, 1 - d], dev)

    def z_copy(d, s):
        if d == 0:
            return remote(ls.at[s], zl.at[s], z_s.at[0], z_r.at[s % 2, 0], device_at(a, q - 1))
        return remote(hs.at[s], zh.at[s], z_s.at[1], z_r.at[s % 2, 1], device_at(a, q + 1))

    def d_copy(d, e, s):
        dev = device_at(a - 1 if d == 0 else a + 1, q - 1 if e == 0 else q + 1)
        src, dst = (ls, dl) if e == 0 else (hs, dh)
        return remote(src.at[s, d], dst.at[s, 1 - d], d_s.at[d, e], d_r.at[s % 2, 1 - d, e], dev)

    def out_ends(what, th, part, rows):
        if what == 0:
            return uf.at[th, part], u_out.at[0, :, rows]
        return fa.at[pl.ds(1, 2), th, part], prec_out.at[pl.ds(1, 2), 0, :, rows]

    def to_mates(src_of, dst, ss, rr):
        for i in range(NQ - 1):
            th, tp = mate(i)
            remote(src_of(th, pl.ds(tp * T, T)), dst, ss, rr, {"strip": 2 * a + th, "period": tp}).start()

    def out_start(what):
        dst = out_ends(what, 0, mine, rows_of(q))[1]
        to_mates(lambda th, part: out_ends(what, th, part, rows_of(q))[0], dst, o_s.at[what], o_r.at[what])

    def home_start():
        here = rows_of(q)
        for src, at in ((fa.at[0], 0), (fa.at[pl.ds(3, 2)], pl.ds(1, 2)), (bf, 3)):
            pick = lambda th, part: src.at[:, th, part] if src is not bf and at != 0 else src.at[th, part]
            to_mates(pick, hf.at[at, :, here], f_s.at[0], f_r.at[0])
        hf[0, :, here] = fa[0, h, mine]
        hf[1, :, here] = fa[3, h, mine]
        hf[2, :, here] = fa[4, h, mine]
        hf[3, :, here] = bf[h, mine]

    def sums_start(s, j):
        here = rows_of(q)
        to_mates(lambda th, part: xs.at[s, th, part], hc.at[j, :, here], c_s.at[0], c_r.at[j])
        hc[j, :, here] = xs[s, h, mine]

    def all_rows(ref):
        return ref.at[:, :, pl.ds(0, ROWS * (NQ - 1))]

    def home_step(j, w):
        if j == 0:
            remote(all_rows(hf), all_rows(hf), f_s.at[0], f_r.at[0], other(0, 1)).wait_recv()
        got = hc.at[j, :, pl.ds(0, ROWS * (NQ - 1))]
        remote(got, got, c_s.at[0], c_r.at[j], other(0, 1)).wait_recv()
        old_ref = hf if j == 0 else hcur
        for t in range(T):
            rate = w / (2.0 * (jnp.full((1, Y), (pe * T + t).astype(jnp.float32)) + 1.0))
            c = hc[j, t]
            cz = roll(c, 1, 0)
            for i, ahead in enumerate((cz, dn_y(cz), up_y(cz), None)):
                old = old_ref[i, t]
                if ahead is None:
                    new = jnp.maximum(old + 2.0 * rate * (c - 1.0), 0.0)
                else:
                    new = jnp.maximum(old + rate * (c - ahead), 0.0) * hm[i]
                if j < INNER - 1:
                    hcur[i, t] = new
                    hacc[i, t] = new if j == 0 else hacc[i, t] + new
                else:
                    mean = (hacc[i, t] + new) * (1.0 / INNER)
                    if ahead is None:
                        bound_out[0, t] = mean
                    else:
                        prec_out[(0, 3, 4)[i], 0, t] = mean

    def out_all(what):
        dst = out_ends(what, 0, mine, pl.ds(0, ROWS * (NQ - 1)))[1]
        return remote(dst, dst, o_s.at[what], o_r.at[what], other(0, 1))

    lanes1 = lax.broadcasted_iota(jnp.int32, (1, Y), 1)
    rows = lax.broadcasted_iota(jnp.int32, (NP, Y), 0)
    lanes = lax.broadcasted_iota(jnp.int32, (NP, Y), 1)

    def tons_of(cls):
        tons = jnp.zeros(cls.shape, jnp.float32)
        for c in range(dens_own.shape[0]):
            tons = jnp.where(cls == c, (1.0 + c) * dens_own[c], tons)
        return tons

    def as_lanes(value):
        sums = jnp.sum(value, axis=1, keepdims=True)
        return jnp.sum(jnp.where(lanes == rows, sums, 0.0), axis=0, keepdims=True)

    def as_rows(line, at=0):
        return jnp.broadcast_to(jnp.sum(jnp.where(lanes == rows + at, line, 0.0), axis=1, keepdims=True), (NP, Y))

    def roll(v, by, axis):
        return pltpu.roll(v, by % v.shape[axis], axis)

    def up_y(v):
        return roll(v, 1, v.ndim - 1)

    def dn_y(v):
        return roll(v, -1, v.ndim - 1)

    def mask_of(code, k, depth, inside):
        ok = (depth >= 1) & (depth < Z)
        y_ids = lax.broadcasted_iota(jnp.int32, depth.shape, 1)
        if k > 0:
            ok = ok & (jnp.broadcast_to((code >> (k - 1)) & 1, depth.shape) == 1)
        if k == 3:
            ok = ok & (y_ids < Y - 1)
        if k == 4:
            ok = ok & (y_ids >= 1)
        if inside is not None:
            ok = ok & (jnp.full(depth.shape, inside.astype(jnp.int32)) == 1)
        return ok.astype(jnp.float32)

    def send_all(*kinds):
        for what in kinds:
            for i in range(NQ - 1):
                in_copy(i, what).start()

    pl.semaphore_wait(barrier, NQ - 1 + pairs - 1)
    send_all(0)
    for there in column:
        pl.semaphore_signal(token.at[0], inc=1, device_id=there, device_id_type=MESH)
    start(None, slope_copy(2))
    start(None, partner_copy(0))
    start(None, partner_copy(1))
    send_all(3)
    for load in loads[6:10]:
        load.wait()
    line = jnp.zeros((1, Y), jnp.float32)
    for t in range(T):
        line = jnp.where(lanes1 == pe * T + t, cap_own[t], line)
        line = jnp.where(lanes1 == NP + pe * T + t, capacity_own[t], line)
    cap_line[...] = line
    capb[unit] = line
    loads[0].wait()
    for b in range(NQ):
        if b + 1 < NQ:
            for k in range(5):
                for t in range(T):
                    hh[b, k, pl.ds(t, 1)] = praw[k, t, pl.ds(ROWS * (b + 1), 1)]
        else:
            hh[b] = jnp.zeros((5, T, Y), jnp.float32)
    hpr[unit] = hh[q]
    send_all(1, 7)
    z_ids = lax.broadcasted_iota(jnp.int32, (ROWS, Y), 0)
    low = z_ids == ROWS - 1
    depth = lax.broadcasted_iota(jnp.int32, (Z, Y), 0)
    loads[5].wait()
    home = {k: mask_of(slope_own[...], k, depth, None) for k in (0, 3, 4)}
    loads[4].wait()
    for i, k in enumerate((0, 3, 4)):
        hm[i] = home[k]
    for t in range(T):
        p0, p3, p4 = (praw[k, t] * home[k] for k in (0, 3, 4))
        gh[t] = ((p0 + p3) + (p4 + braw[t])) - roll(p0 + (up_y(p3) + dn_y(p4)), -1, 0)
    pg[unit] = gh[:, rows_of(q)]
    send_all(2, 4, 5)
    slr[1 + h] = slope_own[...]
    for d in range(2):
        @pl.when(jnp.logical_not(has[d]))
        def _():
            for s in range(STEPS):
                xr[s, d] = jnp.zeros((NP, ROWS, Y), jnp.float32)
            nraw[d] = jnp.zeros((NPD, T, ROWS, Y), jnp.float32)
            hnr[d] = jnp.zeros((NPD, T, Y), jnp.float32)
            slr[3 * d] = jnp.zeros((1, Y), jnp.int32)
        for e in range(2):
            buf = (dh, dl)[e]

            @pl.when(jnp.logical_not(has[d] & up[e]))
            def _():
                for s in range(STEPS):
                    buf[s, d] = jnp.zeros((NT, ROWS, Y), jnp.float32)
    for e in range(2):
        buf = (zh, zl)[e]

        @pl.when(jnp.logical_not(up[e]))
        def _():
            for s in range(STEPS):
                buf[s] = jnp.zeros((2, NT, ROWS, Y), jnp.float32)

    wait_recv(None, slope_copy(2))
    for d in range(2):
        start(has[d], slope_copy(d))
    here, below = z_ids + ROWS * q, jnp.full((ROWS, Y), ROWS * (q + 1))
    for hh_ in range(2):
        code = slr[1 + hh_]
        for k in range(5):
            inside = None
            if k == 1 and hh_ == 1:
                inside = has[1]
            if k == 2 and hh_ == 0:
                inside = has[0]
            act[k, hh_] = mask_of(code, k, here, inside)
            hact[k, hh_] = mask_of(code, k, below, inside)
    for d in range(2):
        wait_recv(has[d], slope_copy(1 - d))
        nact[d] = mask_of(slr[3 * d], 1 + d, here + 1, has[d])

    wait_recv(None, partner_copy(0))
    wait_recv(None, partner_copy(1))
    loads[10].wait()
    loads[11].wait()
    for hh_ in range(2):
        tons = tons_of(tcb[hh_])
        ton[hh_] = tons
        for t in range(NP):
            tb[hh_, t] = 1.0 / (SLOPE * (NP - t) + tons * inv_root)
            pr[hh_, t] = bvb[hh_] * math.exp(-RATE * t)

    t_plane = lax.broadcasted_iota(jnp.int32, (NP, ROWS, Y), 0).astype(jnp.float32)
    t_rows = (
        lax.broadcasted_iota(jnp.int32, (NT, ROWS, Y), 0) * ROWS + lax.broadcasted_iota(jnp.int32, (NT, ROWS, Y), 1)
    ).astype(jnp.float32)

    w = jnp.full((1, Y), om_own[0])

    def set_rates(w):
        rp[...] = w[None] / (2.0 * (t_plane + 1.0))
        rh[...] = w[None] / (2.0 * (t_rows + 1.0))

    set_rates(w)

    loads[1].wait()
    in_all(0).wait_recv()
    for d in range(2):
        start(has[d], relay_copy(d, 0))
    in_all(1).wait_recv()
    for d in range(2):
        start(has[d], relay_copy(d, 1))

    chunks = [(lo, min(CHUNK, NP - lo)) for lo in range(0, NP, CHUNK)]

    def lines(ref, lo, size, *at):
        picked = [ref[(*at, t // ROWS, pl.ds(t % ROWS, 1))] for t in range(lo, lo + size)]
        return jnp.stack([jnp.broadcast_to(p, (ROWS, Y)) for p in picked])

    def from_above(v, line):
        return jnp.where(lax.broadcasted_iota(jnp.int32, v.shape, 1) == 0, line, roll(v, 1, 1))

    def from_below(v, line):
        return jnp.where(lax.broadcasted_iota(jnp.int32, v.shape, 1) == ROWS - 1, line, roll(v, -1, 1))

    def landed(ref, hh_, *at):
        return ref[(*at, pl.ds(hh_ * NPD, NPD))].reshape(NP, ROWS, Y)

    def mask_arcs(ks):
        for k in ks:
            for hh_ in range(2):
                fa[k, hh_] = landed(pp, hh_, k) * act[k, hh_][None]

    def mask_halo(ks):
        for k, hh_ in ks:
            for at in range(NP):
                line = hpr[hh_ * NPD + at // T, k, pl.ds(at % T, 1)]
                fh[k, hh_, at // ROWS, pl.ds(at % ROWS, 1)] = line * hact[k, hh_, 0:1]

    mask_arcs((1, 2))
    mask_halo(((1, 0), (2, 1)))
    for d in range(2):
        wait_recv(has[d], relay_copy(1 - d, 0))
        wait_recv(has[d], relay_copy(1 - d, 1))
        for t in range(NP):
            edge = jnp.broadcast_to(hnr[d, t // T, pl.ds(t % T, 1)], (ROWS, Y))
            fn[d, t] = jnp.where(low, edge, roll(nraw[d, t // T, t % T], -1, 0)) * nact[d]

    def settle(first, cur, acc, at, j, new, old, keep=True):
        if j == 0:
            cur[at] = new
            return None
        if j == 1:
            cur[at] = new
            acc[at] = old + new
            return None
        mean = (acc[at] + new) * (1.0 / INNER)
        diff = mean - first[at]
        if keep:
            first[at] = mean
        return jnp.sum(diff * diff, axis=0)

    def rows_under(edge, lo, size):
        return jnp.stack([
            jnp.broadcast_to(edge[t // ROWS, t % ROWS : t % ROWS + 1], (ROWS, Y)) for t in range(lo, lo + size)
        ])

    def gradient(arcs, near, halo, bounds):
        for hh_ in range(2):
            k_in = 2 - hh_
            edge = (halo[0, hh_] + halo[k_in, 1 - hh_]) + (up_y(halo[3, hh_]) + dn_y(halo[4, hh_]))
            tail = None
            for lo, size in reversed(chunks):
                at = pl.ds(lo, size)
                p0, p3, p4 = arcs[0, hh_, at], arcs[3, hh_, at], arcs[4, hh_, at]
                back = (p0 + arcs[k_in, 1 - hh_, at]) + (up_y(p3) + dn_y(p4))
                g = ((p0 + p3) + (p4 + bounds[hh_, at])) + (arcs[1, hh_, at] + arcs[2, hh_, at])
                g = g - (from_below(back, rows_under(edge, lo, size)) + near[hh_, at])
                for t in range(lo + size - 1, lo - 1, -1):
                    tail = g[t - lo] if tail is None else tail + g[t - lo]
                    tl[hh_, t] = tail

    in_all(2).wait_recv()
    for hh_ in range(2):
        k_in = 2 - hh_
        edge = fh[k_in, 1 - hh_]
        tail = None
        for lo, size in reversed(chunks):
            at = pl.ds(lo, size)
            g = landed(pg, hh_)[lo : lo + size] + (fa[1, hh_, at] + fa[2, hh_, at])
            g = g - (from_below(fa[k_in, 1 - hh_, at], rows_under(edge, lo, size)) + fn[hh_, at])
            for t in range(lo + size - 1, lo - 1, -1):
                tail = g[t - lo] if tail is None else tail + g[t - lo]
                tl[hh_, t] = tail
    loads[3].wait()
    in_all(3).wait_recv()
    for hh_ in range(2):
        uf[hh_] = landed(pu, hh_)
    in_all(7).wait_recv()
    if pairs > 1:
        pl.semaphore_wait(token.at[0], pairs - 1)
    got = capb[0]
    for p in range(1, NPD):
        got = got + capb[p]
    caps = as_rows(got)
    climit = as_rows(got, NP) * blocks_all
    cap_first = cap_sum = inv_tons = None

    def totals(row, s):
        line = as_lanes(row)
        if s > 0:
            return line
        tons = jnp.sum(jnp.sum(ton[0] + ton[1], axis=0, keepdims=True), axis=1, keepdims=True)
        return jnp.where(lanes1 == NP, tons, line)

    for s in range(STEPS):
        j = s % INNER
        last, final = j == INNER - 1, s == STEPS - 1
        u_src = uf if j == 0 else uc
        b_src = bf if j == 0 else bc
        p_src, n_src, h_src = (fa, fn, fh) if j == 0 else (ca, cn, ch)
        inv_w = 1.0 / w
        move_p = jnp.zeros((ROWS, Y), jnp.float32)
        move_d = jnp.zeros((ROWS, Y), jnp.float32)
        if j == 0:
            for hh_ in range(2):
                for t in range(NP):
                    tau = tb[hh_, t] * inv_w
                    tt[hh_, t] = tau * (ton[hh_] * inv_root)
                    tl[hh_, t] = u_src[hh_, t] - tau * (tl[hh_, t] - pr[hh_, t])
        row = jnp.zeros((NP, Y), jnp.float32)
        heads = [None, None]
        for t in range(NP):
            mined = None
            for hh_ in range(2):
                old = u_src[hh_, t]
                new = jnp.maximum(tl[hh_, t] - tt[hh_, t] * caps[t : t + 1, :], 0.0)
                ext = 2.0 * new - old
                if j == 0:
                    uc[hh_, t] = new
                elif j == 1:
                    uc[hh_, t] = new
                    us[hh_, t] = old + new
                else:
                    mean = (us[hh_, t] + new) * (1.0 / INNER)
                    diff = mean - uf[hh_, t]
                    uf[hh_, t] = mean
                    move_p = move_p + diff * diff
                heads[hh_] = ext if t == 0 else heads[hh_] + ext
                xs[s, hh_, t] = heads[hh_]
                hs[s, hh_, t // ROWS, pl.ds(t % ROWS, 1)] = heads[hh_][ROWS - 1 : ROWS]
                if not final:
                    ls[s, hh_, t // ROWS, pl.ds(t % ROWS, 1)] = heads[hh_][0:1]
                part = ton[hh_] * ext
                mined = part if mined is None else mined + part
            row = jnp.where(rows == t, jnp.sum(mined, axis=0, keepdims=True), row)
        if not last:
            reduce_start(s, totals(row, s))
        pl.when(up[1])(z_copy(1, s).start)
        for d in range(2):
            pl.when(has[d])(x_copy(d, s).start)
        for d in range(2):
            pl.when(has[d] & up[1])(d_copy(d, 1, s).start)
        if not final:
            pl.when(up[0])(z_copy(0, s).start)
            for d in range(2):
                pl.when(has[d] & up[0])(d_copy(d, 0, s).start)
        if final:
            out_start(0)
        if s >= STEPS - INNER:
            sums_start(s, j)
        if s == 0:
            send_all(6)
            loads[2].wait()
            in_all(4).wait_recv()
            for hh_ in range(2):
                bf[hh_] = landed(pb, hh_)
        if last:
            reduce_start(s, totals(row, s))

        def arc(k, hh_, at, diff, move):
            old = p_src[k, hh_, at]
            new = jnp.maximum(old + rp[at] * diff, 0.0) * act[k, hh_][None]
            moved = settle(fa, ca, sa, (k, hh_, at), j, new, old, not final or k in (1, 2))
            return move if moved is None else move + moved

        for hh_ in range(2):
            for lo, size in chunks:
                at = pl.ds(lo, size)
                old = b_src[hh_, at]
                new = jnp.maximum(old + 2.0 * rp[at] * (xs[s, hh_, at] - 1.0), 0.0)
                if j == 0:
                    bc[hh_, at] = new
                elif j == 1:
                    bc[hh_, at] = new
                    bs[hh_, at] = old + new
                else:
                    mean = (bs[hh_, at] + new) * (1.0 / INNER)
                    diff = mean - bf[hh_, at]
                    if not final:
                        bf[hh_, at] = mean
                    move_d = move_d + jnp.sum(diff * diff, axis=0)
        if s > STEPS - INNER:
            home_step(j - 1, w)
        wait_recv(up[0], z_copy(1, s))

        def own_arcs(move):
            for lo, size in chunks:
                at = pl.ds(lo, size)
                for hh_ in range(2):
                    c = xs[s, hh_, at]
                    cz = from_above(c, lines(zh, lo, size, s, hh_))
                    move = arc(0, hh_, at, c - cz, move)
                    move = arc(3, hh_, at, c - dn_y(cz), move)
                    move = arc(4, hh_, at, c - up_y(cz), move)
            return move

        if s > 0:
            move_d = own_arcs(move_d)
        for lo, size in chunks:
            at = pl.ds(lo, size)
            c = [xs[s, hh_, at] for hh_ in range(2)]
            cz = [from_above(c[hh_], lines(zh, lo, size, s, hh_)) for hh_ in range(2)]
            move_d = arc(1, 0, at, c[0] - cz[1], move_d)
            move_d = arc(2, 1, at, c[1] - cz[0], move_d)
        for d in range(2):
            wait_recv(has[d], x_copy(1 - d, s))
            wait_recv(has[d] & up[0], d_copy(1 - d, 1, s))
        for lo, size in chunks:
            at = pl.ds(lo, size)
            for d in range(2):
                cz = from_above(xr[s, d, at], lines(dh, lo, size, s, d))
                move_d = arc(2 - d, d, at, xs[s, d, at] - cz, move_d)
        if last:
            cyc = s // INNER
            mp = jnp.sum(move_p, axis=0, keepdims=True)
            md = jnp.sum(move_d, axis=0, keepdims=True)
            reduce_start(STEPS + cyc, as_lanes(jnp.where(rows == 0, mp, jnp.where(rows == 1, md, 0.0))))
        if s == STEPS - INNER - 1:
            home_start()
        if final:
            out_start(1)
            home_step(j, w)
        else:
            wait_recv(up[1], z_copy(0, s))
            for d in range(2):
                wait_recv(has[d] & up[1], d_copy(1 - d, 0, s))
            for lo, size in chunks:
                at = pl.ds(lo, size)
                for d in range(2):
                    old = n_src[d, at]
                    diff = from_below(xr[s, d, at], lines(dl, lo, size, s, d)) - xs[s, d, at]
                    new = jnp.maximum(old + rp[at] * diff, 0.0) * nact[d][None]
                    settle(fn, cn, sn, (d, at), j, new, old)
            if s == 0:
                in_all(5).wait_recv()
                in_all(6).wait_recv()
                mask_arcs((0, 3, 4))
                mask_halo([(k, hh_) for k in (0, 3, 4) for hh_ in range(2)])
                own_arcs(move_d)
            for hh_ in range(2):
                c, cz = zl[s, hh_], hs[s, hh_]
                for k in (0, 3, 4, 1 + hh_):
                    ahead = (cz, hs[s, 1 - hh_], hs[s, 1 - hh_], dn_y(cz), up_y(cz))[k]
                    old = h_src[k, hh_]
                    new = jnp.maximum(old + rh[...] * (c - ahead), 0.0) * hact[k, hh_][None]
                    settle(fh, ch, sh, (k, hh_), j, new, old)
            if last:
                gradient(fa, fn, fh, bf)
            else:
                gradient(ca, cn, ch, bc)
                for hh_ in range(2):
                    for t in range(NP):
                        tau = tb[hh_, t] * inv_w
                        tl[hh_, t] = uc[hh_, t] - tau * (tl[hh_, t] - pr[hh_, t])
        got = reduce_done(s)
        if s == 0:
            inv_tons = 1.0 / jnp.sum(jnp.where(lanes1 == NP, got, 0.0), axis=1, keepdims=True)
        row_total = as_rows(got)
        new_caps = jnp.maximum(caps + w * ((row_total - climit) * inv_tons), 0.0)
        if j == 0:
            cap_first = caps
            cap_sum = new_caps
        else:
            cap_sum = cap_sum + new_caps
        caps = new_caps
        if last:
            caps = cap_sum * (1.0 / INNER)
            cap_move = jnp.sum((caps - cap_first) ** 2, axis=0, keepdims=True)
            if final:
                for t in range(T):
                    few_out[t] = jnp.sum(jnp.where(rows == pe * T + t, caps, 0.0), axis=0)
            tot = as_rows(reduce_done(STEPS + cyc))
            moved = jnp.sqrt((tot[1:2, :] + cap_move + EPS) / (tot[0:1, :] + EPS))
            w = jnp.sqrt(w * moved)
            if not final:
                set_rates(w)
    few_out[T] = w[0]
    u_out[0, :, rows_of(q)] = uf[h, mine]
    for k in (1, 2):
        prec_out[k, 0, :, rows_of(q)] = fa[k, h, mine]
    for what in range(2):
        out_all(what).wait_recv()
    for what in range(2):
        out_all(what).wait_send()
    remote(all_rows(hf), all_rows(hf), f_s.at[0], f_r.at[0], other(0, 1)).wait_send()
    remote(all_rows(hc), all_rows(hc), c_s.at[0], c_r.at[0], other(0, 1)).wait_send()
    for what in range(8):
        in_all(what).wait_send()
    rest = rb.at[:, pl.ds(0, ND - 1)]
    remote(rest, rest, r_s.at[0], r_r.at[0], other(0, 1)).wait_send()

    def wait_sent(cond, ref, sem):
        pl.when(cond)(lambda: remote(ref, ref, sem, sem, other(0, 1)).wait_send())

    rows_down, rows_up = ls.at[pl.ds(0, STEPS - 1)], hs
    wait_sent(up[0], rows_down, z_s.at[0])
    wait_sent(up[1], rows_up, z_s.at[1])
    for d in range(2):
        wait_sent(has[d], xs.at[:, d], x_s.at[d])
        wait_sent(has[d] & up[0], ls.at[pl.ds(0, STEPS - 1), d], d_s.at[d, 0])
        wait_sent(has[d] & up[1], hs.at[:, d], d_s.at[d, 1])
    for cond, copy in sends:
        if cond is None:
            copy.wait_send()
        else:
            pl.when(cond)(lambda copy=copy: copy.wait_send())


def store_kernel(u_ref, prec_ref, bound_ref, few_ref, u_out, prec_out, bound_out, cap_out, w_out, sem):
    stores = (
        pltpu.make_async_copy(prec_ref, prec_out, sem.at[0]),
        pltpu.make_async_copy(u_ref, u_out, sem.at[1]),
        pltpu.make_async_copy(bound_ref, bound_out, sem.at[2]),
    )
    for store in stores:
        store.start()
    T = cap_out.shape[0]
    for t in range(T):
        cap_out[t] = few_ref[t, 0]
    w_out[0] = few_ref[T, 0]
    for store in stores:
        store.wait()


def pair_call(NS, NPD, u, prec, bound, cap, capacity, bv, tc, dens, slope, om):
    _, T, Z, Y = u.shape
    f32 = jnp.float32
    NP, NQ, ND = NPD * T, 2 * NPD, NS * NPD
    NT = NP // ROWS
    vmem = pl.BlockSpec(memory_space=pltpu.VMEM)
    hbm = pl.BlockSpec(memory_space=pl.ANY)
    smem = pl.BlockSpec(memory_space=pltpu.SMEM)
    slots = STEPS + OUTER
    V = lambda *shape: pltpu.VMEM((*shape, Y), f32)
    unit = lambda *n: V(*n, NQ, T, ROWS)
    whole = lambda *n: V(*n, NP, ROWS)
    edge = lambda *n: V(*n, NT, ROWS)
    dma = pltpu.SemaphoreType.DMA
    ours = pl.pallas_call(
        functools.partial(pair_kernel, NS, NPD, T, Z, Y),
        out_shape=(
            pltpu.VMEM(u.shape, f32),
            pltpu.VMEM(prec.shape, f32),
            pltpu.VMEM(bound.shape, f32),
            pltpu.VMEM((T + 1, Y), f32),
        ),
        in_specs=[hbm] * 10,
        out_specs=(vmem, vmem, vmem, vmem),
        scratch_shapes=[
            pltpu.VMEM((1, Y), jnp.int32), pltpu.SMEM(cap.shape, f32), pltpu.SMEM(cap.shape, f32),
            pltpu.SMEM(dens.shape, f32), pltpu.SMEM(om.shape, f32), V(1), V(NQ, 1),
            V(3, Z), V(4, T, Z), V(4, T, Z), V(4, T, Z), V(INNER, T, Z),
            V(5, T, Z), V(T, Z), V(T, Z), V(NQ, 5, T), unit(), unit(), unit(), unit(5), V(NQ, 5, T), V(2, NPD, T, ROWS), V(2, NPD, T),
            V(2, ROWS), pltpu.VMEM((2, ROWS, Y), jnp.int32), pltpu.VMEM((4, 1, Y), jnp.int32),
            whole(5, 2), whole(5, 2), whole(5, 2), whole(2), whole(2), whole(2),
            edge(5, 2), edge(5, 2), edge(5, 2), whole(2), whole(2), whole(2), whole(2), whole(2), whole(2),
            V(5, 2, ROWS), V(2, ROWS), V(5, 2, ROWS), V(2, ROWS), whole(2), whole(2), whole(2), whole(2),
            whole(), edge(),
            whole(STEPS, 2), whole(STEPS, 2), edge(STEPS, 2), edge(STEPS, 2), edge(STEPS, 2), edge(STEPS, 2),
            edge(STEPS, 2), edge(STEPS, 2), V(slots, 1), V(slots, ND, 1),
            pltpu.SemaphoreType.REGULAR((1,)), dma((12,)), dma((8,)), dma((8,)), dma((3,)), dma((3,)), dma((2,)), dma((2,)), dma((2, 2)), dma((2, 2)),
            dma((2,)), dma((2, 2)), dma((2,)), dma((2, 2)), dma((2, 2)), dma((2, 2, 2)), dma((1,)), dma((3,)),
            dma((2,)), dma((2,)), dma((1,)), dma((1,)), dma((1,)), dma((INNER,)),
        ],
        compiler_params=pltpu.CompilerParams(collective_id=1, has_side_effects=True),
    )(u, prec, bound, cap, capacity, bv, tc, dens, slope, om)
    return pl.pallas_call(
        store_kernel,
        out_shape=(
            jax.ShapeDtypeStruct(u.shape, f32),
            jax.ShapeDtypeStruct(prec.shape, f32),
            jax.ShapeDtypeStruct(bound.shape, f32),
            jax.ShapeDtypeStruct(cap.shape, f32),
            jax.ShapeDtypeStruct((1,), f32),
        ),
        in_specs=[vmem] * 4,
        out_specs=(hbm, hbm, hbm, smem, smem),
        scratch_shapes=[dma((3,))],
    )(*[pltpu.with_memory_space_constraint(x, pltpu.VMEM) for x in ours])


def solution(mesh):
    NS, NPD = mesh.shape["strip"], mesh.shape["period"]

    def per_device(u, prec, bound, cap, capacity, bv, tc, dens, slope, om):
        rows_here, T, Z, Y = u.shape
        assert rows_here == 1
        NP = NPD * T
        if NS % 2 == 0 and Z == 2 * NPD * ROWS and NP % ROWS == 0 and 2 * NP < Y:
            return pair_call(NS, NPD, u, prec, bound, cap, capacity, bv, tc, dens, slope, om)
        R = -(-T // 8) * 8
        f32 = jnp.float32
        vmem = pl.BlockSpec(memory_space=pltpu.VMEM)
        hbm = pl.BlockSpec(memory_space=pl.ANY)
        smem = pl.BlockSpec(memory_space=pltpu.SMEM)
        plane = lambda *n: pltpu.VMEM((*n, Z, Y), f32)
        dma = pltpu.SemaphoreType.DMA
        slots = 1 + STEPS + OUTER
        far = max(NPD - 1, 1)
        return pl.pallas_call(
            functools.partial(kernel, NS, NPD, T, Z, Y, R),
            out_shape=(
                pltpu.VMEM(u.shape, f32),
                pltpu.VMEM(prec.shape, f32),
                pltpu.VMEM(bound.shape, f32),
                jax.ShapeDtypeStruct(cap.shape, f32),
                jax.ShapeDtypeStruct((1,), f32),
            ),
            in_specs=[hbm, hbm, hbm, smem, smem, vmem, vmem, smem, vmem, smem],
            out_specs=(vmem, vmem, vmem, smem, smem),
            scratch_shapes=[
                plane(T), plane(T), plane(T), plane(T), plane(T), plane(T),
                plane(7, T), plane(7, T), plane(7, T), plane(7), plane(), plane(T), plane(T), plane(T), plane(),
                plane(STEPS, T), plane(2, STEPS, T), plane(STEPS), plane(STEPS, far),
                plane(STEPS), plane(STEPS, far),
                pltpu.VMEM((slots, 1, Y), f32), pltpu.VMEM((slots, NS, 1, Y), f32),
                pltpu.VMEM((OUTER, 1, Y), f32), pltpu.VMEM((OUTER, NPD, 1, Y), f32),
                pltpu.VMEM((2, 1, Y), jnp.int32),
                plane(5, T), plane(2), plane(2), dma((3,)),
                dma((2, 3)), dma((2, 3)), dma((2, 2, STEPS)), dma((2, 2, STEPS)),
                dma((STEPS, far)), dma((STEPS, far)), dma((STEPS, far)), dma((STEPS, far)),
                dma((slots, NS - 1)), dma((slots, NS - 1)), dma((OUTER, far)), dma((OUTER, far)),
            ],
            compiler_params=pltpu.CompilerParams(collective_id=0, has_side_effects=True),
        )(u, prec, bound, cap, capacity, bv, tc, dens, slope, om)

    in_specs = (
        P("strip", "period", None, None),
        P(None, "strip", "period", None, None),
        P("strip", "period", None, None),
        P("period"),
        P("period"),
        P("strip", None, None),
        P("strip", None, None),
        P(),
        P("strip", None),
        P(),
    )
    out_specs = (
        P("strip", "period", None, None),
        P(None, "strip", "period", None, None),
        P("strip", "period", None, None),
        P("period"),
        P(),
    )
    return jax.shard_map(
        per_device, mesh=mesh, in_specs=in_specs, out_specs=out_specs, check_vma=False
    )
```
